32 devices in a mesh: row: 2 (over y), col: 8 (over z, x), depth: 2 (over core).
Axes of the slice: x: 2, y: 2, z: 4, core: 2. Of those that a mesh axis runs over, the one named last changes fastest.
Arguments:
- a_tiles: bfloat16 [2, 16, 8, 2, 128, 128], P('row', ('col', 'depth')), may hold values from -1.5 to 1.5
- a_cols: int32 [2, 16, 8, 2], P('row', ('col', 'depth')), may hold values from 0 to 15, as said below
- a_count: int32 [2, 16, 8], P('row', ('col', 'depth')), may hold values from 0 to 2, as said below
- b_tiles: bfloat16 [4, 2, 2, 8, 16, 1, 128, 128], P(None, 'row', 'depth', 'col'), may hold values from -1.5 to 1.5
- b_cols: int32 [4, 2, 2, 8, 16, 1], P(None, 'row', 'depth', 'col'), may hold values from 0 to 11, as said below
- b_count: int32 [4, 2, 2, 8, 16], P(None, 'row', 'depth', 'col'), may hold values from 0 to 1, as said below
Outputs:
- product: bfloat16 [2048, 12288], P(('row', 'depth'), 'col')
The draws below stay inside these ranges and needn't reach their ends.
Inputs may be any that keep to these rules, and one draw needn't show every extreme that they name: The entries of a_cols for one row group, inner panel and block row are distinct. `a_count`: some block row holds 2 blocks in every draw. The entries of b_cols for one inner block row are distinct. `b_count`: some inner block row holds 1 block in every draw.
All inputs are finite; a program needn't handle non-finite values.
Results may differ from the reference program's by a relative error of at most 0.001.
Values may be sent and summed in bfloat16 or wider, within the bound.
A program may use at most 128 MiB of HBM per device.

```python
import jax
import jax.numpy as jnp
from jax import lax

TILE = 128
KB = 16
BR = 8
BC = 12
TPR = 2
TPK = 1
SHIFTS = 4
SLOTS = 4
PANELS = 16
ROWS = 2048
COLS = 12288
N_ROW = 2
N_COL = 8
N_DEPTH = 2


def distinct_lists(key, leading, width, needed):
    scores = jax.random.randint(key, leading + (width,), 0, 1 << 20, dtype=jnp.int32) * width + jnp.arange(width, dtype=jnp.int32)
    order_ids = jnp.argsort(scores, axis=-1, stable=True)
    return order_ids[..., :needed].astype(jnp.int32)


def bounded_counts(key, shape_all, most):
    first_key, second_key = jax.random.split(key)
    counts = jax.random.randint(first_key, shape_all, 0, most + 1, dtype=jnp.int32)
    flat_counts = counts.reshape(-1)
    chosen_spot = jax.random.randint(second_key, (), 0, flat_counts.shape[0], dtype=jnp.int32)
    flat_counts = flat_counts.at[chosen_spot].set(most)
    return flat_counts.reshape(shape_all)


def draw_a_cols(key, part):
    return distinct_lists(jax.random.fold_in(key, 11), (N_ROW, PANELS, BR), KB, TPR)


def draw_a_count(key, part):
    return bounded_counts(jax.random.fold_in(key, 12), (N_ROW, PANELS, BR), TPR)


def draw_b_cols(key, part):
    return distinct_lists(jax.random.fold_in(key, 13), (SLOTS, N_ROW, N_DEPTH, N_COL, KB), BC, TPK)


def draw_b_count(key, part):
    return bounded_counts(jax.random.fold_in(key, 14), (SLOTS, N_ROW, N_DEPTH, N_COL, KB), TPK)


def steps_of(own_key, extent, shards, least, high):
    factor_of, own = 1.0, jax.random.fold_in(own_key, 6)
    for axis_at, shards_of in shards:
        draws = jnp.exp(jax.random.uniform(jax.random.fold_in(own, axis_at), (shards_of,), jnp.float32, least / len(shards), high / len(shards)))
        factor_of = factor_of * jnp.repeat(draws, extent[axis_at] // shards_of).reshape([-1 if axis == axis_at else 1 for axis in range(len(extent))])
    return factor_of


def bell_draw(rng, extent, deviation, most, cuts=(), held_as=jnp.bfloat16):
    drawn = deviation * jax.random.normal(rng, extent, jnp.float32)
    if cuts:
        drawn = drawn * steps_of(rng, extent, cuts, -0.22, 0.18)
    return jnp.clip(drawn, -most, most).astype(held_as)


def setup_inputs(seed: int = 0) -> dict:
    key_list = jax.random.split(jax.random.key(seed), 7)
    a_tiles = bell_draw(key_list[0], (N_ROW, PANELS, BR, TPR, TILE, TILE), 0.25, 1.5, ((0, 2), (1, 16)))
    a_cols = draw_a_cols(jax.random.fold_in(key_list[6], 71), 0)
    a_count = draw_a_count(jax.random.fold_in(key_list[6], 71), 0)
    b_tiles = bell_draw(key_list[3], (SLOTS, N_ROW, N_DEPTH, N_COL, KB, TPK, TILE, TILE), 0.25, 1.5, ((1, 2), (2, 2), (3, 8)))
    b_cols = draw_b_cols(jax.random.fold_in(key_list[6], 71), 0)
    b_count = draw_b_count(jax.random.fold_in(key_list[6], 71), 0)
    return dict(a_tiles=a_tiles, a_cols=a_cols, a_count=a_count, b_tiles=b_tiles, b_cols=b_cols, b_count=b_count)


def dense_panel(tiles_b, cols_b, count_b):
    slot_ids = lax.broadcasted_iota(jnp.int32, cols_b.shape, 1)
    valid_slot = slot_ids < count_b[:, None]
    targets = jnp.arange(BC, dtype=jnp.int32)
    placing = jnp.logical_and(cols_b[:, :, None] == targets[None, None, :], valid_slot[:, :, None]).astype(jnp.float32)
    spread = jnp.einsum("kuc,kuab->kacb", placing, tiles_b.astype(jnp.float32), precision=lax.Precision.HIGHEST)
    return spread.astype(jnp.bfloat16).reshape(KB, TILE, BC * TILE)


def panel_product(tiles_a, cols_a, count_a, rows_dense):
    slot_ids = lax.broadcasted_iota(jnp.int32, cols_a.shape, 1)
    valid_slot = slot_ids < count_a[:, None]
    masked = jnp.where(valid_slot[:, :, None, None], tiles_a, jnp.zeros_like(tiles_a))
    chosen = jnp.take(rows_dense, cols_a, axis=0)
    return jnp.einsum("rtab,rtbn->ran", masked.astype(jnp.float32), chosen.astype(jnp.float32), precision=lax.Precision.HIGHEST)


def reference(a_tiles, a_cols, a_count, b_tiles, b_cols, b_count):
    def one_block(flat_index):
        row_group = flat_index // N_COL
        col_group = flat_index % N_COL
        running = jnp.zeros((BR, TILE, BC * TILE), jnp.float32)
        for depth_id in range(N_DEPTH):
            for turn_no in range(SHIFTS):
                panel_no = (row_group + col_group + turn_no) % N_COL
                inner_panel = panel_no * N_DEPTH + depth_id
                slot_no = panel_no // N_ROW
                member = panel_no % N_ROW
                rows_dense = dense_panel(b_tiles[slot_no, member, depth_id, col_group], b_cols[slot_no, member, depth_id, col_group], b_count[slot_no, member, depth_id, col_group])
                running = running + panel_product(a_tiles[row_group, inner_panel], a_cols[row_group, inner_panel], a_count[row_group, inner_panel], rows_dense)
        return running.reshape(BR * TILE, BC * TILE).astype(jnp.bfloat16)

    blocks = lax.map(one_block, jnp.arange(N_ROW * N_COL, dtype=jnp.int32))
    blocks = blocks.reshape(N_ROW, N_COL, BR * TILE, BC * TILE)
    return jnp.transpose(blocks, (0, 2, 1, 3)).reshape(ROWS, COLS)
```

```python
import functools
import math

import jax
import jax.numpy as jnp
from jax import lax
from jax.experimental import pallas as pl
from jax.experimental.pallas import tpu as pltpu
from jax.sharding import PartitionSpec as P

BC = 12
SHIFTS = 4


def for_sending(array):
    return jax.tree.map(lambda a: a.astype(jnp.bfloat16) if a.dtype == jnp.float32 else a, array)


def shifted(value, axis, steps):
    count = lax.axis_size(axis)
    pairs = [(source, (source + steps) % count) for source in range(count)]
    return lax.ppermute(value, axis, pairs)


def dense_panel(tiles_b, cols_b, count_b, width):
    slot_ids = lax.broadcasted_iota(jnp.int32, cols_b.shape, 1)
    valid_slot = slot_ids < count_b[:, None]
    targets = lax.broadcasted_iota(jnp.int32, (1, 1, width), 2)
    placing = jnp.logical_and(cols_b[:, :, None] == targets, valid_slot[:, :, None]).astype(
        jnp.bfloat16
    )
    spread = jnp.einsum("kuc,kuab->kacb", placing, tiles_b, preferred_element_type=jnp.float32)
    inner_blocks = tiles_b.shape[0]
    tile_size = tiles_b.shape[2]
    return spread.astype(jnp.bfloat16).reshape(inner_blocks, tile_size, width * tile_size)


def panel_product(tiles_a, cols_a, count_a, rows_dense):
    block_rows = tiles_a.shape[0]
    per_row = tiles_a.shape[1]
    tile_size = tiles_a.shape[2]
    slot_ids = lax.broadcasted_iota(jnp.int32, cols_a.shape, 1)
    valid_slot = slot_ids < count_a[:, None]
    masked = jnp.where(valid_slot[:, :, None, None], tiles_a, jnp.zeros_like(tiles_a))
    group_rows = math.gcd(block_rows, 4)

    def one_group(pieces):
        tiles_part, cols_part = pieces
        picks = lax.broadcasted_iota(jnp.int32, cols_part.shape + (rows_dense.shape[0],), 2)
        picks = (cols_part[:, :, None] == picks).astype(rows_dense.dtype)
        chosen = jnp.einsum("rtk,kbn->rtbn", picks, rows_dense, preferred_element_type=jnp.float32)
        chosen = chosen.astype(rows_dense.dtype)
        return jnp.einsum("rtab,rtbn->ran", tiles_part, chosen, preferred_element_type=jnp.float32)

    grouped = lax.map(
        one_group,
        (
            masked.reshape(block_rows // group_rows, group_rows, per_row, tile_size, tile_size),
            cols_a.reshape(block_rows // group_rows, group_rows, per_row),
        ),
    )
    return grouped.reshape(block_rows, tile_size, rows_dense.shape[2])


def roll_slots(stack, offset):
    slot_total = stack[0].shape[0]
    return tuple(
        (
            lax.dynamic_slice_in_dim(
                jnp.concatenate([member, member], 0), offset % slot_total, slot_total, 0
            )
            for member in stack
        )
    )


def select_if(flag, fresh, stale):
    return tuple((jnp.where(flag, new_part, old_part) for new_part, old_part in zip(fresh, stale)))


def local(a_tiles, a_cols, a_count, b_tiles, b_cols, b_count):
    rows_axis = lax.axis_size("row")
    cols_axis = lax.axis_size("col")
    row_group = lax.axis_index("row")
    col_group = lax.axis_index("col")
    tiles_a = a_tiles[0, 0]
    cols_a = a_cols[0, 0]
    count_a = a_count[0, 0]
    tiles_b = b_tiles[:, 0, 0, 0]
    cols_b = b_cols[:, 0, 0, 0]
    count_b = b_count[:, 0, 0, 0]
    for bit_pos in range((rows_axis - 1).bit_length()):
        stride = 1 << bit_pos
        moved = (
            shifted(tiles_a, "col", cols_axis - stride),
            shifted(for_sending(cols_a), "col", cols_axis - stride).astype(cols_a.dtype),
            shifted(for_sending(count_a), "col", cols_axis - stride).astype(count_a.dtype),
        )
        tiles_a, cols_a, count_a = select_if(
            row_group // stride % 2 == 1, moved, (tiles_a, cols_a, count_a)
        )
    for bit_pos in range((cols_axis - 1).bit_length()):
        stride = 1 << bit_pos
        nearby = stride % rows_axis
        if nearby:
            moved = (
                shifted(tiles_b, "row", rows_axis - nearby),
                shifted(for_sending(cols_b), "row", rows_axis - nearby).astype(cols_b.dtype),
                shifted(for_sending(count_b), "row", rows_axis - nearby).astype(count_b.dtype),
            )
        else:
            moved = (tiles_b, cols_b, count_b)
        moved = roll_slots(moved, (row_group + stride) // rows_axis)
        tiles_b, cols_b, count_b = select_if(
            col_group // stride % 2 == 1, moved, (tiles_b, cols_b, count_b)
        )
    tile_size = tiles_a.shape[2]
    running = jnp.zeros((tiles_a.shape[0], tile_size, BC * tile_size), jnp.float32)
    for turn_no in range(SHIFTS):
        current_tiles = tiles_b[0]
        current_cols = cols_b[0]
        current_count = count_b[0]
        rows_dense = dense_panel(current_tiles, current_cols, current_count, BC)
        running = running + panel_product(tiles_a, cols_a, count_a, rows_dense)
        if turn_no + 1 < SHIFTS:
            tiles_a, cols_a, count_a = (
                shifted(tiles_a, "col", cols_axis - 1),
                shifted(for_sending(cols_a), "col", cols_axis - 1).astype(cols_a.dtype),
                shifted(for_sending(count_a), "col", cols_axis - 1).astype(count_a.dtype),
            )
            moved = (
                shifted(tiles_b, "row", rows_axis - 1),
                shifted(for_sending(cols_b), "row", rows_axis - 1).astype(cols_b.dtype),
                shifted(for_sending(count_b), "row", rows_axis - 1).astype(count_b.dtype),
            )
            tiles_b, cols_b, count_b = roll_slots(moved, (row_group + 1) // rows_axis)
    flat_running = running.reshape(-1, running.shape[2])
    summed = lax.psum(flat_running, "depth")
    half_rows = flat_running.shape[0] // lax.axis_size("depth")
    own_rows = lax.dynamic_slice_in_dim(summed, lax.axis_index("depth") * half_rows, half_rows, 0)
    return own_rows.astype(jnp.bfloat16)


REACH = SHIFTS + 1
CHUNKS = 4
WIDTH = 1
MESH_ID = pl.DeviceIdType.MESH


def gather_multiply(n_col, a_cols, a_count, b_cols, b_count, a_ref, b_ref, out_ref, A, Bn0, Bn1, Gn0, Gn1, Bf0, Bf1, Gf0, Gf1, MA, MC, MB, MK, SA, SC, SB, SK, run, ktab, ptab, ltab,
                    send_m, recv_m, send_a, recv_a, send_b, recv_b, recv_n, recv_p, local_sem):
    row = lax.axis_index("row")
    col = lax.axis_index("col")
    dep = lax.axis_index("depth")
    side = lax.rem(col, 2)
    half = A.shape[2]
    per_row = A.shape[3]
    size = A.shape[4]
    inner = Bn0.shape[0]
    out_cols = out_ref.shape[1] // size
    terms = SHIFTS * 2 * per_row
    zero_at = half * terms
    parts = half // WIDTH
    units = [(d, pl.ds(h * WIDTH, WIDTH)) for d in range(2) for h in range(parts)]
    count_u = len(units)
    step_b = inner // CHUNKS

    def at(col_offset, flip_depth=False, flip_row=False):
        return (
            1 - row if flip_row else row,
            lax.rem(col + col_offset + n_col, n_col),
            1 - dep if flip_depth else dep,
        )

    chain_dev = at(-2)
    twin_dev = at(0, True)
    row_dev = at(0, False, True)
    side_dev = (row, col + 1 - 2 * side, dep)

    def remote(src, dst, ssem, rsem, dev):
        return pltpu.make_async_remote_copy(
            src_ref=src, dst_ref=dst, send_sem=ssem, recv_sem=rsem, device_id=dev, device_id_type=MESH_ID
        )

    def drain(ref, sem):
        pltpu.make_async_copy(ref, ref, sem).wait()

    s_near = [side + 2 * k for k in range(2)]
    s_far = [1 - side + 2 * k for k in range(2)]
    m_near = [lax.rem(row + col + s, n_col) // 2 for s in s_near]
    m_far = [lax.rem(1 - row + col + s, n_col) // 2 for s in s_far]
    m_mine = [lax.rem(row + col + s, n_col) // 2 for s in s_far]
    near_own, near_twin = (Bn0, Bn1), (Gn0, Gn1)
    far_own, far_twin = (Bf0, Bf1), (Gf0, Gf1)
    index_local = [
        pltpu.make_async_copy(src, dst.at[0], local_sem.at[n])
        for n, (src, dst) in enumerate(((a_cols, MA), (a_count, MC), (b_cols, MB), (b_count, MK)))
    ]
    b_local = [pltpu.make_async_copy(b_ref.at[m_near[k]], near_own[k], local_sem.at[4 + k]) for k in range(2)]
    a_local = pltpu.make_async_copy(a_ref.at[pl.ds(dep * half, half)], A.at[0, 0], local_sem.at[6])
    for copy in index_local + b_local + [a_local]:
        copy.start()

    barrier = pltpu.get_barrier_semaphore()
    reach = REACH - 1
    offsets = [o for o in range(1, n_col) if o <= reach or n_col - o <= reach]
    peers = [at(o, flip) for o in offsets for flip in (False, True)]
    peers += [twin_dev, row_dev, at(0, True, True)]
    for peer in peers:
        pl.semaphore_signal(barrier, inc=1, device_id=peer, device_id_type=MESH_ID)
    pl.semaphore_wait(barrier, len(peers))

    index_copies = []
    for q in range(REACH):
        for d in range(2):
            slot = q * 2 + d
            if slot:
                for n, (src, dst) in enumerate(((a_cols, MA), (a_count, MC))):
                    index_copies.append(
                        remote(src, dst.at[slot], send_m.at[n], recv_m.at[n], at(-q, d == 1))
                    )
    for slot in range(1, 4):
        for n, (src, dst) in enumerate(((b_cols, MB), (b_count, MK))):
            index_copies.append(
                remote(
                    src, dst.at[slot], send_m.at[2 + n], recv_m.at[2 + n],
                    at(0, slot % 2 == 1, slot >= 2),
                )
            )

    swap = [
        remote(
            a_ref.at[pl.ds((1 - dep) * half + h * WIDTH, WIDTH)], A.at[0, 1, pl.ds(h * WIDTH, WIDTH)],
            send_a.at[0], recv_a.at[0, parts + h], twin_dev,
        )
        for h in range(parts)
    ]
    first = [a_ref.at[pl.ds(dep * half + h * WIDTH, WIDTH)] for h in range(parts)]
    first += [A.at[0, 1, pl.ds(h * WIDTH, WIDTH)] for h in range(parts)]

    def to_panel(p, sources, send_row, dev):
        return [
            remote(src, A.at[p, d, r], send_a.at[send_row], recv_a.at[p, u], dev)
            for u, ((d, r), src) in enumerate(zip(units, sources))
        ]

    def panel(p):
        return [A.at[p, d, r] for d, r in units]

    chain = to_panel(2, first, 1, chain_dev)
    chain2 = to_panel(4, panel(2), 2, chain_dev)
    odd1 = to_panel(1, first, 3, side_dev)
    odd3 = to_panel(3, panel(2), 4, side_dev)
    even1 = to_panel(1, panel(2), 3, side_dev)
    even3 = to_panel(3, panel(4), 4, side_dev)

    near_b = [
        remote(b_ref.at[m_near[k]], near_twin[k], send_b.at[0], recv_n, twin_dev)
        for k in range(2)
    ]
    far_b, pass_b = [], []
    for k in range(2):
        for c in range(CHUNKS):
            part = pl.ds(c * step_b, step_b)
            far_b.append(
                remote(
                    b_ref.at[m_far[k], part], far_own[k].at[part],
                    send_b.at[1], recv_b.at[k, c], row_dev,
                )
            )
            pass_b.append(
                remote(
                    far_own[k].at[part], far_twin[k].at[part],
                    send_b.at[2], recv_p.at[k], twin_dev,
                )
            )

    for copy in index_copies[:2] + index_copies[-6:]:
        copy.start()
    for copy in index_copies[2:-6]:
        copy.start()
    for r in range(parts):
        chain[r].start()
        swap[r].start()

        @pl.when(side == 1)
        def _():
            odd1[r].start()

    for copy in far_b:
        copy.start()
    for copy in near_b:
        copy.start()
    run[zero_at] = jnp.zeros(run.shape[1:], jnp.float32)
    for r in range(parts):
        swap[r].wait_recv()
        chain[parts + r].start()

        @pl.when(side == 1)
        def _():
            odd1[parts + r].start()

    groups = [(s, m, k, d, far) for k in range(2) for far, s, m in ((0, s_near[k], m_near[k]), (1, s_far[k], m_mine[k]))
              for d in range(2)]

    def tables(r, carry):
        cs = []
        for s, m, _, d, far in groups:
            slot = (s + row) * 2 + d
            used = SC[slot, 0, dep * half + r]
            for t in range(per_row):
                k = SA[slot, t, dep * half + r]
                c = SB[2 * far + d, m, 0, k]
                ok = jnp.logical_and(used > t, SK[2 * far + d, m, 0, k] > 0)
                c = jnp.where(ok, c, -1)
                here = r * terms + len(cs)
                before = jnp.int32(zero_at)
                for at_p, c_p in enumerate(cs):
                    before = jnp.where(c_p == c, r * terms + at_p, before)
                ktab[here] = k
                ptab[here] = before
                cs.append(c)
        for c in range(out_cols):
            last = jnp.int32(zero_at)
            for at_p, c_p in enumerate(cs):
                last = jnp.where(c_p == c, r * terms + at_p, last)
            ltab[r * out_cols + c] = last
        return carry

    def product(g, d, r, t, right):
        here = r * terms + g * per_row + t
        value = jnp.dot(A[groups[g][0] + row, d, r, t], right[ktab[here]], preferred_element_type=jnp.float32)
        run[here] = value + run[ptab[here]]

    def whole_group(g, right):
        d = groups[g][3]

        def one(t, carry):
            for r in range(half):
                product(g, d, r, t, right)
            return carry

        lax.fori_loop(0, per_row, one, 0)

    begin = count_u // 4
    lag = begin + count_u * 3 // 8
    for u in range(count_u):
        chain[u].wait_recv()
        chain2[u].start()

        @pl.when(side == 0)
        def _():
            even1[u].start()

        @pl.when(side == 1)
        def _():
            odd3[u].start()

        for c in range(u * CHUNKS // count_u, (u + 1) * CHUNKS // count_u):
            far_b[c].wait_recv()
            pass_b[c].start()
        if u == begin:
            for copy in index_local:
                copy.wait()
            for n, ref in enumerate((MA, MC, MB, MK)):
                drain(ref.at[pl.ds(1, ref.shape[0] - 1)], recv_m.at[n])
            scalars = [
                pltpu.make_async_copy(src, dst, local_sem.at[n])
                for n, (src, dst) in enumerate(((MA, SA), (MC, SC), (MB, SB), (MK, SK)))
            ]
            for copy in scalars:
                copy.start()
            for copy in scalars:
                copy.wait()
        for r in range(half):
            if u == begin + r * count_u // (2 * half):
                tables(r, 0)

    def near_unit(u):
        odd3[u].wait_recv()
        d, h = u // parts, u % parts
        for t in range(per_row):
            for r in range(h * WIDTH, (h + 1) * WIDTH):
                product(4 + d, d, r, t, (Bn1, Gn1)[d])

    done = 0
    for u in range(count_u):
        chain2[u].wait_recv()

        @pl.when(side == 0)
        def _():
            even3[u].start()

        for c in range(CHUNKS + u * CHUNKS // count_u, CHUNKS + (u + 1) * CHUNKS // count_u):
            far_b[c].wait_recv()
            pass_b[c].start()
        if u == begin:
            a_local.wait()
            for copy in b_local:
                copy.wait()
            drain(A.at[pl.ds(0, 2)], recv_n)
            for copy in odd1:
                copy.wait_recv()
            drain(Gf0, recv_p.at[0])
        for g, right in enumerate((Bn0, Gn0, Bf0, Gf0)):
            if u == begin + g * count_u // 8:
                whole_group(g, right)
        if u >= lag:
            near_unit(done)
            done += 1
    for u in range(done, count_u):
        near_unit(u)
    whole_group(6, Bf1)
    drain(Gf1, recv_p.at[1])
    whole_group(7, Gf1)

    def place(r, carry):
        rows = pl.ds(pl.multiple_of(r * size, size), size)
        for c in range(out_cols):
            out_ref[rows, c * size : (c + 1) * size] = run[ltab[r * out_cols + c]].astype(out_ref.dtype)
        return carry

    lax.fori_loop(0, half, place, 0)

    for n, ref in enumerate((MA, MC, MB, MK)):
        drain(ref.at[pl.ds(0, ref.shape[0] - 1)], send_m.at[n])
    drain(A.at[0, 1], send_a.at[0])
    for n in range(1, 5):
        drain(A.at[n], send_a.at[n])
    for n in range(3):
        drain(A.at[pl.ds(0, 2)], send_b.at[n])


def local_fast(n_col, a_tiles, a_cols, a_count, b_tiles, b_cols, b_count):
    block_rows, per_row, size = a_tiles.shape[2:5]
    slots, inner = b_tiles.shape[0], b_tiles.shape[4]
    half = block_rows // 2
    terms = SHIFTS * 2 * per_row
    count = half * terms
    panels = REACH * 2
    hbm = pl.BlockSpec(memory_space=pltpu.HBM)
    vmem = pl.BlockSpec(memory_space=pltpu.VMEM)
    index_shapes = [(panels, per_row, block_rows), (panels, 1, block_rows), (4, slots, 1, inner), (4, slots, 1, inner)]
    call = pl.pallas_call(
        functools.partial(gather_multiply, n_col),
        out_shape=jax.ShapeDtypeStruct((half * size, BC * size), jnp.bfloat16),
        in_specs=[hbm] * 6,
        out_specs=vmem,
        scratch_shapes=[pltpu.VMEM((REACH, 2, half, per_row, size, size), jnp.bfloat16)]
        + [pltpu.VMEM((inner, size, size), jnp.bfloat16)] * 8
        + [pltpu.VMEM(shape, jnp.int32) for shape in index_shapes]
        + [pltpu.SMEM(shape, jnp.int32) for shape in index_shapes]
        + [
            pltpu.VMEM((count + 1, size, size), jnp.float32),
            pltpu.SMEM((count,), jnp.int32),
            pltpu.SMEM((count,), jnp.int32),
            pltpu.SMEM((half * BC,), jnp.int32),
            pltpu.SemaphoreType.DMA((4,)),
            pltpu.SemaphoreType.DMA((4,)),
            pltpu.SemaphoreType.DMA((5,)),
            pltpu.SemaphoreType.DMA((REACH, 2 * half)),
            pltpu.SemaphoreType.DMA((3,)),
            pltpu.SemaphoreType.DMA((2, CHUNKS)),
            pltpu.SemaphoreType.DMA,
            pltpu.SemaphoreType.DMA((2,)),
            pltpu.SemaphoreType.DMA((7,)),
        ],
        compiler_params=pltpu.CompilerParams(
            collective_id=0, has_side_effects=True, vmem_limit_bytes=40 * 1024 * 1024
        ),
    )
    operands = [
        jnp.swapaxes(a_cols.reshape(block_rows, per_row), 0, 1),
        a_count.reshape(1, block_rows),
        b_cols.reshape(slots, 1, inner),
        b_count.reshape(slots, 1, inner),
        a_tiles.reshape(block_rows, per_row, size, size),
        b_tiles.reshape(slots, inner, size, size),
    ]
    return call(*(pltpu.with_memory_space_constraint(x, pltpu.HBM) for x in operands))


def solution(mesh):
    placed = (
        P("row", ("col", "depth"), None, None, None, None),
        P("row", ("col", "depth"), None, None),
        P("row", ("col", "depth"), None),
        P(None, "row", "depth", "col", None, None, None, None),
        P(None, "row", "depth", "col", None, None),
        P(None, "row", "depth", "col", None),
    )
    n_col = mesh.shape["col"]
    if mesh.shape["row"] == 2 and mesh.shape["depth"] == 2 and n_col % 2 == 0 and n_col > SHIFTS:
        body = functools.partial(local_fast, n_col)
    else:
        body = local
    return jax.shard_map(
        body, mesh=mesh, in_specs=placed, out_specs=P(("row", "depth"), "col"), check_vma=False
    )
```

```python
import functools
import math

import jax
import jax.numpy as jnp
from jax import lax
from jax.experimental import pallas as pl
from jax.experimental.pallas import tpu as pltpu
from jax.sharding import PartitionSpec as P

BC = 12
SHIFTS = 4


def for_sending(array):
    return jax.tree.map(lambda a: a.astype(jnp.bfloat16) if a.dtype == jnp.float32 else a, array)


def shifted(value, axis, steps):
    count = lax.axis_size(axis)
    pairs = [(source, (source + steps) % count) for source in range(count)]
    return lax.ppermute(value, axis, pairs)


def dense_panel(tiles_b, cols_b, count_b, width):
    slot_ids = lax.broadcasted_iota(jnp.int32, cols_b.shape, 1)
    valid_slot = slot_ids < count_b[:, None]
    targets = lax.broadcasted_iota(jnp.int32, (1, 1, width), 2)
    placing = jnp.logical_and(cols_b[:, :, None] == targets, valid_slot[:, :, None]).astype(
        jnp.bfloat16
    )
    spread = jnp.einsum("kuc,kuab->kacb", placing, tiles_b, preferred_element_type=jnp.float32)
    inner_blocks = tiles_b.shape[0]
    tile_size = tiles_b.shape[2]
    return spread.astype(jnp.bfloat16).reshape(inner_blocks, tile_size, width * tile_size)


def panel_product(tiles_a, cols_a, count_a, rows_dense):
    block_rows = tiles_a.shape[0]
    per_row = tiles_a.shape[1]
    tile_size = tiles_a.shape[2]
    slot_ids = lax.broadcasted_iota(jnp.int32, cols_a.shape, 1)
    valid_slot = slot_ids < count_a[:, None]
    masked = jnp.where(valid_slot[:, :, None, None], tiles_a, jnp.zeros_like(tiles_a))
    group_rows = math.gcd(block_rows, 4)

    def one_group(pieces):
        tiles_part, cols_part = pieces
        picks = lax.broadcasted_iota(jnp.int32, cols_part.shape + (rows_dense.shape[0],), 2)
        picks = (cols_part[:, :, None] == picks).astype(rows_dense.dtype)
        chosen = jnp.einsum("rtk,kbn->rtbn", picks, rows_dense, preferred_element_type=jnp.float32)
        chosen = chosen.astype(rows_dense.dtype)
        return jnp.einsum("rtab,rtbn->ran", tiles_part, chosen, preferred_element_type=jnp.float32)

    grouped = lax.map(
        one_group,
        (
            masked.reshape(block_rows // group_rows, group_rows, per_row, tile_size, tile_size),
            cols_a.reshape(block_rows // group_rows, group_rows, per_row),
        ),
    )
    return grouped.reshape(block_rows, tile_size, rows_dense.shape[2])


def roll_slots(stack, offset):
    slot_total = stack[0].shape[0]
    return tuple(
        (
            lax.dynamic_slice_in_dim(
                jnp.concatenate([member, member], 0), offset % slot_total, slot_total, 0
            )
            for member in stack
        )
    )


def select_if(flag, fresh, stale):
    return tuple((jnp.where(flag, new_part, old_part) for new_part, old_part in zip(fresh, stale)))


def local(a_tiles, a_cols, a_count, b_tiles, b_cols, b_count):
    rows_axis = lax.axis_size("row")
    cols_axis = lax.axis_size("col")
    row_group = lax.axis_index("row")
    col_group = lax.axis_index("col")
    tiles_a = a_tiles[0, 0]
    cols_a = a_cols[0, 0]
    count_a = a_count[0, 0]
    tiles_b = b_tiles[:, 0, 0, 0]
    cols_b = b_cols[:, 0, 0, 0]
    count_b = b_count[:, 0, 0, 0]
    for bit_pos in range((rows_axis - 1).bit_length()):
        stride = 1 << bit_pos
        moved = (
            shifted(tiles_a, "col", cols_axis - stride),
            shifted(for_sending(cols_a), "col", cols_axis - stride).astype(cols_a.dtype),
            shifted(for_sending(count_a), "col", cols_axis - stride).astype(count_a.dtype),
        )
        tiles_a, cols_a, count_a = select_if(
            row_group // stride % 2 == 1, moved, (tiles_a, cols_a, count_a)
        )
    for bit_pos in range((cols_axis - 1).bit_length()):
        stride = 1 << bit_pos
        nearby = stride % rows_axis
        if nearby:
            moved = (
                shifted(tiles_b, "row", rows_axis - nearby),
                shifted(for_sending(cols_b), "row", rows_axis - nearby).astype(cols_b.dtype),
                shifted(for_sending(count_b), "row", rows_axis - nearby).astype(count_b.dtype),
            )
        else:
            moved = (tiles_b, cols_b, count_b)
        moved = roll_slots(moved, (row_group + stride) // rows_axis)
        tiles_b, cols_b, count_b = select_if(
            col_group // stride % 2 == 1, moved, (tiles_b, cols_b, count_b)
        )
    tile_size = tiles_a.shape[2]
    running = jnp.zeros((tiles_a.shape[0], tile_size, BC * tile_size), jnp.float32)
    for turn_no in range(SHIFTS):
        current_tiles = tiles_b[0]
        current_cols = cols_b[0]
        current_count = count_b[0]
        rows_dense = dense_panel(current_tiles, current_cols, current_count, BC)
        running = running + panel_product(tiles_a, cols_a, count_a, rows_dense)
        if turn_no + 1 < SHIFTS:
            tiles_a, cols_a, count_a = (
                shifted(tiles_a, "col", cols_axis - 1),
                shifted(for_sending(cols_a), "col", cols_axis - 1).astype(cols_a.dtype),
                shifted(for_sending(count_a), "col", cols_axis - 1).astype(count_a.dtype),
            )
            moved = (
                shifted(tiles_b, "row", rows_axis - 1),
                shifted(for_sending(cols_b), "row", rows_axis - 1).astype(cols_b.dtype),
                shifted(for_sending(count_b), "row", rows_axis - 1).astype(count_b.dtype),
            )
            tiles_b, cols_b, count_b = roll_slots(moved, (row_group + 1) // rows_axis)
    flat_running = running.reshape(-1, running.shape[2])
    summed = lax.psum(flat_running, "depth")
    half_rows = flat_running.shape[0] // lax.axis_size("depth")
    own_rows = lax.dynamic_slice_in_dim(summed, lax.axis_index("depth") * half_rows, half_rows, 0)
    return own_rows.astype(jnp.bfloat16)


REACH = SHIFTS + 1
CHUNKS = 4
LATE = 1
MESH_ID = pl.DeviceIdType.MESH


def gather_multiply(n_col, a_cols, a_count, b_cols, b_count, a_ref, b_ref, out_ref, A, Bn0, Bn1, Bf0, Bf1,
                    Gn0, Gn1, Gf0, Gf1, MA, MB, SA, SB, run, ktab, ptab, ltab,
                    send_m, recv_m, send_a, recv_a, send_b, recv_b, recv_n, ready, local_sem):
    row = lax.axis_index("row")
    col = lax.axis_index("col")
    dep = lax.axis_index("depth")
    side = lax.rem(col, 2)
    z = lax.div(col, 2)
    top = n_col // 2 - 1
    per_row, size = A.shape[1:3]
    units = A.shape[0] // REACH
    half = units // 2
    inner = Bn0.shape[0]
    out_cols = out_ref.shape[1] // size
    terms = SHIFTS * 2 * per_row
    zero_at = half * terms
    step_b = inner // CHUNKS
    row0, row1, side0, side1 = row == 0, row == 1, side == 0, side == 1

    def both(*flags):
        return functools.reduce(jnp.logical_and, flags)

    def at(col_offset, flip_depth=False, flip_row=False):
        return (
            1 - row if flip_row else row,
            lax.rem(col + col_offset + n_col, n_col),
            1 - dep if flip_depth else dep,
        )

    twin_dev, row_dev = at(0, True), at(0, False, True)
    side_dev = (row, col + 1 - 2 * side, dep)
    down, up, down2, up2 = at(-2), at(2), at(-4), at(4)

    def remote(src, dst, ssem, rsem, dev):
        return pltpu.make_async_remote_copy(
            src_ref=src, dst_ref=dst, send_sem=ssem, recv_sem=rsem, device_id=dev, device_id_type=MESH_ID
        )

    def signal(sem, dev):
        pl.semaphore_signal(sem, inc=1, device_id=dev, device_id_type=MESH_ID)

    def drain(ref, sem):
        pltpu.make_async_copy(ref, ref, sem).wait()

    def start(copies, *flags):
        def go():
            for copy in copies:
                copy.start()

        if flags:
            pl.when(both(*flags))(go)
        else:
            go()

    s_near = [side + 2 * k for k in range(2)]
    s_far = [1 - side + 2 * k for k in range(2)]
    m_near = [lax.rem(row + col + s, n_col) // 2 for s in s_near]
    m_far = [lax.rem(1 - row + col + s, n_col) // 2 for s in s_far]
    m_mine = [lax.rem(row + col + s, n_col) // 2 for s in s_far]
    near_own, near_twin = (Bn0, Bn1), (Gn0, Gn1)
    far_own, far_twin = (Bf0, Bf1), (Gf0, Gf1)

    index_local = [
        pltpu.make_async_copy(src, dst, local_sem.at[n])
        for n, (src, dst) in enumerate((
            (a_cols, MA.at[0, pl.ds(0, per_row)]), (a_count, MA.at[0, pl.ds(per_row, 1)]),
            (b_cols, MB.at[0, 0]), (b_count, MB.at[0, 1]),
        ))
    ]
    b_local = [pltpu.make_async_copy(b_ref.at[m_near[k]], near_own[k], local_sem.at[4 + k]) for k in range(2)]
    a_local = pltpu.make_async_copy(a_ref.at[pl.ds(dep * half, half)], A.at[pl.ds(0, half)], local_sem.at[6])
    start(index_local + b_local + [a_local])

    @pl.when(row0)
    def _():
        for slot in range(2 * SHIFTS, 2 * REACH):
            MA[slot] = jnp.zeros(MA.shape[1:], MA.dtype)

    barrier = pltpu.get_barrier_semaphore()
    signal(barrier, twin_dev)
    pl.when(row0)(lambda: signal(barrier, row_dev))
    pl.when(side0)(lambda: signal(barrier, side_dev))
    pl.when(z < top)(lambda: signal(barrier, up))
    pl.when(z == 0)(lambda: signal(barrier, down))
    pl.when(both(row1, z == 1))(lambda: signal(barrier, down2))
    greeted = 1 + row + side + jnp.where(z > 0, 1, 0) + jnp.where(z == top, 1 + row, 0)
    pl.semaphore_wait(barrier, greeted)
    pl.when(row1)(lambda: signal(ready.at[0], row_dev))
    pl.when(side1)(lambda: signal(ready.at[1], side_dev))
    pl.when(z == top)(lambda: signal(ready.at[2], up))
    pl.when(both(row1, z == top))(lambda: signal(ready.at[2], up2))

    def unit(p, u):
        return A.at[p * units + u]

    own = [a_ref.at[dep * half + r] for r in range(half)] + [unit(0, half + r) for r in range(half)]

    def to_panel(p, sources, n, dev):
        return [remote(src, unit(p, u), send_a.at[n], recv_a.at[p, u], dev) for u, src in enumerate(sources)]

    def panel(p):
        return [unit(p, u) for u in range(units)]

    swap = [
        remote(a_ref.at[(1 - dep) * half + r], unit(0, half + r), send_a.at[0], recv_a.at[0, r], twin_dev)
        for r in range(half)
    ]
    chain = to_panel(2, own, 1, down)
    chain2 = to_panel(4, panel(2), 2, down)
    skip = to_panel(4, own, 3, down2)
    own_x1 = to_panel(1, own, 4, side_dev)
    fwd_x1 = to_panel(1, panel(2), 4, side_dev)
    fwd_x3 = to_panel(3, panel(2), 5, side_dev)
    top_x3 = to_panel(3, panel(4), 5, side_dev)
    low_x3 = to_panel(3, panel(1), 6, down)
    late = range(units - LATE, units)

    near_b = [remote(b_ref.at[m_near[k]], near_twin[k], send_b.at[0], recv_n, twin_dev) for k in range(2)]
    far_b, pass_b = [], []
    for k in range(2):
        for c in range(CHUNKS):
            part = pl.ds(c * step_b, step_b)
            far_b.append(
                remote(b_ref.at[m_far[k], part], far_own[k].at[part], send_b.at[1], recv_b.at[k, c], row_dev)
            )
            pass_b.append(
                remote(
                    far_own[k].at[part], far_twin[k].at[part], send_b.at[2], recv_b.at[2 + k, 0], twin_dev
                )
            )

    def index_a(src, dst, n, sem, dev):
        return remote(MA.at[pl.ds(src, n)], MA.at[pl.ds(dst, n)], send_m.at[sem], recv_m.at[dst // 2], dev)

    swap_m = remote(MA.at[0], MA.at[1], send_m.at[0], recv_m.at[0], twin_dev)
    near_m = remote(MB.at[0], MB.at[1], send_m.at[1], recv_m.at[5], twin_dev)
    far_m = remote(MB.at[0], MB.at[2], send_m.at[1], recv_m.at[6], row_dev)
    pass_m = remote(MB.at[2], MB.at[3], send_m.at[1], recv_m.at[7], twin_dev)
    chain_m, chain2_m, skip_m = index_a(0, 4, 2, 0, down), index_a(4, 8, 2, 2, down), index_a(0, 8, 2, 3, down2)
    own_x1_m, fwd_x1_m = index_a(0, 2, 2, 0, side_dev), index_a(4, 2, 2, 0, side_dev)
    fwd_x3_m, low_x3_m = index_a(4, 6, 2, 4, side_dev), index_a(2, 6, 2, 4, down)

    for copy in index_local:
        copy.wait()
    start([swap_m] + swap)
    first = half // 2
    start(chain[:first], z > 0)
    start(own_x1[:first], side1)
    pl.when(row0)(lambda: pl.semaphore_wait(ready.at[0], 1))
    start([far_m] + far_b + [near_m] + near_b)
    swap_m.wait_recv()
    start([chain_m], z > 0)
    start([own_x1_m], side1)
    start(chain[first:half], z > 0)
    start(own_x1[first:half], side1)
    for r in range(half):
        swap[r].wait_recv()
    start(chain[half:], z > 0)
    start(own_x1[half:], side1)

    @pl.when(z == 0)
    def _():
        pl.semaphore_wait(ready.at[2], 1)
        start(chain[:first] + [chain_m] + chain[first:])

    @pl.when(both(row1, z == 1))
    def _():
        pl.semaphore_wait(ready.at[2], 1)
        start(skip[:1] + [skip_m])

    pl.when(side0)(lambda: pl.semaphore_wait(ready.at[1], 1))
    run[zero_at] = jnp.zeros(run.shape[1:], jnp.float32)

    def far_part(n):
        far_b[n].wait_recv()
        pass_b[n].start()

    def low(u):
        recv(1, u)
        start([low_x3[u]], side1, *([] if u in late else [row0]))

    def recv(p, u):
        drain(unit(p, u), recv_a.at[p, u])

    groups = [(s, m, k, d, far) for k in range(2) for far, s, m in ((0, s_near[k], m_near[k]), (1, s_far[k], m_mine[k]))
              for d in range(2)]

    def tables(r):
        cs = []
        for s, m, _, d, far in groups:
            slot = (s + row) * 2 + d
            used = SA[slot, per_row, dep * half + r]
            for t in range(per_row):
                k = SA[slot, t, dep * half + r]
                c = SB[2 * far + d, 0, m, 0, k]
                ok = jnp.logical_and(used > t, SB[2 * far + d, 1, m, 0, k] > 0)
                c = jnp.where(ok, c, -1)
                here = r * terms + len(cs)
                before = jnp.int32(zero_at)
                for at_p, c_p in enumerate(cs):
                    before = jnp.where(c_p == c, r * terms + at_p, before)
                ktab[here] = k
                ptab[here] = before
                cs.append(c)
        for c in range(out_cols):
            last = jnp.int32(zero_at)
            for at_p, c_p in enumerate(cs):
                last = jnp.where(c_p == c, r * terms + at_p, last)
            ltab[r * out_cols + c] = last

    def product(g, r, t, right):
        s, _, _, d, _ = groups[g]
        here = r * terms + g * per_row + t
        left = A[(s + row) * units + d * half + r, t]
        value = jnp.dot(left, right[ktab[here]], preferred_element_type=jnp.float32)
        run[here] = value + run[ptab[here]]

    def whole_group(g, right):
        def one(t, carry):
            for r in range(half):
                product(g, r, t, right)
            return carry

        lax.fori_loop(0, per_row, one, 0)

    def unit_of(g, r, right):
        for t in range(per_row):
            product(g, r, t, right)

    for u in range(units):
        recv(2, u)
        start([chain2[u]], row1, z > 0)
        start([fwd_x1[u]], side0)
        start([fwd_x3[u]], side1)
        if u == 0:
            drain(MA.at[pl.ds(4, 2)], recv_m.at[2])
            start([chain2_m], row1, z > 0)
            start([fwd_x1_m], side0)
            start([fwd_x3_m], side1)
            far_m.wait_recv()
            pass_m.start()
        if u == units - 2:
            start(skip[1:], row1, z == 1)
        if u == units // 2:
            drain(MA.at[pl.ds(2, 2)], recv_m.at[1])
            start([low_x3_m], side1)
        if u >= 3:
            low(u - 3)
        if u % 2:
            far_part(u // 2)

    def near_unit(u):
        pl.when(row != side)(lambda: recv(3, u))
        pl.when(both(row1, side1))(lambda: recv(4, u))
        unit_of(4 + u // half, u % half, (Bn1, Gn1)[u // half])

    near_done = 0
    for u in range(units):
        @pl.when(both(row1, side0))
        def _():
            recv(4, u)
            if u not in late:
                top_x3[u].start()

        if u < 3:
            low(units - 3 + u)
        if u == 0:
            drain(MA.at[pl.ds(6, 2)], recv_m.at[3])
            pl.when(row1)(lambda: drain(MA.at[pl.ds(8, 2)], recv_m.at[4]))
            near_m.wait_recv()
            pass_m.wait_recv()
            scalars = [pltpu.make_async_copy(MA, SA, local_sem.at[0]), pltpu.make_async_copy(MB, SB, local_sem.at[1])]
            start(scalars)
            for copy in scalars:
                copy.wait()
            for copy in b_local + [a_local]:
                copy.wait()
            drain(A.at[pl.ds(0, 2 * units)], recv_n)
            drain(A.at[pl.ds(0, units)], recv_b.at[2, 0])
        if u % 2:
            far_part(CHUNKS + u // 2)
        if 1 <= u <= half:
            tables(u - 1)
        if u == half:
            whole_group(0, Bn0)
        if u == half + 1:
            whole_group(1, Gn0)
            whole_group(2, Bf0)
        if u == half + 2:
            whole_group(3, Gf0)
        if u > half + 1:
            for w in range(near_done, near_done + 3):
                near_unit(w)
            near_done += 3
    for u in range(near_done, units):
        near_unit(u)

    def far_unit(u, right):
        pl.when(row == side)(lambda: recv(3, u))
        unit_of(6 + u // half, u % half, right)

    for u in range(half):
        far_unit(u, Bf1)
    drain(A.at[pl.ds(0, units)], recv_b.at[3, 0])
    for u in range(half, units):
        far_unit(u, Gf1)

    def place(r, carry):
        rows = pl.ds(pl.multiple_of(r * size, size), size)
        for c in range(out_cols):
            out_ref[rows, c * size : (c + 1) * size] = run[ltab[r * out_cols + c]].astype(out_ref.dtype)
        return carry

    lax.fori_loop(0, half, place, 0)

    def sent(n, sem, *flags):
        if flags:
            pl.when(both(*flags))(lambda: drain(A.at[pl.ds(0, n)], sem))
        else:
            drain(A.at[pl.ds(0, n)], sem)

    sent(half, send_a.at[0])
    sent(units, send_a.at[1])
    sent(units, send_a.at[2], row1, z > 0)
    sent(units, send_a.at[3], row1, z == 1)
    sent(units, send_a.at[4])
    sent(units, send_a.at[5], side1)
    sent(units - LATE, send_a.at[5], side0, row1)
    sent(units, send_a.at[6], side1, row0)
    sent(LATE, send_a.at[6], side1, row1)
    for n in range(3):
        sent(2 * units, send_b.at[n])
    drain(MA.at[pl.ds(0, 5)], send_m.at[0])
    drain(MB.at[pl.ds(0, 3)], send_m.at[1])
    pl.when(both(row1, z > 0))(lambda: drain(MA.at[pl.ds(0, 2)], send_m.at[2]))
    pl.when(both(row1, z == 1))(lambda: drain(MA.at[pl.ds(0, 2)], send_m.at[3]))
    pl.when(side1)(lambda: drain(MA.at[pl.ds(0, 4)], send_m.at[4]))


def local_fast(n_col, a_tiles, a_cols, a_count, b_tiles, b_cols, b_count):
    block_rows, per_row, size = a_tiles.shape[2:5]
    slots, inner = b_tiles.shape[0], b_tiles.shape[4]
    half = block_rows // 2
    count = half * SHIFTS * 2 * per_row
    hbm = pl.BlockSpec(memory_space=pltpu.HBM)
    index_shapes = [(REACH * 2, per_row + 1, block_rows), (4, 2, slots, 1, inner)]
    call = pl.pallas_call(
        functools.partial(gather_multiply, n_col),
        out_shape=jax.ShapeDtypeStruct((half * size, BC * size), jnp.bfloat16),
        in_specs=[hbm] * 6,
        out_specs=pl.BlockSpec(memory_space=pltpu.VMEM),
        scratch_shapes=[pltpu.VMEM((REACH * block_rows, per_row, size, size), jnp.bfloat16)]
        + [pltpu.VMEM((inner, size, size), jnp.bfloat16)] * 8
        + [pltpu.VMEM(shape, jnp.int32) for shape in index_shapes]
        + [pltpu.SMEM(shape, jnp.int32) for shape in index_shapes]
        + [
            pltpu.VMEM((count + 1, size, size), jnp.float32),
            pltpu.SMEM((count,), jnp.int32),
            pltpu.SMEM((count,), jnp.int32),
            pltpu.SMEM((half * BC,), jnp.int32),
            pltpu.SemaphoreType.DMA((5,)),
            pltpu.SemaphoreType.DMA((8,)),
            pltpu.SemaphoreType.DMA((7,)),
            pltpu.SemaphoreType.DMA((REACH, block_rows)),
            pltpu.SemaphoreType.DMA((3,)),
            pltpu.SemaphoreType.DMA((4, CHUNKS)),
            pltpu.SemaphoreType.DMA,
            pltpu.SemaphoreType.REGULAR((3,)),
            pltpu.SemaphoreType.DMA((7,)),
        ],
        compiler_params=pltpu.CompilerParams(
            collective_id=0, has_side_effects=True, vmem_limit_bytes=40 * 1024 * 1024
        ),
    )
    operands = [
        jnp.swapaxes(a_cols.reshape(block_rows, per_row), 0, 1),
        a_count.reshape(1, block_rows),
        b_cols.reshape(slots, 1, inner),
        b_count.reshape(slots, 1, inner),
        a_tiles.reshape(block_rows, per_row, size, size),
        b_tiles.reshape(slots, inner, size, size),
    ]
    return call(*(pltpu.with_memory_space_constraint(x, pltpu.HBM) for x in operands))


def solution(mesh):
    placed = (
        P("row", ("col", "depth"), None, None, None, None),
        P("row", ("col", "depth"), None, None),
        P("row", ("col", "depth"), None),
        P(None, "row", "depth", "col", None, None, None, None),
        P(None, "row", "depth", "col", None, None),
        P(None, "row", "depth", "col", None),
    )
    n_col = mesh.shape["col"]
    if mesh.shape["row"] == 2 and mesh.shape["depth"] == 2 and n_col == 2 * SHIFTS:
        body = functools.partial(local_fast, n_col)
    else:
        body = local
    return jax.shard_map(
        body, mesh=mesh, in_specs=placed, out_specs=P(("row", "depth"), "col"), check_vma=False
    )
```

```python
import functools
import math

import jax
import jax.numpy as jnp
from jax import lax
from jax.experimental import pallas as pl
from jax.experimental.pallas import tpu as pltpu
from jax.sharding import PartitionSpec as P

BC = 12
SHIFTS = 4


def for_sending(array):
    return jax.tree.map(lambda a: a.astype(jnp.bfloat16) if a.dtype == jnp.float32 else a, array)


def shifted(value, axis, steps):
    count = lax.axis_size(axis)
    pairs = [(source, (source + steps) % count) for source in range(count)]
    return lax.ppermute(value, axis, pairs)


def dense_panel(tiles_b, cols_b, count_b, width):
    slot_ids = lax.broadcasted_iota(jnp.int32, cols_b.shape, 1)
    valid_slot = slot_ids < count_b[:, None]
    targets = lax.broadcasted_iota(jnp.int32, (1, 1, width), 2)
    placing = jnp.logical_and(cols_b[:, :, None] == targets, valid_slot[:, :, None]).astype(
        jnp.bfloat16
    )
    spread = jnp.einsum("kuc,kuab->kacb", placing, tiles_b, preferred_element_type=jnp.float32)
    inner_blocks = tiles_b.shape[0]
    tile_size = tiles_b.shape[2]
    return spread.astype(jnp.bfloat16).reshape(inner_blocks, tile_size, width * tile_size)


def panel_product(tiles_a, cols_a, count_a, rows_dense):
    block_rows = tiles_a.shape[0]
    per_row = tiles_a.shape[1]
    tile_size = tiles_a.shape[2]
    slot_ids = lax.broadcasted_iota(jnp.int32, cols_a.shape, 1)
    valid_slot = slot_ids < count_a[:, None]
    masked = jnp.where(valid_slot[:, :, None, None], tiles_a, jnp.zeros_like(tiles_a))
    group_rows = math.gcd(block_rows, 4)

    def one_group(pieces):
        tiles_part, cols_part = pieces
        picks = lax.broadcasted_iota(jnp.int32, cols_part.shape + (rows_dense.shape[0],), 2)
        picks = (cols_part[:, :, None] == picks).astype(rows_dense.dtype)
        chosen = jnp.einsum("rtk,kbn->rtbn", picks, rows_dense, preferred_element_type=jnp.float32)
        chosen = chosen.astype(rows_dense.dtype)
        return jnp.einsum("rtab,rtbn->ran", tiles_part, chosen, preferred_element_type=jnp.float32)

    grouped = lax.map(
        one_group,
        (
            masked.reshape(block_rows // group_rows, group_rows, per_row, tile_size, tile_size),
            cols_a.reshape(block_rows // group_rows, group_rows, per_row),
        ),
    )
    return grouped.reshape(block_rows, tile_size, rows_dense.shape[2])


def roll_slots(stack, offset):
    slot_total = stack[0].shape[0]
    return tuple(
        (
            lax.dynamic_slice_in_dim(
                jnp.concatenate([member, member], 0), offset % slot_total, slot_total, 0
            )
            for member in stack
        )
    )


def select_if(flag, fresh, stale):
    return tuple((jnp.where(flag, new_part, old_part) for new_part, old_part in zip(fresh, stale)))


def local(a_tiles, a_cols, a_count, b_tiles, b_cols, b_count):
    rows_axis = lax.axis_size("row")
    cols_axis = lax.axis_size("col")
    row_group = lax.axis_index("row")
    col_group = lax.axis_index("col")
    tiles_a = a_tiles[0, 0]
    cols_a = a_cols[0, 0]
    count_a = a_count[0, 0]
    tiles_b = b_tiles[:, 0, 0, 0]
    cols_b = b_cols[:, 0, 0, 0]
    count_b = b_count[:, 0, 0, 0]
    for bit_pos in range((rows_axis - 1).bit_length()):
        stride = 1 << bit_pos
        moved = (
            shifted(tiles_a, "col", cols_axis - stride),
            shifted(for_sending(cols_a), "col", cols_axis - stride).astype(cols_a.dtype),
            shifted(for_sending(count_a), "col", cols_axis - stride).astype(count_a.dtype),
        )
        tiles_a, cols_a, count_a = select_if(
            row_group // stride % 2 == 1, moved, (tiles_a, cols_a, count_a)
        )
    for bit_pos in range((cols_axis - 1).bit_length()):
        stride = 1 << bit_pos
        nearby = stride % rows_axis
        if nearby:
            moved = (
                shifted(tiles_b, "row", rows_axis - nearby),
                shifted(for_sending(cols_b), "row", rows_axis - nearby).astype(cols_b.dtype),
                shifted(for_sending(count_b), "row", rows_axis - nearby).astype(count_b.dtype),
            )
        else:
            moved = (tiles_b, cols_b, count_b)
        moved = roll_slots(moved, (row_group + stride) // rows_axis)
        tiles_b, cols_b, count_b = select_if(
            col_group // stride % 2 == 1, moved, (tiles_b, cols_b, count_b)
        )
    tile_size = tiles_a.shape[2]
    running = jnp.zeros((tiles_a.shape[0], tile_size, BC * tile_size), jnp.float32)
    for turn_no in range(SHIFTS):
        current_tiles = tiles_b[0]
        current_cols = cols_b[0]
        current_count = count_b[0]
        rows_dense = dense_panel(current_tiles, current_cols, current_count, BC)
        running = running + panel_product(tiles_a, cols_a, count_a, rows_dense)
        if turn_no + 1 < SHIFTS:
            tiles_a, cols_a, count_a = (
                shifted(tiles_a, "col", cols_axis - 1),
                shifted(for_sending(cols_a), "col", cols_axis - 1).astype(cols_a.dtype),
                shifted(for_sending(count_a), "col", cols_axis - 1).astype(count_a.dtype),
            )
            moved = (
                shifted(tiles_b, "row", rows_axis - 1),
                shifted(for_sending(cols_b), "row", rows_axis - 1).astype(cols_b.dtype),
                shifted(for_sending(count_b), "row", rows_axis - 1).astype(count_b.dtype),
            )
            tiles_b, cols_b, count_b = roll_slots(moved, (row_group + 1) // rows_axis)
    flat_running = running.reshape(-1, running.shape[2])
    summed = lax.psum(flat_running, "depth")
    half_rows = flat_running.shape[0] // lax.axis_size("depth")
    own_rows = lax.dynamic_slice_in_dim(summed, lax.axis_index("depth") * half_rows, half_rows, 0)
    return own_rows.astype(jnp.bfloat16)


REACH = SHIFTS + 1
CHUNKS = 4
LATE = 1
MESH_ID = pl.DeviceIdType.MESH


def gather_multiply(n_col, a_cols, a_count, b_cols, b_count, a_ref, b_ref, out_ref, A, Bn0, Bn1, Bf0, Bf1,
                    Gn0, Gn1, Gf0, Gf1, MA, MB, SA, SB, run, ktab, ptab, ltab,
                    send_m, recv_m, send_a, recv_a, send_b, recv_b, recv_n, ready, local_sem):
    row = lax.axis_index("row")
    col = lax.axis_index("col")
    dep = lax.axis_index("depth")
    side = lax.rem(col, 2)
    z = lax.div(col, 2)
    top = n_col // 2 - 1
    per_row, size = A.shape[1:3]
    units = A.shape[0] // REACH
    half = units // 2
    inner = Bn0.shape[0]
    out_cols = out_ref.shape[1] // size
    terms = SHIFTS * 2 * per_row
    zero_at = half * terms
    step_b = inner // CHUNKS
    row0, row1, side0, side1 = row == 0, row == 1, side == 0, side == 1

    def both(*flags):
        return functools.reduce(jnp.logical_and, flags)

    def at(col_offset, flip_depth=False, flip_row=False):
        return (
            1 - row if flip_row else row,
            lax.rem(col + col_offset + n_col, n_col),
            1 - dep if flip_depth else dep,
        )

    twin_dev, row_dev = at(0, True), at(0, False, True)
    side_dev = (row, col + 1 - 2 * side, dep)
    down, up, down2, up2 = at(-2), at(2), at(-4), at(4)

    def remote(src, dst, ssem, rsem, dev):
        return pltpu.make_async_remote_copy(
            src_ref=src, dst_ref=dst, send_sem=ssem, recv_sem=rsem, device_id=dev, device_id_type=MESH_ID
        )

    def signal(sem, dev):
        pl.semaphore_signal(sem, inc=1, device_id=dev, device_id_type=MESH_ID)

    def drain(ref, sem):
        pltpu.make_async_copy(ref, ref, sem).wait()

    def start(copies, *flags):
        def go():
            for copy in copies:
                copy.start()

        if flags:
            pl.when(both(*flags))(go)
        else:
            go()

    s_near = [side + 2 * k for k in range(2)]
    s_far = [1 - side + 2 * k for k in range(2)]
    m_near = [lax.rem(row + col + s, n_col) // 2 for s in s_near]
    m_far = [lax.rem(1 - row + col + s, n_col) // 2 for s in s_far]
    m_mine = [lax.rem(row + col + s, n_col) // 2 for s in s_far]
    near_own, near_twin = (Bn0, Bn1), (Gn0, Gn1)
    far_own, far_twin = (Bf0, Bf1), (Gf0, Gf1)

    index_local = [
        pltpu.make_async_copy(src, dst, local_sem.at[n])
        for n, (src, dst) in enumerate((
            (a_cols, MA.at[0, pl.ds(0, per_row)]), (a_count, MA.at[0, pl.ds(per_row, 1)]),
            (b_cols, MB.at[0, 0]), (b_count, MB.at[0, 1]),
        ))
    ]
    b_local = [pltpu.make_async_copy(b_ref.at[m_near[k]], near_own[k], local_sem.at[4 + k]) for k in range(2)]
    a_local = pltpu.make_async_copy(a_ref.at[pl.ds(dep * half, half)], A.at[pl.ds(0, half)], local_sem.at[6])
    start(index_local + b_local + [a_local])

    @pl.when(row0)
    def _():
        for slot in range(2 * SHIFTS, 2 * REACH):
            MA[slot] = jnp.zeros(MA.shape[1:], MA.dtype)

    barrier = pltpu.get_barrier_semaphore()
    signal(barrier, twin_dev)
    pl.when(row0)(lambda: signal(barrier, row_dev))
    pl.when(side0)(lambda: signal(barrier, side_dev))
    pl.when(z < top)(lambda: signal(barrier, up))
    pl.when(z == 0)(lambda: signal(barrier, down))
    pl.when(both(row1, z == 1))(lambda: signal(barrier, down2))
    greeted = 1 + row + side + jnp.where(z > 0, 1, 0) + jnp.where(z == top, 1 + row, 0)
    pl.semaphore_wait(barrier, greeted)
    pl.when(row1)(lambda: signal(ready.at[0], row_dev))
    pl.when(side1)(lambda: signal(ready.at[1], side_dev))
    pl.when(z == top)(lambda: signal(ready.at[2], up))
    pl.when(both(row1, z == top))(lambda: signal(ready.at[2], up2))

    def unit(p, u):
        return A.at[p * units + u]

    own = [a_ref.at[dep * half + r] for r in range(half)] + [unit(0, half + r) for r in range(half)]

    def landed(p, u):
        return recv_a.at[(p - 1) * units + u]

    def to_panel(p, sources, n, dev):
        return [remote(src, unit(p, u), send_a.at[n], landed(p, u), dev) for u, src in enumerate(sources)]

    def panel(p):
        return [unit(p, u) for u in range(units)]

    swap = [
        remote(a_ref.at[(1 - dep) * half + r], unit(0, half + r), send_a.at[0], landed(REACH, r), twin_dev)
        for r in range(half)
    ]
    chain = to_panel(2, own, 1, down)
    chain2 = to_panel(4, panel(2), 2, down)
    skip = to_panel(4, own, 3, down2)
    own_x1 = to_panel(1, own, 4, side_dev)
    fwd_x1 = to_panel(1, panel(2), 4, side_dev)
    fwd_x3 = to_panel(3, panel(2), 5, side_dev)
    top_x3 = to_panel(3, panel(4)[: units - LATE], 5, side_dev)
    low_x3 = to_panel(3, panel(1), 6, down)

    near_b = [remote(b_ref.at[m_near[k]], near_twin[k], send_b.at[0], recv_n, twin_dev) for k in range(2)]
    far_b, pass_b = [], []
    for k in range(2):
        for c in range(CHUNKS):
            part = pl.ds(c * step_b, step_b)
            far_b.append(
                remote(b_ref.at[m_far[k], part], far_own[k].at[part], send_b.at[1], recv_b.at[k * CHUNKS + c], row_dev)
            )
            pass_b.append(
                remote(
                    far_own[k].at[part], far_twin[k].at[part], send_b.at[2], recv_b.at[2 * CHUNKS + k], twin_dev
                )
            )

    def index_a(src, dst, n, sem, dev):
        return remote(MA.at[pl.ds(src, n)], MA.at[pl.ds(dst, n)], send_m.at[sem], recv_m.at[dst // 2], dev)

    swap_m = remote(MA.at[0], MA.at[1], send_m.at[0], recv_m.at[0], twin_dev)
    near_m = remote(MB.at[0], MB.at[1], send_m.at[1], recv_m.at[5], twin_dev)
    far_m = remote(MB.at[0], MB.at[2], send_m.at[1], recv_m.at[6], row_dev)
    pass_m = remote(MB.at[2], MB.at[3], send_m.at[1], recv_m.at[7], twin_dev)
    chain_m, chain2_m, skip_m = index_a(0, 4, 2, 0, down), index_a(4, 8, 2, 2, down), index_a(0, 8, 2, 3, down2)
    own_x1_m, fwd_x1_m = index_a(0, 2, 2, 0, side_dev), index_a(4, 2, 2, 0, side_dev)
    fwd_x3_m, low_x3_m = index_a(4, 6, 2, 4, side_dev), index_a(2, 6, 2, 4, down)

    for copy in index_local:
        copy.wait()
    start([swap_m] + swap)
    start(chain[:2], z > 0)
    start(own_x1[:2], side1)
    pl.when(row0)(lambda: pl.semaphore_wait(ready.at[0], 1))
    start([far_m] + far_b + [near_m] + near_b)
    swap_m.wait_recv()
    start([chain_m] + chain[2:half], z > 0)
    start([own_x1_m] + own_x1[2:half], side1)
    for copy in swap:
        copy.wait_recv()

    @pl.when(z == 0)
    def _():
        pl.semaphore_wait(ready.at[2], 1)
        start([chain_m] + chain[:half])

    @pl.when(both(row1, z == 1))
    def _():
        pl.semaphore_wait(ready.at[2], 1)
        start([skip_m] + skip[:1])

    pl.when(side0)(lambda: pl.semaphore_wait(ready.at[1], 1))
    run[zero_at] = jnp.zeros(run.shape[1:], jnp.float32)

    def far_part(n):
        far_b[n].wait_recv()
        pass_b[n].start()

    def low(u):
        recv(1, u)
        start([low_x3[u]], side1, *([] if u >= units - LATE else [row0]))

    def recv(p, u):
        drain(unit(p, u), landed(p, u))

    groups = [(s, m, k, d, far) for k in range(2) for far, s, m in ((0, s_near[k], m_near[k]), (1, s_far[k], m_mine[k]))
              for d in range(2)]

    def tables(r):
        cs = []
        for s, m, _, d, far in groups:
            slot = (s + row) * 2 + d
            used = SA[slot, per_row, dep * half + r]
            for t in range(per_row):
                k = SA[slot, t, dep * half + r]
                c = SB[2 * far + d, 0, m, 0, k]
                ok = jnp.logical_and(used > t, SB[2 * far + d, 1, m, 0, k] > 0)
                c = jnp.where(ok, c, -1)
                here = r * terms + len(cs)
                before = jnp.int32(zero_at)
                for at_p, c_p in enumerate(cs):
                    before = jnp.where(c_p == c, r * terms + at_p, before)
                ktab[here] = k
                ptab[here] = before
                cs.append(c)
        for c in range(out_cols):
            last = jnp.int32(zero_at)
            for at_p, c_p in enumerate(cs):
                last = jnp.where(c_p == c, r * terms + at_p, last)
            ltab[r * out_cols + c] = last

    def products(g, wanted, right):
        s, _, _, d, _ = groups[g]
        values = []
        for r, t in wanted:
            here = r * terms + g * per_row + t
            left = A[(s + row) * units + d * half + r, t]
            values.append((here, jnp.dot(left, right[ktab[here]], preferred_element_type=jnp.float32)))
        for here, value in values:
            run[here] = value + run[ptab[here]]

    def unit_of(g, r, right):
        products(g, [(r, t) for t in range(per_row)], right)

    def whole_group(g, right):
        for r in range(half):
            unit_of(g, r, right)

    for u in range(units):
        recv(2, u)
        if u == 0:
            drain(MA.at[pl.ds(4, 2)], recv_m.at[2])
            start([chain2_m], row1, z > 0)
            start([fwd_x1_m], side0)
            start([fwd_x3_m], side1)
        start([fwd_x1[u]], side0)
        if u == 2:
            drain(MA.at[pl.ds(2, 2)], recv_m.at[1])
            start([low_x3_m], side1)
        if u < half:
            start([chain[half + u]])
            start([own_x1[half + u]], side1)
        else:
            start(chain2[2 * (u - half) : 2 * (u - half) + 2], row1, z > 0)
            start(fwd_x3[2 * (u - half) : 2 * (u - half) + 2], side1)
        if u == 0:
            far_m.wait_recv()
            pass_m.start()
        if u == units - 3:
            start(skip[1:], row1, z == 1)
        if u >= 3:
            low(u - 3)
        if u % 2:
            far_part(u // 2)

    def near_unit(u):
        pl.when(row != side)(lambda: recv(3, u))
        pl.when(both(row1, side1))(lambda: recv(4, u))
        unit_of(4 + u // half, u % half, (Bn1, Gn1)[u // half])

    scalars = [pltpu.make_async_copy(MA, SA, local_sem.at[0]), pltpu.make_async_copy(MB, SB, local_sem.at[1])]

    for u in range(units):
        @pl.when(both(row1, side0))
        def _():
            recv(4, u)
            if u < units - LATE:
                top_x3[u].start()

        if u < 3:
            low(units - 3 + u)
        if u == 0:
            drain(MA.at[pl.ds(6, 2)], recv_m.at[3])
            pl.when(row1)(lambda: drain(MA.at[pl.ds(8, 2)], recv_m.at[4]))
            near_m.wait_recv()
            pass_m.wait_recv()
            start(scalars)
        if u == 1:
            for copy in scalars + b_local + [a_local]:
                copy.wait()
            drain(A.at[pl.ds(0, 2 * units)], recv_n)
            drain(A.at[pl.ds(0, units)], recv_b.at[2 * CHUNKS])
        if u in (1, 3, 5):
            far_part(CHUNKS + u // 2)
        if u in (1, 2):
            for r in range((u - 1) * half // 2, u * half // 2):
                tables(r)
        if u == 3:
            whole_group(0, Bn0)
        if u == 4:
            whole_group(1, Gn0)
            whole_group(2, Bf0)
        if u == 5:
            whole_group(3, Gf0)
        if u == 6:
            for w in range(half):
                near_unit(w)
        if u == 7:
            for w in range(half, units - 2):
                near_unit(w)
    far_part(2 * CHUNKS - 1)

    def far_unit(u):
        pl.when(row == side)(lambda: recv(3, u))
        unit_of(6 + u // half, u % half, (Bf1, Gf1)[u // half])

    def place(r):
        for c in range(out_cols):
            out_ref[r * size : (r + 1) * size, c * size : (c + 1) * size] = run[ltab[r * out_cols + c]].astype(
                out_ref.dtype
            )

    def last_row():
        near_unit(units - 1)
        far_unit(half - 1)

    for r in range(half - 2):
        far_unit(r)
    near_unit(units - 2)
    far_unit(half - 2)
    pl.when(z < top)(last_row)
    drain(A.at[pl.ds(0, units)], recv_b.at[2 * CHUNKS + 1])
    for r in range(half - 2):
        far_unit(half + r)
        place(r)
    pl.when(z == top)(last_row)
    for r in range(half - 2, half):
        far_unit(half + r)
        place(r)

    def sent(n, sem, *flags):
        if flags:
            pl.when(both(*flags))(lambda: drain(A.at[pl.ds(0, n)], sem))
        else:
            drain(A.at[pl.ds(0, n)], sem)

    sent(half, send_a.at[0])
    sent(units, send_a.at[1])
    sent(units, send_a.at[2], row1, z > 0)
    sent(units, send_a.at[3], row1, z == 1)
    sent(units, send_a.at[4])
    sent(units, send_a.at[5], side1)
    sent(units - LATE, send_a.at[5], side0, row1)
    sent(units, send_a.at[6], side1, row0)
    sent(LATE, send_a.at[6], side1, row1)
    for n in range(3):
        sent(2 * units, send_b.at[n])
    drain(MA.at[pl.ds(0, 5)], send_m.at[0])
    drain(MB.at[pl.ds(0, 3)], send_m.at[1])
    pl.when(both(row1, z > 0))(lambda: drain(MA.at[pl.ds(0, 2)], send_m.at[2]))
    pl.when(both(row1, z == 1))(lambda: drain(MA.at[pl.ds(0, 2)], send_m.at[3]))
    pl.when(side1)(lambda: drain(MA.at[pl.ds(0, 4)], send_m.at[4]))


def local_fast(n_col, a_tiles, a_cols, a_count, b_tiles, b_cols, b_count):
    block_rows, per_row, size = a_tiles.shape[2:5]
    slots, inner = b_tiles.shape[0], b_tiles.shape[4]
    half = block_rows // 2
    count = half * SHIFTS * 2 * per_row
    hbm = pl.BlockSpec(memory_space=pltpu.HBM)
    index_shapes = [(REACH * 2, per_row + 1, block_rows), (4, 2, slots, 1, inner)]
    call = pl.pallas_call(
        functools.partial(gather_multiply, n_col),
        out_shape=jax.ShapeDtypeStruct((half * size, BC * size), jnp.bfloat16),
        in_specs=[hbm] * 6,
        out_specs=pl.BlockSpec(memory_space=pltpu.VMEM),
        scratch_shapes=[pltpu.VMEM((REACH * block_rows, per_row, size, size), jnp.bfloat16)]
        + [pltpu.VMEM((inner, size, size), jnp.bfloat16)] * 8
        + [pltpu.VMEM(shape, jnp.int32) for shape in index_shapes]
        + [pltpu.SMEM(shape, jnp.int32) for shape in index_shapes]
        + [
            pltpu.VMEM((count + 1, size, size), jnp.float32),
            pltpu.SMEM((count,), jnp.int32),
            pltpu.SMEM((count,), jnp.int32),
            pltpu.SMEM((half * BC,), jnp.int32),
            pltpu.SemaphoreType.DMA((5,)),
            pltpu.SemaphoreType.DMA((8,)),
            pltpu.SemaphoreType.DMA((7,)),
            pltpu.SemaphoreType.DMA((SHIFTS * block_rows + half,)),
            pltpu.SemaphoreType.DMA((3,)),
            pltpu.SemaphoreType.DMA((2 * CHUNKS + 2,)),
            pltpu.SemaphoreType.DMA,
            pltpu.SemaphoreType.REGULAR((3,)),
            pltpu.SemaphoreType.DMA((7,)),
        ],
        compiler_params=pltpu.CompilerParams(
            collective_id=0, has_side_effects=True, vmem_limit_bytes=40 * 1024 * 1024
        ),
    )
    operands = [
        jnp.swapaxes(a_cols.reshape(block_rows, per_row), 0, 1),
        a_count.reshape(1, block_rows),
        b_cols.reshape(slots, 1, inner),
        b_count.reshape(slots, 1, inner),
        a_tiles.reshape(block_rows, per_row, size, size),
        b_tiles.reshape(slots, inner, size, size),
    ]
    return call(*(pltpu.with_memory_space_constraint(x, pltpu.HBM) for x in operands))


def solution(mesh):
    placed = (
        P("row", ("col", "depth"), None, None, None, None),
        P("row", ("col", "depth"), None, None),
        P("row", ("col", "depth"), None),
        P(None, "row", "depth", "col", None, None, None, None),
        P(None, "row", "depth", "col", None, None),
        P(None, "row", "depth", "col", None),
    )
    n_col = mesh.shape["col"]
    if mesh.shape["row"] == 2 and mesh.shape["depth"] == 2 and n_col == 2 * SHIFTS:
        body = functools.partial(local_fast, n_col)
    else:
        body = local
    return jax.shard_map(
        body, mesh=mesh, in_specs=placed, out_specs=P(("row", "depth"), "col"), check_vma=False
    )
```

```python
import functools
import math

import jax
import jax.numpy as jnp
from jax import lax
from jax.experimental import pallas as pl
from jax.experimental.pallas import tpu as pltpu
from jax.sharding import PartitionSpec as P

BC = 12
SHIFTS = 4


def for_sending(array):
    return jax.tree.map(lambda a: a.astype(jnp.bfloat16) if a.dtype == jnp.float32 else a, array)


def shifted(value, axis, steps):
    count = lax.axis_size(axis)
    pairs = [(source, (source + steps) % count) for source in range(count)]
    return lax.ppermute(value, axis, pairs)


def dense_panel(tiles_b, cols_b, count_b, width):
    slot_ids = lax.broadcasted_iota(jnp.int32, cols_b.shape, 1)
    valid_slot = slot_ids < count_b[:, None]
    targets = lax.broadcasted_iota(jnp.int32, (1, 1, width), 2)
    placing = jnp.logical_and(cols_b[:, :, None] == targets, valid_slot[:, :, None]).astype(
        jnp.bfloat16
    )
    spread = jnp.einsum("kuc,kuab->kacb", placing, tiles_b, preferred_element_type=jnp.float32)
    inner_blocks = tiles_b.shape[0]
    tile_size = tiles_b.shape[2]
    return spread.astype(jnp.bfloat16).reshape(inner_blocks, tile_size, width * tile_size)


def panel_product(tiles_a, cols_a, count_a, rows_dense):
    block_rows = tiles_a.shape[0]
    per_row = tiles_a.shape[1]
    tile_size = tiles_a.shape[2]
    slot_ids = lax.broadcasted_iota(jnp.int32, cols_a.shape, 1)
    valid_slot = slot_ids < count_a[:, None]
    masked = jnp.where(valid_slot[:, :, None, None], tiles_a, jnp.zeros_like(tiles_a))
    group_rows = math.gcd(block_rows, 4)

    def one_group(pieces):
        tiles_part, cols_part = pieces
        picks = lax.broadcasted_iota(jnp.int32, cols_part.shape + (rows_dense.shape[0],), 2)
        picks = (cols_part[:, :, None] == picks).astype(rows_dense.dtype)
        chosen = jnp.einsum("rtk,kbn->rtbn", picks, rows_dense, preferred_element_type=jnp.float32)
        chosen = chosen.astype(rows_dense.dtype)
        return jnp.einsum("rtab,rtbn->ran", tiles_part, chosen, preferred_element_type=jnp.float32)

    grouped = lax.map(
        one_group,
        (
            masked.reshape(block_rows // group_rows, group_rows, per_row, tile_size, tile_size),
            cols_a.reshape(block_rows // group_rows, group_rows, per_row),
        ),
    )
    return grouped.reshape(block_rows, tile_size, rows_dense.shape[2])


def roll_slots(stack, offset):
    slot_total = stack[0].shape[0]
    return tuple(
        (
            lax.dynamic_slice_in_dim(
                jnp.concatenate([member, member], 0), offset % slot_total, slot_total, 0
            )
            for member in stack
        )
    )


def select_if(flag, fresh, stale):
    return tuple((jnp.where(flag, new_part, old_part) for new_part, old_part in zip(fresh, stale)))


def local(a_tiles, a_cols, a_count, b_tiles, b_cols, b_count):
    rows_axis = lax.axis_size("row")
    cols_axis = lax.axis_size("col")
    row_group = lax.axis_index("row")
    col_group = lax.axis_index("col")
    tiles_a = a_tiles[0, 0]
    cols_a = a_cols[0, 0]
    count_a = a_count[0, 0]
    tiles_b = b_tiles[:, 0, 0, 0]
    cols_b = b_cols[:, 0, 0, 0]
    count_b = b_count[:, 0, 0, 0]
    for bit_pos in range((rows_axis - 1).bit_length()):
        stride = 1 << bit_pos
        moved = (
            shifted(tiles_a, "col", cols_axis - stride),
            shifted(for_sending(cols_a), "col", cols_axis - stride).astype(cols_a.dtype),
            shifted(for_sending(count_a), "col", cols_axis - stride).astype(count_a.dtype),
        )
        tiles_a, cols_a, count_a = select_if(
            row_group // stride % 2 == 1, moved, (tiles_a, cols_a, count_a)
        )
    for bit_pos in range((cols_axis - 1).bit_length()):
        stride = 1 << bit_pos
        nearby = stride % rows_axis
        if nearby:
            moved = (
                shifted(tiles_b, "row", rows_axis - nearby),
                shifted(for_sending(cols_b), "row", rows_axis - nearby).astype(cols_b.dtype),
                shifted(for_sending(count_b), "row", rows_axis - nearby).astype(count_b.dtype),
            )
        else:
            moved = (tiles_b, cols_b, count_b)
        moved = roll_slots(moved, (row_group + stride) // rows_axis)
        tiles_b, cols_b, count_b = select_if(
            col_group // stride % 2 == 1, moved, (tiles_b, cols_b, count_b)
        )
    tile_size = tiles_a.shape[2]
    running = jnp.zeros((tiles_a.shape[0], tile_size, BC * tile_size), jnp.float32)
    for turn_no in range(SHIFTS):
        current_tiles = tiles_b[0]
        current_cols = cols_b[0]
        current_count = count_b[0]
        rows_dense = dense_panel(current_tiles, current_cols, current_count, BC)
        running = running + panel_product(tiles_a, cols_a, count_a, rows_dense)
        if turn_no + 1 < SHIFTS:
            tiles_a, cols_a, count_a = (
                shifted(tiles_a, "col", cols_axis - 1),
                shifted(for_sending(cols_a), "col", cols_axis - 1).astype(cols_a.dtype),
                shifted(for_sending(count_a), "col", cols_axis - 1).astype(count_a.dtype),
            )
            moved = (
                shifted(tiles_b, "row", rows_axis - 1),
                shifted(for_sending(cols_b), "row", rows_axis - 1).astype(cols_b.dtype),
                shifted(for_sending(count_b), "row", rows_axis - 1).astype(count_b.dtype),
            )
            tiles_b, cols_b, count_b = roll_slots(moved, (row_group + 1) // rows_axis)
    flat_running = running.reshape(-1, running.shape[2])
    summed = lax.psum(flat_running, "depth")
    half_rows = flat_running.shape[0] // lax.axis_size("depth")
    own_rows = lax.dynamic_slice_in_dim(summed, lax.axis_index("depth") * half_rows, half_rows, 0)
    return own_rows.astype(jnp.bfloat16)


REACH = SHIFTS + 1
PARTS = ((8, 8), (7, 6, 3))
LATE = 1
MESH_ID = pl.DeviceIdType.MESH


def gather_multiply(n_col, a_cols, a_count, b_cols, b_count, a_ref, b_ref, out_ref, A, Bn0, Bn1, Bf0, Bf1,
                    Gn0, Gn1, Gf0, Gf1, MA, MB, SA, SB, run, ktab, ptab, ltab,
                    send_m, recv_m, send_a, recv_a, send_b, recv_b, passed, ready, local_sem):
    row = lax.axis_index("row")
    col = lax.axis_index("col")
    dep = lax.axis_index("depth")
    side = lax.rem(col, 2)
    z = lax.div(col, 2)
    top = n_col // 2 - 1
    per_row, size = A.shape[1:3]
    units = A.shape[0] // REACH
    half = units // 2
    inner = Bn0.shape[0]
    out_cols = out_ref.shape[1] // size
    terms = SHIFTS * 2 * per_row
    zero_at = half * terms
    row0, row1, side0, side1 = row == 0, row == 1, side == 0, side == 1

    def both(*flags):
        return functools.reduce(jnp.logical_and, flags)

    def at(col_offset, flip_depth=False, flip_row=False):
        return (
            1 - row if flip_row else row,
            lax.rem(col + col_offset + n_col, n_col),
            1 - dep if flip_depth else dep,
        )

    twin_dev, row_dev = at(0, True), at(0, False, True)
    side_dev = (row, col + 1 - 2 * side, dep)
    down, up, down2, up2 = at(-2), at(2), at(-4), at(4)

    def remote(src, dst, ssem, rsem, dev):
        return pltpu.make_async_remote_copy(
            src_ref=src, dst_ref=dst, send_sem=ssem, recv_sem=rsem, device_id=dev, device_id_type=MESH_ID
        )

    def signal(sem, dev):
        pl.semaphore_signal(sem, inc=1, device_id=dev, device_id_type=MESH_ID)

    def drain(ref, sem):
        pltpu.make_async_copy(ref, ref, sem).wait()

    def start(copies, *flags):
        def go():
            for copy in copies:
                copy.start()

        if flags:
            pl.when(both(*flags))(go)
        else:
            go()

    s_near = [side + 2 * k for k in range(2)]
    s_far = [1 - side + 2 * k for k in range(2)]
    m_near = [lax.rem(row + col + s, n_col) // 2 for s in s_near]
    m_far = [lax.rem(1 - row + col + s, n_col) // 2 for s in s_far]
    m_mine = [lax.rem(row + col + s, n_col) // 2 for s in s_far]
    near_own, near_twin = (Bn0, Bn1), (Gn0, Gn1)
    far_own, far_twin = (Bf0, Bf1), (Gf0, Gf1)

    index_local = [
        pltpu.make_async_copy(src, dst, local_sem.at[n])
        for src, dst, n in (
            (a_cols, MA.at[0, pl.ds(0, per_row)], 0), (a_count, MA.at[0, pl.ds(per_row, 1)], 0),
            (b_cols, MB.at[0, 0], 1), (b_count, MB.at[0, 1], 1),
        )
    ]
    b_local = [pltpu.make_async_copy(b_ref.at[m_near[k]], near_own[k], local_sem.at[2]) for k in range(2)]
    a_local = pltpu.make_async_copy(a_ref.at[pl.ds(dep * half, half)], A.at[pl.ds(0, half)], local_sem.at[2])
    start(index_local + b_local + [a_local])

    @pl.when(row0)
    def _():
        for slot in range(2 * SHIFTS, 2 * REACH):
            MA[slot] = jnp.zeros(MA.shape[1:], MA.dtype)

    barrier = pltpu.get_barrier_semaphore()
    signal(barrier, twin_dev)
    pl.when(row0)(lambda: signal(barrier, row_dev))
    pl.when(side0)(lambda: signal(barrier, side_dev))
    pl.when(z < top)(lambda: signal(barrier, up))
    pl.when(z == 0)(lambda: signal(barrier, down))
    pl.when(both(row1, z == 1))(lambda: signal(barrier, down2))
    greeted = 1 + row + side + jnp.where(z > 0, 1, 0) + jnp.where(z == top, 1 + row, 0)
    pl.semaphore_wait(barrier, greeted)
    pl.when(row1)(lambda: signal(ready.at[0], row_dev))
    pl.when(side1)(lambda: signal(ready.at[1], side_dev))
    pl.when(z == top)(lambda: signal(ready.at[2], up))
    pl.when(both(row1, z == top))(lambda: signal(ready.at[2], up2))

    def unit(p, u):
        return A.at[p * units + u]

    own = [a_ref.at[dep * half + r] for r in range(half)] + [unit(0, half + r) for r in range(half)]

    def landed(p, u):
        return recv_a.at[(SHIFTS - 1) * units + u // 2 if p == 1 else (p - 2) * units + u]

    def to_panel(p, sources, n, dev):
        return [remote(src, unit(p, u), send_a.at[n], landed(p, u), dev) for u, src in enumerate(sources)]

    def panel(p):
        return [unit(p, u) for u in range(units)]

    swap = [
        remote(a_ref.at[(1 - dep) * half + r], unit(0, half + r), send_a.at[0], recv_a.at[(SHIFTS - 1) * units + half + r // 2], twin_dev)
        for r in range(half)
    ]
    chain = to_panel(2, own, 0, down)
    chain2 = to_panel(4, panel(2), 1, down)
    skip = to_panel(4, own, 1, down2)
    own_x1 = to_panel(1, own, 0, side_dev)
    fwd_x1 = to_panel(1, panel(2), 0, side_dev)
    fwd_x3 = to_panel(3, panel(2), 2, side_dev)
    top_x3 = to_panel(3, panel(4)[: units - LATE], 2, side_dev)
    low_x3 = to_panel(3, panel(1), 2, down)

    near_b = [remote(b_ref.at[m_near[k]], near_twin[k], send_b, passed.at[2], twin_dev) for k in range(2)]
    far_b, pass_b = [], []
    for k, sizes in enumerate(PARTS):
        for c, blocks in enumerate(sizes):
            part = pl.ds(sum(sizes[:c]) * inner // 16, blocks * inner // 16)
            far_b.append(
                remote(b_ref.at[m_far[k], part], far_own[k].at[part], send_b, recv_b.at[len(far_b)], row_dev)
            )
            pass_b.append(remote(far_own[k].at[part], far_twin[k].at[part], send_b, passed.at[k], twin_dev))

    def index_a(src, dst, n, sem, dev):
        return remote(MA.at[pl.ds(src, n)], MA.at[pl.ds(dst, n)], send_m.at[sem], recv_m.at[min(dst // 2, 3)], dev)

    swap_m = remote(MA.at[0], MA.at[1], send_m.at[0], recv_m.at[0], twin_dev)
    near_m = remote(MB.at[0], MB.at[1], send_m.at[1], recv_m.at[4], twin_dev)
    far_m = remote(MB.at[0], MB.at[2], send_m.at[1], recv_m.at[5], row_dev)
    pass_m = remote(MB.at[2], MB.at[3], send_m.at[1], recv_m.at[4], twin_dev)
    chain_m, chain2_m, skip_m = index_a(0, 4, 2, 0, down), index_a(4, 8, 2, 2, down), index_a(0, 8, 2, 3, down2)
    own_x1_m, fwd_x1_m = index_a(0, 2, 2, 0, side_dev), index_a(4, 2, 2, 0, side_dev)
    fwd_x3_m, low_x3_m = index_a(4, 6, 2, 4, side_dev), index_a(2, 6, 2, 4, down)

    drain(MA.at[0], local_sem.at[0])
    drain(MB.at[0], local_sem.at[1])
    start([swap_m] + swap)
    start(chain[:2], z > 0)
    start(own_x1[:2], side1)
    pl.when(row0)(lambda: pl.semaphore_wait(ready.at[0], 1))
    start([far_m] + far_b + [near_m] + near_b)
    swap_m.wait_recv()
    start([chain_m] + chain[2:half], z > 0)
    start([own_x1_m] + own_x1[2:half], side1)
    for n in range(half // 2):
        drain(A.at[pl.ds(0, 2)], recv_a.at[(SHIFTS - 1) * units + half + n])

    @pl.when(z == 0)
    def _():
        pl.semaphore_wait(ready.at[2], 1)
        start([chain_m] + chain[:half])

    @pl.when(both(row1, z == 1))
    def _():
        pl.semaphore_wait(ready.at[2], 1)
        start([skip_m] + skip)

    pl.when(side0)(lambda: pl.semaphore_wait(ready.at[1], 1))
    run[zero_at] = jnp.zeros(run.shape[1:], jnp.float32)

    def far_part(n):
        far_b[n].wait_recv()
        pass_b[n].start()

    def low(u):
        drain(A.at[pl.ds(0, 2)], landed(1, u))
        for w in (u, u + 1):
            start([low_x3[w]], side1, *([] if w >= units - LATE else [row0]))

    def recv(p, u):
        drain(unit(p, u), landed(p, u))

    groups = [(s, m, k, d, far) for k in range(2) for far, s, m in ((0, s_near[k], m_near[k]), (1, s_far[k], m_mine[k]))
              for d in range(2)]

    def tables(r):
        cs = []
        for s, m, _, d, far in groups:
            slot = (s + row) * 2 + d
            used = SA[slot, per_row, dep * half + r]
            for t in range(per_row):
                k = SA[slot, t, dep * half + r]
                c = SB[2 * far + d, 0, m, 0, k]
                ok = jnp.logical_and(used > t, SB[2 * far + d, 1, m, 0, k] > 0)
                c = jnp.where(ok, c, -1)
                here = r * terms + len(cs)
                before = jnp.int32(zero_at)
                for at_p, c_p in enumerate(cs):
                    before = jnp.where(c_p == c, r * terms + at_p, before)
                ktab[here] = k
                ptab[here] = before
                cs.append(c)
        for c in range(out_cols):
            last = jnp.int32(zero_at)
            for at_p, c_p in enumerate(cs):
                last = jnp.where(c_p == c, r * terms + at_p, last)
            ltab[r * out_cols + c] = last

    rights = (Bn0, Gn0, Bf0, Gf0, Bn1, Gn1, Bf1, Gf1)

    def products(wanted):
        held = None
        for g, r in wanted:
            s, _, _, d, _ = groups[g]
            for t in range(per_row):
                here = r * terms + g * per_row + t
                left = A[(s + row) * units + d * half + r, t]
                value = jnp.dot(left, rights[g][ktab[here]], preferred_element_type=jnp.float32)
                if held is not None:
                    run[held[0]] = held[1] + run[ptab[held[0]]]
                held = here, value
        run[held[0]] = held[1] + run[ptab[held[0]]]

    def whole_group(g):
        products([(g, r) for r in range(half)])

    for u in range(units):
        recv(2, u)
        if u == 0:
            drain(MA.at[pl.ds(4, 2)], recv_m.at[2])
            start([chain2_m], row1, z > 0)
            start([fwd_x1_m], side0)
            start([fwd_x3_m], side1)
        start([fwd_x1[u]], side0)
        if u == 2:
            drain(MA.at[pl.ds(2, 2)], recv_m.at[1])
            start([low_x3_m], side1)
        if u < half:
            start([chain[half + u]])
            start([own_x1[half + u]], side1)
        else:
            start(chain2[2 * (u - half) : 2 * (u - half) + 2], row1, z > 0)
            start(fwd_x3[2 * (u - half) : 2 * (u - half) + 2], side1)
        if u == 0:
            far_m.wait_recv()
            pass_m.start()
        if u in (4, 6):
            low(u - 4)
        if u in (3, 7):
            far_part(u // 4)

    def near_units(*wanted):
        @pl.when(row != side)
        def _():
            for u in wanted:
                recv(3, u)

        @pl.when(both(row1, side1))
        def _():
            for u in wanted:
                recv(4, u)

        products([(4 + u // half, u % half) for u in wanted])

    def far_units(*wanted):
        @pl.when(row == side)
        def _():
            for u in wanted:
                recv(3, u)

        if units - 1 in wanted:
            pl.when(both(row1, side0))(lambda: recv(4, units - 1))
        products([(6 + u // half, u % half) for u in wanted])

    scalars = [pltpu.make_async_copy(MA, SA, local_sem.at[0]), pltpu.make_async_copy(MB, SB, local_sem.at[1])]

    for u in range(units):
        if u < units - LATE:
            @pl.when(both(row1, side0))
            def _():
                recv(4, u)
                top_x3[u].start()

        if u in (0, 2):
            low(half + u)
        if u == 0:
            pl.when(row0)(lambda: drain(MA.at[pl.ds(6, 2)], recv_m.at[3]))
            pl.when(row1)(lambda: drain(MA.at[pl.ds(6, 4)], recv_m.at[3]))
            drain(MB.at[pl.ds(0, 2)], recv_m.at[4])
            start(scalars)
        if u == 1:
            for copy in scalars:
                copy.wait()
            drain(A.at[pl.ds(0, 2 * units + half)], local_sem.at[2])
            drain(A.at[pl.ds(0, 2 * units)], passed.at[2])
            drain(A.at[pl.ds(0, units)], passed.at[0])
        if u in (3, 5):
            far_part((u + 1) // 2)
        if u in (1, 2):
            for r in range((u - 1) * half // 2, u * half // 2):
                tables(r)
        if u == 2:
            whole_group(0)
        if u == 3:
            whole_group(1)
            whole_group(2)
        if u == 4:
            whole_group(3)
            near_units(0)
        if u == 5:
            near_units(1, 2)
        if u == 6:
            near_units(3, 4)
    far_part(len(far_b) - 1)

    def place(*rows):
        for r in rows:
            for c in range(out_cols):
                out_ref[r * size : (r + 1) * size, c * size : (c + 1) * size] = run[ltab[r * out_cols + c]].astype(
                    out_ref.dtype
                )

    def last_pass():
        drain(A.at[pl.ds(0, units)], passed.at[1])

    @pl.when(z < top)
    def _():
        near_units(5, 6, 7)
        far_units(0, 1, 2, 3)
        last_pass()
        far_units(4, 5, 6, 7)
        place(0, 1, 2, 3)

    @pl.when(z == top)
    def _():
        far_units(0)
        near_units(5)
        far_units(1)
        last_pass()
        far_units(4, 5)
        place(0, 1)
        near_units(6)
        far_units(2)
        far_units(6)
        place(2)
        near_units(7)
        far_units(3)
        far_units(7)
        place(3)

    def sent(n, sem, *flags):
        if flags:
            pl.when(both(*flags))(lambda: drain(A.at[pl.ds(0, n)], sem))
        else:
            drain(A.at[pl.ds(0, n)], sem)

    sent(2 * units + half, send_a.at[0])
    sent(units, send_a.at[1], row1, z > 1)
    sent(2 * units, send_a.at[1], row1, z == 1)
    sent(2 * units, send_a.at[2], side1, row0)
    sent(units + LATE, send_a.at[2], side1, row1)
    sent(units - LATE, send_a.at[2], side0, row1)
    drain(run.at[pl.ds(0, 6 * units)], send_b)
    drain(MA.at[pl.ds(0, 5)], send_m.at[0])
    drain(MB.at[pl.ds(0, 3)], send_m.at[1])
    pl.when(both(row1, z > 0))(lambda: drain(MA.at[pl.ds(0, 2)], send_m.at[2]))
    pl.when(both(row1, z == 1))(lambda: drain(MA.at[pl.ds(0, 2)], send_m.at[3]))
    pl.when(side1)(lambda: drain(MA.at[pl.ds(0, 4)], send_m.at[4]))


def local_fast(n_col, a_tiles, a_cols, a_count, b_tiles, b_cols, b_count):
    block_rows, per_row, size = a_tiles.shape[2:5]
    slots, inner = b_tiles.shape[0], b_tiles.shape[4]
    half = block_rows // 2
    count = half * SHIFTS * 2 * per_row
    hbm = pl.BlockSpec(memory_space=pltpu.HBM)
    index_shapes = [(REACH * 2, per_row + 1, block_rows), (4, 2, slots, 1, inner)]
    call = pl.pallas_call(
        functools.partial(gather_multiply, n_col),
        out_shape=jax.ShapeDtypeStruct((half * size, BC * size), jnp.bfloat16),
        in_specs=[hbm] * 6,
        out_specs=pl.BlockSpec(memory_space=pltpu.VMEM),
        scratch_shapes=[pltpu.VMEM((REACH * block_rows, per_row, size, size), jnp.bfloat16)]
        + [pltpu.VMEM((inner, size, size), jnp.bfloat16)] * 8
        + [pltpu.VMEM(shape, jnp.int32) for shape in index_shapes]
        + [pltpu.SMEM(shape, jnp.int32) for shape in index_shapes]
        + [
            pltpu.VMEM((count + 1, size, size), jnp.float32),
            pltpu.SMEM((count,), jnp.int32),
            pltpu.SMEM((count,), jnp.int32),
            pltpu.SMEM((half * BC,), jnp.int32),
            pltpu.SemaphoreType.DMA((5,)),
            pltpu.SemaphoreType.DMA((6,)),
            pltpu.SemaphoreType.DMA((3,)),
            pltpu.SemaphoreType.DMA(((SHIFTS - 1) * block_rows + half + half // 2,)),
            pltpu.SemaphoreType.DMA,
            pltpu.SemaphoreType.DMA((sum(map(len, PARTS)),)),
            pltpu.SemaphoreType.DMA((3,)),
            pltpu.SemaphoreType.REGULAR((3,)),
            pltpu.SemaphoreType.DMA((3,)),
        ],
        compiler_params=pltpu.CompilerParams(
            collective_id=0, has_side_effects=True, vmem_limit_bytes=40 * 1024 * 1024
        ),
    )
    operands = [
        jnp.swapaxes(a_cols.reshape(block_rows, per_row), 0, 1),
        a_count.reshape(1, block_rows),
        b_cols.reshape(slots, 1, inner),
        b_count.reshape(slots, 1, inner),
        a_tiles.reshape(block_rows, per_row, size, size),
        b_tiles.reshape(slots, inner, size, size),
    ]
    return call(*(pltpu.with_memory_space_constraint(x, pltpu.HBM) for x in operands))


def solution(mesh):
    placed = (
        P("row", ("col", "depth"), None, None, None, None),
        P("row", ("col", "depth"), None, None),
        P("row", ("col", "depth"), None),
        P(None, "row", "depth", "col", None, None, None, None),
        P(None, "row", "depth", "col", None, None),
        P(None, "row", "depth", "col", None),
    )
    n_col = mesh.shape["col"]
    if mesh.shape["row"] == 2 and mesh.shape["depth"] == 2 and n_col == 2 * SHIFTS:
        body = functools.partial(local_fast, n_col)
    else:
        body = local
    return jax.shard_map(
        body, mesh=mesh, in_specs=placed, out_specs=P(("row", "depth"), "col"), check_vma=False
    )
```

```python
import functools
import math

import jax
import jax.numpy as jnp
from jax import lax
from jax.experimental import pallas as pl
from jax.experimental.pallas import tpu as pltpu
from jax.sharding import PartitionSpec as P

BC = 12
SHIFTS = 4


def for_sending(array):
    return jax.tree.map(lambda a: a.astype(jnp.bfloat16) if a.dtype == jnp.float32 else a, array)


def shifted(value, axis, steps):
    count = lax.axis_size(axis)
    pairs = [(source, (source + steps) % count) for source in range(count)]
    return lax.ppermute(value, axis, pairs)


def dense_panel(tiles_b, cols_b, count_b, width):
    slot_ids = lax.broadcasted_iota(jnp.int32, cols_b.shape, 1)
    valid_slot = slot_ids < count_b[:, None]
    targets = lax.broadcasted_iota(jnp.int32, (1, 1, width), 2)
    placing = jnp.logical_and(cols_b[:, :, None] == targets, valid_slot[:, :, None]).astype(
        jnp.bfloat16
    )
    spread = jnp.einsum("kuc,kuab->kacb", placing, tiles_b, preferred_element_type=jnp.float32)
    inner_blocks = tiles_b.shape[0]
    tile_size = tiles_b.shape[2]
    return spread.astype(jnp.bfloat16).reshape(inner_blocks, tile_size, width * tile_size)


def panel_product(tiles_a, cols_a, count_a, rows_dense):
    block_rows = tiles_a.shape[0]
    per_row = tiles_a.shape[1]
    tile_size = tiles_a.shape[2]
    slot_ids = lax.broadcasted_iota(jnp.int32, cols_a.shape, 1)
    valid_slot = slot_ids < count_a[:, None]
    masked = jnp.where(valid_slot[:, :, None, None], tiles_a, jnp.zeros_like(tiles_a))
    group_rows = math.gcd(block_rows, 4)

    def one_group(pieces):
        tiles_part, cols_part = pieces
        picks = lax.broadcasted_iota(jnp.int32, cols_part.shape + (rows_dense.shape[0],), 2)
        picks = (cols_part[:, :, None] == picks).astype(rows_dense.dtype)
        chosen = jnp.einsum("rtk,kbn->rtbn", picks, rows_dense, preferred_element_type=jnp.float32)
        chosen = chosen.astype(rows_dense.dtype)
        return jnp.einsum("rtab,rtbn->ran", tiles_part, chosen, preferred_element_type=jnp.float32)

    grouped = lax.map(
        one_group,
        (
            masked.reshape(block_rows // group_rows, group_rows, per_row, tile_size, tile_size),
            cols_a.reshape(block_rows // group_rows, group_rows, per_row),
        ),
    )
    return grouped.reshape(block_rows, tile_size, rows_dense.shape[2])


def roll_slots(stack, offset):
    slot_total = stack[0].shape[0]
    return tuple(
        (
            lax.dynamic_slice_in_dim(
                jnp.concatenate([member, member], 0), offset % slot_total, slot_total, 0
            )
            for member in stack
        )
    )


def select_if(flag, fresh, stale):
    return tuple((jnp.where(flag, new_part, old_part) for new_part, old_part in zip(fresh, stale)))


def local(a_tiles, a_cols, a_count, b_tiles, b_cols, b_count):
    rows_axis = lax.axis_size("row")
    cols_axis = lax.axis_size("col")
    row_group = lax.axis_index("row")
    col_group = lax.axis_index("col")
    tiles_a = a_tiles[0, 0]
    cols_a = a_cols[0, 0]
    count_a = a_count[0, 0]
    tiles_b = b_tiles[:, 0, 0, 0]
    cols_b = b_cols[:, 0, 0, 0]
    count_b = b_count[:, 0, 0, 0]
    for bit_pos in range((rows_axis - 1).bit_length()):
        stride = 1 << bit_pos
        moved = (
            shifted(tiles_a, "col", cols_axis - stride),
            shifted(for_sending(cols_a), "col", cols_axis - stride).astype(cols_a.dtype),
            shifted(for_sending(count_a), "col", cols_axis - stride).astype(count_a.dtype),
        )
        tiles_a, cols_a, count_a = select_if(
            row_group // stride % 2 == 1, moved, (tiles_a, cols_a, count_a)
        )
    for bit_pos in range((cols_axis - 1).bit_length()):
        stride = 1 << bit_pos
        nearby = stride % rows_axis
        if nearby:
            moved = (
                shifted(tiles_b, "row", rows_axis - nearby),
                shifted(for_sending(cols_b), "row", rows_axis - nearby).astype(cols_b.dtype),
                shifted(for_sending(count_b), "row", rows_axis - nearby).astype(count_b.dtype),
            )
        else:
            moved = (tiles_b, cols_b, count_b)
        moved = roll_slots(moved, (row_group + stride) // rows_axis)
        tiles_b, cols_b, count_b = select_if(
            col_group // stride % 2 == 1, moved, (tiles_b, cols_b, count_b)
        )
    tile_size = tiles_a.shape[2]
    running = jnp.zeros((tiles_a.shape[0], tile_size, BC * tile_size), jnp.float32)
    for turn_no in range(SHIFTS):
        current_tiles = tiles_b[0]
        current_cols = cols_b[0]
        current_count = count_b[0]
        rows_dense = dense_panel(current_tiles, current_cols, current_count, BC)
        running = running + panel_product(tiles_a, cols_a, count_a, rows_dense)
        if turn_no + 1 < SHIFTS:
            tiles_a, cols_a, count_a = (
                shifted(tiles_a, "col", cols_axis - 1),
                shifted(for_sending(cols_a), "col", cols_axis - 1).astype(cols_a.dtype),
                shifted(for_sending(count_a), "col", cols_axis - 1).astype(count_a.dtype),
            )
            moved = (
                shifted(tiles_b, "row", rows_axis - 1),
                shifted(for_sending(cols_b), "row", rows_axis - 1).astype(cols_b.dtype),
                shifted(for_sending(count_b), "row", rows_axis - 1).astype(count_b.dtype),
            )
            tiles_b, cols_b, count_b = roll_slots(moved, (row_group + 1) // rows_axis)
    flat_running = running.reshape(-1, running.shape[2])
    summed = lax.psum(flat_running, "depth")
    half_rows = flat_running.shape[0] // lax.axis_size("depth")
    own_rows = lax.dynamic_slice_in_dim(summed, lax.axis_index("depth") * half_rows, half_rows, 0)
    return own_rows.astype(jnp.bfloat16)


REACH = SHIFTS + 1
PARTS = ((8, 8), (7, 6, 3))
LATE = 1
SPLIT = 6
MESH_ID = pl.DeviceIdType.MESH


def gather_multiply(n_col, a_cols, a_count, b_cols, b_count, a_ref, b_ref, out_ref, A, Bn0, Bn1, Bf0, Bf1,
                    Gn0, Gn1, Gf0, Gf1, MA, MB, SA, SB, run, ktab, ptab, ltab,
                    send_m, recv_m, send_a, recv_a, send_b, recv_b, passed, halves, ready, local_sem):
    row = lax.axis_index("row")
    col = lax.axis_index("col")
    dep = lax.axis_index("depth")
    side = lax.rem(col, 2)
    z = lax.div(col, 2)
    top = n_col // 2 - 1
    per_row, size = A.shape[1:3]
    units = A.shape[0] // REACH
    half = units // 2
    inner = Bn0.shape[0]
    out_cols = out_ref.shape[1] // size
    terms = SHIFTS * 2 * per_row
    zero_at = half * terms
    row0, row1, side0, side1 = row == 0, row == 1, side == 0, side == 1

    def both(*flags):
        return functools.reduce(jnp.logical_and, flags)

    def at(col_offset, flip_depth=False, flip_row=False):
        return (
            1 - row if flip_row else row,
            lax.rem(col + col_offset + n_col, n_col),
            1 - dep if flip_depth else dep,
        )

    twin_dev, row_dev = at(0, True), at(0, False, True)
    side_dev = (row, col + 1 - 2 * side, dep)
    down, up, down2, up2 = at(-2), at(2), at(-4), at(4)

    def remote(src, dst, ssem, rsem, dev):
        return pltpu.make_async_remote_copy(
            src_ref=src, dst_ref=dst, send_sem=ssem, recv_sem=rsem, device_id=dev, device_id_type=MESH_ID
        )

    def signal(sem, dev):
        pl.semaphore_signal(sem, inc=1, device_id=dev, device_id_type=MESH_ID)

    def drain(ref, sem):
        pltpu.make_async_copy(ref, ref, sem).wait()

    def start(copies, *flags):
        def go():
            for copy in copies:
                copy.start()

        if flags:
            pl.when(both(*flags))(go)
        else:
            go()

    s_near = [side + 2 * k for k in range(2)]
    s_far = [1 - side + 2 * k for k in range(2)]
    m_near = [lax.rem(row + col + s, n_col) // 2 for s in s_near]
    m_far = [lax.rem(1 - row + col + s, n_col) // 2 for s in s_far]
    m_mine = [lax.rem(row + col + s, n_col) // 2 for s in s_far]
    near_own, near_twin = (Bn0, Bn1), (Gn0, Gn1)
    far_own, far_twin = (Bf0, Bf1), (Gf0, Gf1)

    index_local = [
        pltpu.make_async_copy(src, dst, local_sem.at[n])
        for src, dst, n in (
            (a_cols, MA.at[0, pl.ds(0, per_row)], 0), (a_count, MA.at[0, pl.ds(per_row, 1)], 0),
            (b_cols, MB.at[0, 0], 1), (b_count, MB.at[0, 1], 1),
        )
    ]
    b_local = [pltpu.make_async_copy(b_ref.at[m_near[k]], near_own[k], local_sem.at[2]) for k in range(2)]
    a_local = pltpu.make_async_copy(a_ref.at[pl.ds(dep * half, half)], A.at[pl.ds(0, half)], local_sem.at[2])
    start(index_local + b_local + [a_local])

    @pl.when(row0)
    def _():
        for slot in range(2 * SHIFTS, 2 * REACH):
            MA[slot] = jnp.zeros(MA.shape[1:], MA.dtype)

    barrier = pltpu.get_barrier_semaphore()
    signal(barrier, twin_dev)
    pl.when(row0)(lambda: signal(barrier, row_dev))
    pl.when(side0)(lambda: signal(barrier, side_dev))
    pl.when(z < top)(lambda: signal(barrier, up))
    pl.when(z == 0)(lambda: signal(barrier, down))
    pl.when(both(row1, z == 1))(lambda: signal(barrier, down2))
    greeted = 1 + row + side + jnp.where(z > 0, 1, 0) + jnp.where(z == top, 1 + row, 0)
    pl.semaphore_wait(barrier, greeted)
    pl.when(row1)(lambda: signal(ready.at[0], row_dev))
    pl.when(side1)(lambda: signal(ready.at[1], side_dev))
    pl.when(z == top)(lambda: signal(ready.at[2], up))
    pl.when(both(row1, z == top))(lambda: signal(ready.at[2], up2))

    def unit(p, u):
        return A.at[p * units + u]

    own = [a_ref.at[dep * half + r] for r in range(half)] + [unit(0, half + r) for r in range(half)]

    def landed(p, u):
        return recv_a.at[(SHIFTS - 1) * units + u // 2 if p == 1 else (p - 2) * units + u]

    def to_panel(p, sources, n, dev, split=-1):
        copies = []
        for u, src in enumerate(sources):
            dst = unit(p, u)
            if u == split:
                for t in range(per_row):
                    sem = halves.at[t] if p == SHIFTS else landed(p, u)
                    copies.append(remote(src.at[t], dst.at[t], send_a.at[n], sem, dev))
            else:
                copies.append(remote(src, dst, send_a.at[n], landed(p, u), dev))
        return copies

    def panel(p):
        return [unit(p, u) for u in range(units)]

    swap = [
        remote(a_ref.at[(1 - dep) * half + r], unit(0, half + r), send_a.at[0], recv_a.at[(SHIFTS - 1) * units + half + r // 2], twin_dev)
        for r in range(half)
    ]
    chain = to_panel(2, own, 0, down)
    chain2 = to_panel(4, panel(2), 1, down, SPLIT)
    skip = to_panel(4, own, 1, down2, SPLIT)
    own_x1 = to_panel(1, own, 0, side_dev)
    fwd_x1 = to_panel(1, panel(2), 0, side_dev)
    fwd_x3 = to_panel(3, panel(2), 2, side_dev)
    top_x3 = to_panel(3, panel(4)[: units - LATE], 2, side_dev, SPLIT)
    low_x3 = to_panel(3, panel(1), 2, down)

    near_b = [remote(b_ref.at[m_near[k]], near_twin[k], send_b, passed.at[2], twin_dev) for k in range(2)]
    far_b, pass_b = [], []
    for k, sizes in enumerate(PARTS):
        for c, blocks in enumerate(sizes):
            part = pl.ds(sum(sizes[:c]) * inner // 16, blocks * inner // 16)
            far_b.append(
                remote(b_ref.at[m_far[k], part], far_own[k].at[part], send_b, recv_b.at[len(far_b)], row_dev)
            )
            pass_b.append(remote(far_own[k].at[part], far_twin[k].at[part], send_b, passed.at[k], twin_dev))

    def index_a(src, dst, n, sem, dev):
        return remote(MA.at[pl.ds(src, n)], MA.at[pl.ds(dst, n)], send_m.at[sem], recv_m.at[min(dst // 2, 3)], dev)

    swap_m = remote(MA.at[0], MA.at[1], send_m.at[0], recv_m.at[0], twin_dev)
    near_m = remote(MB.at[0], MB.at[1], send_m.at[1], recv_m.at[4], twin_dev)
    far_m = remote(MB.at[0], MB.at[2], send_m.at[1], recv_m.at[5], row_dev)
    pass_m = remote(MB.at[2], MB.at[3], send_m.at[1], recv_m.at[4], twin_dev)
    chain_m, chain2_m, skip_m = index_a(0, 4, 2, 0, down), index_a(4, 8, 2, 2, down), index_a(0, 8, 2, 3, down2)
    own_x1_m, fwd_x1_m = index_a(0, 2, 2, 0, side_dev), index_a(4, 2, 2, 0, side_dev)
    fwd_x3_m, low_x3_m = index_a(4, 6, 2, 4, side_dev), index_a(2, 6, 2, 4, down)

    drain(MA.at[0], local_sem.at[0])
    drain(MB.at[0], local_sem.at[1])
    start([swap_m] + swap)
    start(chain[:2], z > 0)
    start(own_x1[:2], side1)
    pl.when(row0)(lambda: pl.semaphore_wait(ready.at[0], 1))
    start([far_m] + far_b + [near_m] + near_b)
    swap_m.wait_recv()
    start([chain_m] + chain[2:half], z > 0)
    start([own_x1_m] + own_x1[2:half], side1)
    for n in range(half // 2):
        drain(A.at[pl.ds(0, 2)], recv_a.at[(SHIFTS - 1) * units + half + n])

    @pl.when(z == 0)
    def _():
        pl.semaphore_wait(ready.at[2], 1)
        start([chain_m] + chain[:half])

    @pl.when(both(row1, z == 1))
    def _():
        pl.semaphore_wait(ready.at[2], 1)
        start([skip_m] + skip)

    pl.when(side0)(lambda: pl.semaphore_wait(ready.at[1], 1))
    run[zero_at] = jnp.zeros(run.shape[1:], jnp.float32)

    def far_part(n):
        far_b[n].wait_recv()
        pass_b[n].start()

    def low(u):
        drain(A.at[pl.ds(0, 2)], landed(1, u))
        for w in (u, u + 1):
            start([low_x3[w]], side1, *([] if w >= units - LATE else [row0]))

    def recv(p, u):
        if p == 4 and u == SPLIT:
            for t in range(per_row):
                drain(unit(p, u).at[t], halves.at[t])
        else:
            drain(unit(p, u), landed(p, u))

    groups = [(s, m, k, d, far) for k in range(2) for far, s, m in ((0, s_near[k], m_near[k]), (1, s_far[k], m_mine[k]))
              for d in range(2)]

    def tables(r):
        cs = []
        for s, m, _, d, far in groups:
            slot = (s + row) * 2 + d
            used = SA[slot, per_row, dep * half + r]
            for t in range(per_row):
                k = SA[slot, t, dep * half + r]
                c = SB[2 * far + d, 0, m, 0, k]
                ok = jnp.logical_and(used > t, SB[2 * far + d, 1, m, 0, k] > 0)
                c = jnp.where(ok, c, -1)
                here = r * terms + len(cs)
                before = jnp.int32(zero_at)
                for at_p, c_p in enumerate(cs):
                    before = jnp.where(c_p == c, r * terms + at_p, before)
                ktab[here] = k
                ptab[here] = before
                cs.append(c)
        for c in range(out_cols):
            last = jnp.int32(zero_at)
            for at_p, c_p in enumerate(cs):
                last = jnp.where(c_p == c, r * terms + at_p, last)
            ltab[r * out_cols + c] = last

    rights = (Bn0, Gn0, Bf0, Gf0, Bn1, Gn1, Bf1, Gf1)

    def products(wanted):
        held = None
        for g, r in wanted:
            s, _, _, d, _ = groups[g]
            for t in range(per_row):
                here = r * terms + g * per_row + t
                left = A[(s + row) * units + d * half + r, t]
                value = jnp.dot(left, rights[g][ktab[here]], preferred_element_type=jnp.float32)
                if held is not None:
                    run[held[0]] = held[1] + run[ptab[held[0]]]
                held = here, value
        run[held[0]] = held[1] + run[ptab[held[0]]]

    def whole_group(g):
        products([(g, r) for r in range(half)])

    for u in range(units):
        recv(2, u)
        if u == 0:
            drain(MA.at[pl.ds(4, 2)], recv_m.at[2])
            start([chain2_m], row1, z > 0)
            start([fwd_x1_m], side0)
            start([fwd_x3_m], side1)
        start([fwd_x1[u]], side0)
        if u == 2:
            drain(MA.at[pl.ds(2, 2)], recv_m.at[1])
            start([low_x3_m], side1)
        if u < half:
            start([chain[half + u]])
            start([own_x1[half + u]], side1)
        else:
            start(chain2[2 * (u - half) : 2 * (u - half) + 2 + (u == units - 1)], row1, z > 0)
            start(fwd_x3[2 * (u - half) : 2 * (u - half) + 2], side1)
        if u == 0:
            far_m.wait_recv()
            pass_m.start()
        if u in (4, 6):
            low(u - 4)
        if u in (3, 7):
            far_part(u // 4)

    def near_units(*wanted):
        @pl.when(row != side)
        def _():
            for u in wanted:
                recv(3, u)

        @pl.when(both(row1, side1))
        def _():
            for u in wanted:
                recv(4, u)

        products([(4 + u // half, u % half) for u in wanted])

    def far_units(*wanted):
        @pl.when(row == side)
        def _():
            for u in wanted:
                recv(3, u)

        if units - 1 in wanted:
            pl.when(both(row1, side0))(lambda: recv(4, units - 1))
        products([(6 + u // half, u % half) for u in wanted])

    scalars = [pltpu.make_async_copy(MA, SA, local_sem.at[0]), pltpu.make_async_copy(MB, SB, local_sem.at[1])]

    for u in range(units):
        if u < units - LATE:
            @pl.when(both(row1, side0))
            def _():
                if u == SPLIT:
                    for t in range(per_row):
                        drain(unit(4, u).at[t], halves.at[t])
                        top_x3[u + t].start()
                else:
                    recv(4, u)
                    top_x3[u].start()

        if u in (0, 2):
            low(half + u)
        if u == 0:
            pl.when(row0)(lambda: drain(MA.at[pl.ds(6, 2)], recv_m.at[3]))
            pl.when(row1)(lambda: drain(MA.at[pl.ds(6, 4)], recv_m.at[3]))
            drain(MB.at[pl.ds(0, 2)], recv_m.at[4])
            start(scalars)
        if u == 1:
            for copy in scalars:
                copy.wait()
            drain(A.at[pl.ds(0, 2 * units + half)], local_sem.at[2])
            drain(A.at[pl.ds(0, 2 * units)], passed.at[2])
            drain(A.at[pl.ds(0, units)], passed.at[0])
        if u in (3, 5):
            far_part((u + 1) // 2)
        if u in (1, 2):
            for r in range((u - 1) * half // 2, u * half // 2):
                tables(r)
        if u == 2:
            whole_group(0)
        if u == 3:
            whole_group(1)
            whole_group(2)
        if u == 4:
            whole_group(3)
            near_units(0)
        if u == 5:
            near_units(1, 2)
    far_part(len(far_b) - 1)

    def place(*rows):
        for r in rows:
            for c in range(out_cols):
                out_ref[r * size : (r + 1) * size, c * size : (c + 1) * size] = run[ltab[r * out_cols + c]].astype(
                    out_ref.dtype
                )

    def last_pass():
        drain(A.at[pl.ds(0, units)], passed.at[1])

    @pl.when(side0)
    def _():
        near_units(3, 4, 5, 6, 7)
        far_units(0, 1, 2, 3)
        last_pass()
        far_units(4, 5, 6, 7)
        place(0, 1, 2, 3)

    @pl.when(both(side1, z < top))
    def _():
        near_units(3, 4, 5, 6, 7)
        far_units(0, 1, 2, 3)
        last_pass()
        far_units(4, 5)
        place(0, 1)
        far_units(6, 7)
        place(2, 3)

    @pl.when(both(side1, z == top))
    def _():
        near_units(3, 4)
        far_units(0)
        near_units(5)
        far_units(1)
        last_pass()
        near_units(6)
        far_units(2)
        far_units(4, 5)
        place(0, 1)
        near_units(7)
        far_units(3)
        far_units(6, 7)
        place(2, 3)

    def sent(n, sem, *flags):
        if flags:
            pl.when(both(*flags))(lambda: drain(A.at[pl.ds(0, n)], sem))
        else:
            drain(A.at[pl.ds(0, n)], sem)

    sent(2 * units + half, send_a.at[0])
    sent(units, send_a.at[1], row1, z > 1)
    sent(2 * units, send_a.at[1], row1, z == 1)
    sent(2 * units, send_a.at[2], side1, row0)
    sent(units + LATE, send_a.at[2], side1, row1)
    sent(units - LATE, send_a.at[2], side0, row1)
    drain(run.at[pl.ds(0, 6 * units)], send_b)
    drain(MA.at[pl.ds(0, 5)], send_m.at[0])
    drain(MB.at[pl.ds(0, 3)], send_m.at[1])
    pl.when(both(row1, z > 0))(lambda: drain(MA.at[pl.ds(0, 2)], send_m.at[2]))
    pl.when(both(row1, z == 1))(lambda: drain(MA.at[pl.ds(0, 2)], send_m.at[3]))
    pl.when(side1)(lambda: drain(MA.at[pl.ds(0, 4)], send_m.at[4]))


def local_fast(n_col, a_tiles, a_cols, a_count, b_tiles, b_cols, b_count):
    block_rows, per_row, size = a_tiles.shape[2:5]
    slots, inner = b_tiles.shape[0], b_tiles.shape[4]
    half = block_rows // 2
    count = half * SHIFTS * 2 * per_row
    hbm = pl.BlockSpec(memory_space=pltpu.HBM)
    index_shapes = [(REACH * 2, per_row + 1, block_rows), (4, 2, slots, 1, inner)]
    call = pl.pallas_call(
        functools.partial(gather_multiply, n_col),
        out_shape=jax.ShapeDtypeStruct((half * size, BC * size), jnp.bfloat16),
        in_specs=[hbm] * 6,
        out_specs=pl.BlockSpec(memory_space=pltpu.VMEM),
        scratch_shapes=[pltpu.VMEM((REACH * block_rows, per_row, size, size), jnp.bfloat16)]
        + [pltpu.VMEM((inner, size, size), jnp.bfloat16)] * 8
        + [pltpu.VMEM(shape, jnp.int32) for shape in index_shapes]
        + [pltpu.SMEM(shape, jnp.int32) for shape in index_shapes]
        + [
            pltpu.VMEM((count + 1, size, size), jnp.float32),
            pltpu.SMEM((count,), jnp.int32),
            pltpu.SMEM((count,), jnp.int32),
            pltpu.SMEM((half * BC,), jnp.int32),
            pltpu.SemaphoreType.DMA((5,)),
            pltpu.SemaphoreType.DMA((6,)),
            pltpu.SemaphoreType.DMA((3,)),
            pltpu.SemaphoreType.DMA(((SHIFTS - 1) * block_rows + half + half // 2,)),
            pltpu.SemaphoreType.DMA,
            pltpu.SemaphoreType.DMA((sum(map(len, PARTS)),)),
            pltpu.SemaphoreType.DMA((3,)),
            pltpu.SemaphoreType.DMA((per_row,)),
            pltpu.SemaphoreType.REGULAR((3,)),
            pltpu.SemaphoreType.DMA((3,)),
        ],
        compiler_params=pltpu.CompilerParams(
            collective_id=0, has_side_effects=True, vmem_limit_bytes=40 * 1024 * 1024
        ),
    )
    operands = [
        jnp.swapaxes(a_cols.reshape(block_rows, per_row), 0, 1),
        a_count.reshape(1, block_rows),
        b_cols.reshape(slots, 1, inner),
        b_count.reshape(slots, 1, inner),
        a_tiles.reshape(block_rows, per_row, size, size),
        b_tiles.reshape(slots, inner, size, size),
    ]
    return call(*(pltpu.with_memory_space_constraint(x, pltpu.HBM) for x in operands))


def solution(mesh):
    placed = (
        P("row", ("col", "depth"), None, None, None, None),
        P("row", ("col", "depth"), None, None),
        P("row", ("col", "depth"), None),
        P(None, "row", "depth", "col", None, None, None, None),
        P(None, "row", "depth", "col", None, None),
        P(None, "row", "depth", "col", None),
    )
    n_col = mesh.shape["col"]
    if mesh.shape["row"] == 2 and mesh.shape["depth"] == 2 and n_col == 2 * SHIFTS:
        body = functools.partial(local_fast, n_col)
    else:
        body = local
    return jax.shard_map(
        body, mesh=mesh, in_specs=placed, out_specs=P(("row", "depth"), "col"), check_vma=False
    )
```

```python
import functools
import math

import jax
import jax.numpy as jnp
from jax import lax
from jax.experimental import pallas as pl
from jax.experimental.pallas import tpu as pltpu
from jax.sharding import PartitionSpec as P

BC = 12
SHIFTS = 4


def for_sending(array):
    return jax.tree.map(lambda a: a.astype(jnp.bfloat16) if a.dtype == jnp.float32 else a, array)


def shifted(value, axis, steps):
    count = lax.axis_size(axis)
    pairs = [(source, (source + steps) % count) for source in range(count)]
    return lax.ppermute(value, axis, pairs)


def dense_panel(tiles_b, cols_b, count_b, width):
    slot_ids = lax.broadcasted_iota(jnp.int32, cols_b.shape, 1)
    valid_slot = slot_ids < count_b[:, None]
    targets = lax.broadcasted_iota(jnp.int32, (1, 1, width), 2)
    placing = jnp.logical_and(cols_b[:, :, None] == targets, valid_slot[:, :, None]).astype(
        jnp.bfloat16
    )
    spread = jnp.einsum("kuc,kuab->kacb", placing, tiles_b, preferred_element_type=jnp.float32)
    inner_blocks = tiles_b.shape[0]
    tile_size = tiles_b.shape[2]
    return spread.astype(jnp.bfloat16).reshape(inner_blocks, tile_size, width * tile_size)


def panel_product(tiles_a, cols_a, count_a, rows_dense):
    block_rows = tiles_a.shape[0]
    per_row = tiles_a.shape[1]
    tile_size = tiles_a.shape[2]
    slot_ids = lax.broadcasted_iota(jnp.int32, cols_a.shape, 1)
    valid_slot = slot_ids < count_a[:, None]
    masked = jnp.where(valid_slot[:, :, None, None], tiles_a, jnp.zeros_like(tiles_a))
    group_rows = math.gcd(block_rows, 4)

    def one_group(pieces):
        tiles_part, cols_part = pieces
        picks = lax.broadcasted_iota(jnp.int32, cols_part.shape + (rows_dense.shape[0],), 2)
        picks = (cols_part[:, :, None] == picks).astype(rows_dense.dtype)
        chosen = jnp.einsum("rtk,kbn->rtbn", picks, rows_dense, preferred_element_type=jnp.float32)
        chosen = chosen.astype(rows_dense.dtype)
        return jnp.einsum("rtab,rtbn->ran", tiles_part, chosen, preferred_element_type=jnp.float32)

    grouped = lax.map(
        one_group,
        (
            masked.reshape(block_rows // group_rows, group_rows, per_row, tile_size, tile_size),
            cols_a.reshape(block_rows // group_rows, group_rows, per_row),
        ),
    )
    return grouped.reshape(block_rows, tile_size, rows_dense.shape[2])


def roll_slots(stack, offset):
    slot_total = stack[0].shape[0]
    return tuple(
        (
            lax.dynamic_slice_in_dim(
                jnp.concatenate([member, member], 0), offset % slot_total, slot_total, 0
            )
            for member in stack
        )
    )


def select_if(flag, fresh, stale):
    return tuple((jnp.where(flag, new_part, old_part) for new_part, old_part in zip(fresh, stale)))


def local(a_tiles, a_cols, a_count, b_tiles, b_cols, b_count):
    rows_axis = lax.axis_size("row")
    cols_axis = lax.axis_size("col")
    row_group = lax.axis_index("row")
    col_group = lax.axis_index("col")
    tiles_a = a_tiles[0, 0]
    cols_a = a_cols[0, 0]
    count_a = a_count[0, 0]
    tiles_b = b_tiles[:, 0, 0, 0]
    cols_b = b_cols[:, 0, 0, 0]
    count_b = b_count[:, 0, 0, 0]
    for bit_pos in range((rows_axis - 1).bit_length()):
        stride = 1 << bit_pos
        moved = (
            shifted(tiles_a, "col", cols_axis - stride),
            shifted(for_sending(cols_a), "col", cols_axis - stride).astype(cols_a.dtype),
            shifted(for_sending(count_a), "col", cols_axis - stride).astype(count_a.dtype),
        )
        tiles_a, cols_a, count_a = select_if(
            row_group // stride % 2 == 1, moved, (tiles_a, cols_a, count_a)
        )
    for bit_pos in range((cols_axis - 1).bit_length()):
        stride = 1 << bit_pos
        nearby = stride % rows_axis
        if nearby:
            moved = (
                shifted(tiles_b, "row", rows_axis - nearby),
                shifted(for_sending(cols_b), "row", rows_axis - nearby).astype(cols_b.dtype),
                shifted(for_sending(count_b), "row", rows_axis - nearby).astype(count_b.dtype),
            )
        else:
            moved = (tiles_b, cols_b, count_b)
        moved = roll_slots(moved, (row_group + stride) // rows_axis)
        tiles_b, cols_b, count_b = select_if(
            col_group // stride % 2 == 1, moved, (tiles_b, cols_b, count_b)
        )
    tile_size = tiles_a.shape[2]
    running = jnp.zeros((tiles_a.shape[0], tile_size, BC * tile_size), jnp.float32)
    for turn_no in range(SHIFTS):
        current_tiles = tiles_b[0]
        current_cols = cols_b[0]
        current_count = count_b[0]
        rows_dense = dense_panel(current_tiles, current_cols, current_count, BC)
        running = running + panel_product(tiles_a, cols_a, count_a, rows_dense)
        if turn_no + 1 < SHIFTS:
            tiles_a, cols_a, count_a = (
                shifted(tiles_a, "col", cols_axis - 1),
                shifted(for_sending(cols_a), "col", cols_axis - 1).astype(cols_a.dtype),
                shifted(for_sending(count_a), "col", cols_axis - 1).astype(count_a.dtype),
            )
            moved = (
                shifted(tiles_b, "row", rows_axis - 1),
                shifted(for_sending(cols_b), "row", rows_axis - 1).astype(cols_b.dtype),
                shifted(for_sending(count_b), "row", rows_axis - 1).astype(count_b.dtype),
            )
            tiles_b, cols_b, count_b = roll_slots(moved, (row_group + 1) // rows_axis)
    flat_running = running.reshape(-1, running.shape[2])
    summed = lax.psum(flat_running, "depth")
    half_rows = flat_running.shape[0] // lax.axis_size("depth")
    own_rows = lax.dynamic_slice_in_dim(summed, lax.axis_index("depth") * half_rows, half_rows, 0)
    return own_rows.astype(jnp.bfloat16)


REACH = SHIFTS + 1
PARTS = ((16,), (7, 6, 3))
LATE = 1
SPLIT = 6
FIRST = 3
MESH_ID = pl.DeviceIdType.MESH


def gather_multiply(n_col, a_cols, a_count, b_cols, b_count, a_ref, b_ref, out_ref, A, Bn0, Bn1, Bf0, Bf1,
                    Gn0, Gn1, Gf0, Gf1, MA, MB, SA, SB, run, ktab, ptab, ltab,
                    send_m, recv_m, send_a, recv_1, recv_2, recv_3, recv_4, swapped, send_b, recv_b, passed, ready,
                    local_sem):
    row = lax.axis_index("row")
    col = lax.axis_index("col")
    dep = lax.axis_index("depth")
    side = lax.rem(col, 2)
    z = lax.div(col, 2)
    top = n_col // 2 - 1
    per_row, size = A.shape[1:3]
    units = A.shape[0] // REACH
    half = units // 2
    inner = Bn0.shape[0]
    out_cols = out_ref.shape[1] // size
    terms = SHIFTS * 2 * per_row
    zero_at = half * terms
    row0, row1, side0, side1 = row == 0, row == 1, side == 0, side == 1

    def both(*flags):
        return functools.reduce(jnp.logical_and, flags)

    def at(col_offset, flip_depth=False, flip_row=False):
        return (
            1 - row if flip_row else row,
            lax.rem(col + col_offset + n_col, n_col),
            1 - dep if flip_depth else dep,
        )

    twin_dev, row_dev = at(0, True), at(0, False, True)
    side_dev = (row, col + 1 - 2 * side, dep)
    down, up, down2, up2 = at(-2), at(2), at(-4), at(4)

    def remote(src, dst, ssem, rsem, dev):
        return pltpu.make_async_remote_copy(
            src_ref=src, dst_ref=dst, send_sem=ssem, recv_sem=rsem, device_id=dev, device_id_type=MESH_ID
        )

    def signal(sem, dev):
        pl.semaphore_signal(sem, inc=1, device_id=dev, device_id_type=MESH_ID)

    def drain(ref, sem):
        pltpu.make_async_copy(ref, ref, sem).wait()

    def start(copies, *flags):
        def go():
            for copy in copies:
                copy.start()

        if flags:
            pl.when(both(*flags))(go)
        else:
            go()

    s_near = [side + 2 * k for k in range(2)]
    s_far = [1 - side + 2 * k for k in range(2)]
    m_near = [lax.rem(row + col + s, n_col) // 2 for s in s_near]
    m_far = [lax.rem(1 - row + col + s, n_col) // 2 for s in s_far]
    m_mine = [lax.rem(row + col + s, n_col) // 2 for s in s_far]
    near_own, near_twin = (Bn0, Bn1), (Gn0, Gn1)
    far_own, far_twin = (Bf0, Bf1), (Gf0, Gf1)

    index_local = [
        pltpu.make_async_copy(src, dst, local_sem.at[n])
        for src, dst, n in (
            (a_cols, MA.at[0, pl.ds(0, per_row)], 0), (a_count, MA.at[0, pl.ds(per_row, 1)], 0),
            (b_cols, MB.at[0, 0], 1), (b_count, MB.at[0, 1], 1),
        )
    ]
    b_local = [pltpu.make_async_copy(b_ref.at[m_near[k]], near_own[k], local_sem.at[2]) for k in range(2)]
    a_local = pltpu.make_async_copy(a_ref.at[pl.ds(dep * half, half)], A.at[pl.ds(0, half)], local_sem.at[2])
    start(index_local + b_local + [a_local])

    @pl.when(row0)
    def _():
        for slot in range(2 * SHIFTS, 2 * REACH):
            MA[slot] = jnp.zeros(MA.shape[1:], MA.dtype)

    barrier = pltpu.get_barrier_semaphore()
    signal(barrier, twin_dev)
    pl.when(row0)(lambda: signal(barrier, row_dev))
    pl.when(side0)(lambda: signal(barrier, side_dev))
    pl.when(z < top)(lambda: signal(barrier, up))
    pl.when(z == 0)(lambda: signal(barrier, down))
    pl.when(both(row1, z == 1))(lambda: signal(barrier, down2))
    greeted = 1 + row + side + jnp.where(z > 0, 1, 0) + jnp.where(z == top, 1 + row, 0)
    pl.semaphore_wait(barrier, greeted)
    pl.when(row1)(lambda: signal(ready.at[0], row_dev))
    pl.when(side1)(lambda: signal(ready.at[1], side_dev))
    pl.when(z == top)(lambda: signal(ready.at[2], up))
    pl.when(both(row1, z == top))(lambda: signal(ready.at[2], up2))

    def unit(p, u):
        return A.at[p * units + u]

    own = [a_ref.at[dep * half + r] for r in range(half)] + [unit(0, half + r) for r in range(half)]

    def landed(p, u):
        return {1: recv_1, 2: recv_2, 3: recv_3, 4: recv_4}[p].at[{1: u // 2, 3: max(u - FIRST + 1, 0)}.get(p, u)]

    def to_panel(p, sources, dev, split=-1):
        copies = []
        for u, src in enumerate(sources):
            dst = unit(p, u)
            if u == split:
                for t in range(per_row):
                    sem = landed(p, units - 1 + t if p == SHIFTS and t else u)
                    copies.append(remote(src.at[t], dst.at[t], send_a, sem, dev))
            else:
                copies.append(remote(src, dst, send_a, landed(p, u), dev))
        return copies

    def panel(p):
        return [unit(p, u) for u in range(units)]

    swap = [
        remote(a_ref.at[(1 - dep) * half + r], unit(0, half + r), send_a, swapped, twin_dev)
        for r in range(half)
    ]
    chain = to_panel(2, own, down)
    chain2 = to_panel(4, panel(2), down, SPLIT)
    skip = to_panel(4, own, down2, SPLIT)
    own_x1 = to_panel(1, own, side_dev)
    fwd_x1 = to_panel(1, panel(2), side_dev)
    fwd_x3 = to_panel(3, panel(2), side_dev)
    top_x3 = to_panel(3, panel(4)[: units - LATE], side_dev, SPLIT)
    low_x3 = to_panel(3, panel(1), down)

    near_b = [remote(b_ref.at[m_near[k]], near_twin[k], send_b, passed.at[0], twin_dev) for k in range(2)]
    far_b, pass_b = [], []
    for k, sizes in enumerate(PARTS):
        for c, blocks in enumerate(sizes):
            part = pl.ds(sum(sizes[:c]) * inner // 16, blocks * inner // 16)
            far_b.append(
                remote(b_ref.at[m_far[k], part], far_own[k].at[part], send_b, recv_b.at[len(far_b)], row_dev)
            )
            pass_b.append(remote(far_own[k].at[part], far_twin[k].at[part], send_b, passed.at[k], twin_dev))

    def index_a(src, dst, dev):
        return remote(MA.at[pl.ds(src, 2)], MA.at[pl.ds(dst, 2)], send_m.at[0], recv_m.at[min(dst // 2, 3)], dev)

    swap_m = remote(MA.at[0], MA.at[1], send_m.at[0], recv_m.at[0], twin_dev)
    near_m = remote(MB.at[0], MB.at[1], send_m.at[1], recv_m.at[4], twin_dev)
    far_m = remote(MB.at[0], MB.at[2], send_m.at[1], recv_m.at[5], row_dev)
    pass_m = remote(MB.at[2], MB.at[3], send_m.at[1], recv_m.at[4], twin_dev)
    chain_m, chain2_m, skip_m = index_a(0, 4, down), index_a(4, 8, down), index_a(0, 8, down2)
    own_x1_m, fwd_x1_m = index_a(0, 2, side_dev), index_a(4, 2, side_dev)
    fwd_x3_m, low_x3_m = index_a(4, 6, side_dev), index_a(2, 6, down)

    drain(MA.at[0], local_sem.at[0])
    drain(MB.at[0], local_sem.at[1])
    start([swap_m] + swap)
    start(chain[:2], z > 0)
    start(own_x1[:2], side1)
    pl.when(row0)(lambda: pl.semaphore_wait(ready.at[0], 1))
    start([far_m] + far_b + [near_m] + near_b)
    swap_m.wait_recv()
    start([chain_m] + chain[2:half], z > 0)
    start([own_x1_m] + own_x1[2:half], side1)
    drain(A.at[pl.ds(0, half)], swapped)

    @pl.when(z == 0)
    def _():
        pl.semaphore_wait(ready.at[2], 1)
        start([chain_m] + chain[:half])

    @pl.when(both(row1, z == 1))
    def _():
        pl.semaphore_wait(ready.at[2], 1)
        start([skip_m] + skip)

    pl.when(side0)(lambda: pl.semaphore_wait(ready.at[1], 1))
    run[zero_at] = jnp.zeros(run.shape[1:], jnp.float32)

    def far_part(n):
        far_b[n].wait_recv()
        pass_b[n].start()

    def low(u):
        drain(A.at[pl.ds(0, 2)], landed(1, u))
        for w in (u, u + 1):
            start([low_x3[w]], side1, *([] if w >= units - LATE else [row0]))

    def recv(p, u):
        if p == 4 and u == SPLIT:
            for t in range(per_row):
                recv_half(t)
        elif p != 3 or u >= FIRST:
            drain(unit(p, u), landed(p, u))
        elif u == 0:
            drain(A.at[pl.ds(0, FIRST)], landed(p, u))

    def recv_half(t):
        drain(unit(SHIFTS, SPLIT).at[t], landed(SHIFTS, units - 1 + t if t else SPLIT))

    groups = [(s, m, k, d, far) for k in range(2) for far, s, m in ((0, s_near[k], m_near[k]), (1, s_far[k], m_mine[k]))
              for d in range(2)]

    def tables(r):
        cs = []
        for s, m, _, d, far in groups:
            slot = (s + row) * 2 + d
            used = SA[slot, per_row, dep * half + r]
            for t in range(per_row):
                k = SA[slot, t, dep * half + r]
                c = SB[2 * far + d, 0, m, 0, k]
                ok = jnp.logical_and(used > t, SB[2 * far + d, 1, m, 0, k] > 0)
                c = jnp.where(ok, c, -1)
                here = r * terms + len(cs)
                before = jnp.int32(zero_at)
                for at_p, c_p in enumerate(cs):
                    before = jnp.where(c_p == c, r * terms + at_p, before)
                ktab[here] = k
                ptab[here] = before
                cs.append(c)
        for c in range(out_cols):
            last = jnp.int32(zero_at)
            for at_p, c_p in enumerate(cs):
                last = jnp.where(c_p == c, r * terms + at_p, last)
            ltab[r * out_cols + c] = last

    rights = (Bn0, Gn0, Bf0, Gf0, Bn1, Gn1, Bf1, Gf1)

    def dots(g, r):
        s, _, _, d, _ = groups[g]
        values = []
        for t in range(per_row):
            here = r * terms + g * per_row + t
            left = A[(s + row) * units + d * half + r, t]
            values.append((here, jnp.dot(left, rights[g][ktab[here]], preferred_element_type=jnp.float32)))
        return values

    def add(values):
        for here, value in values:
            run[here] = value + run[ptab[here]]

    def products(wanted):
        held = []
        for g, r in wanted:
            fresh = dots(g, r)
            add(held)
            held = fresh
        add(held)

    def whole_group(g):
        products([(g, r) for r in range(half)])

    for u in range(units):
        recv(2, u)
        if u == 0:
            drain(MA.at[pl.ds(4, 2)], recv_m.at[2])
            start([chain2_m], row1, z > 0)
            start([fwd_x1_m], side0)
            start([fwd_x3_m], side1)
        start([fwd_x1[u]], side0)
        if u == 2:
            drain(MA.at[pl.ds(2, 2)], recv_m.at[1])
            start([low_x3_m], side1)
        if u < half:
            start([chain[half + u]])
            start([own_x1[half + u]], side1)
        else:
            start(chain2[2 * (u - half) : 2 * (u - half) + 2 + (u == units - 1)], row1, z > 0)
            start(fwd_x3[2 * (u - half) : 2 * (u - half) + 2], side1)
        if u == 0:
            far_m.wait_recv()
            pass_m.start()
        if u in (4, 6):
            low(u - 4)
        if u == units - 1:
            far_part(0)

    def arrive_near(*wanted):
        @pl.when(row != side)
        def _():
            for u in wanted:
                recv(3, u)

        @pl.when(both(row1, side1))
        def _():
            for u in wanted:
                recv(4, u)

    def near_units(*wanted):
        arrive_near(*wanted)
        products([(4 + u // half, u % half) for u in wanted])

    def arrive_far(*wanted):
        @pl.when(row == side)
        def _():
            for u in wanted:
                recv(3, u)

        if units - 1 in wanted:
            pl.when(both(row1, side0))(lambda: recv(4, units - 1))

    def far_units(*wanted):
        arrive_far(*wanted)
        products([(6 + u // half, u % half) for u in wanted])

    scalars = [pltpu.make_async_copy(MA.at[pl.ds(0, 2 * REACH)], SA, local_sem.at[0]), pltpu.make_async_copy(MB, SB, local_sem.at[1])]

    for u in range(units):
        if u < units - LATE:
            @pl.when(both(row1, side0))
            def _():
                if u == SPLIT:
                    for t in range(per_row):
                        recv_half(t)
                        top_x3[u + t].start()
                else:
                    recv(4, u)
                    top_x3[u].start()

        if u in (0, 2):
            low(half + u)
        if u == 0:
            pl.when(row0)(lambda: drain(MA.at[pl.ds(6, 2)], recv_m.at[3]))
            pl.when(row1)(lambda: drain(MA.at[pl.ds(6, 4)], recv_m.at[3]))
            drain(MB.at[pl.ds(0, 2)], recv_m.at[4])
            start(scalars)
        if u == 1:
            for copy in scalars:
                copy.wait()
            drain(A.at[pl.ds(0, 2 * units + half)], local_sem.at[2])
            drain(A.at[pl.ds(0, 3 * units)], passed.at[0])
        if u in (3, 5):
            far_part(u // 2)
        if u in (1, 2):
            for r in range((u - 1) * half // 2, u * half // 2):
                tables(r)
        if u == 2:
            whole_group(0)
        if u == 3:
            whole_group(1)
            whole_group(2)
        if u == 4:
            whole_group(3)
            near_units(0)
        if u == 5:
            near_units(1, 2)
    far_part(len(far_b) - 1)

    def place(r):
        for c in range(out_cols):
            out_ref[r * size : (r + 1) * size, c * size : (c + 1) * size] = run[ltab[r * out_cols + c]].astype(
                out_ref.dtype
            )

    def finish(*rows, near=False):
        wanted = [half + r for r in rows]
        if near:
            arrive_near(units - 1)
            wanted.append(half - 1)
        arrive_far(*wanted)
        steps = [(7, r) for r in rows]
        if near:
            steps[-1:] = [(5, half - 1), (6, half - 1), (7, half - 1)]
        held = None
        for g, r in steps + [(None, None)]:
            fresh = None if g is None else (g, r, dots(g, r))
            if held is not None:
                add(held[2])
                if held[0] == 7:
                    place(held[1])
            held = fresh

    def last_pass():
        drain(A.at[pl.ds(0, units)], passed.at[1])

    @pl.when(side0)
    def _():
        near_units(3, 4, 5, 6, 7)
        far_units(0, 1, 2, 3)
        last_pass()
        finish(0, 1, 2, 3)

    @pl.when(both(side1, z < top))
    def _():
        near_units(3, 4, 5, 6, 7)
        far_units(0, 1, 2, 3)
        last_pass()
        finish(0, 1)
        finish(2, 3)

    @pl.when(both(side1, z == top))
    def _():
        near_units(3, 4)
        far_units(0)
        near_units(5)
        far_units(1)
        last_pass()
        near_units(6)
        far_units(2)
        finish(0, 1)
        finish(2, 3, near=True)

    for r in range(2):
        for side_n, flag in enumerate((side0, side1)):
            for more, where in (((0, z >= 0),) if r == 0 else ((0, z == 0), (2, z == 1), (1, z > 1))):
                here = both(row == r, flag, where)
                across = (0, 2 * units) if r == 0 else (units - LATE, units + LATE)
                n = 2 * units + half + across[side_n] + more * units
                pl.when(here)(functools.partial(drain, run.at[pl.ds(0, n)], send_a))
                pl.when(here)(functools.partial(drain, MA.at[pl.ds(0, 5 + 4 * side_n + 2 * more)], send_m.at[0]))
    drain(run.at[pl.ds(0, 6 * units)], send_b)
    drain(MB.at[pl.ds(0, 3)], send_m.at[1])


def local_fast(n_col, a_tiles, a_cols, a_count, b_tiles, b_cols, b_count):
    block_rows, per_row, size = a_tiles.shape[2:5]
    slots, inner = b_tiles.shape[0], b_tiles.shape[4]
    half = block_rows // 2
    count = half * SHIFTS * 2 * per_row
    hbm = pl.BlockSpec(memory_space=pltpu.HBM)
    index_shapes = [(REACH * 2, per_row + 1, block_rows), (4, 2, slots, 1, inner)]
    index_vmem = [(REACH * 2 + 4, per_row + 1, block_rows), index_shapes[1]]
    call = pl.pallas_call(
        functools.partial(gather_multiply, n_col),
        out_shape=jax.ShapeDtypeStruct((half * size, BC * size), jnp.bfloat16),
        in_specs=[hbm] * 6,
        out_specs=pl.BlockSpec(memory_space=pltpu.VMEM),
        scratch_shapes=[pltpu.VMEM((REACH * block_rows, per_row, size, size), jnp.bfloat16)]
        + [pltpu.VMEM((inner, size, size), jnp.bfloat16)] * 8
        + [pltpu.VMEM(shape, jnp.int32) for shape in index_vmem]
        + [pltpu.SMEM(shape, jnp.int32) for shape in index_shapes]
        + [
            pltpu.VMEM((count + 1, size, size), jnp.float32),
            pltpu.SMEM((count,), jnp.int32),
            pltpu.SMEM((count,), jnp.int32),
            pltpu.SMEM((half * BC,), jnp.int32),
            pltpu.SemaphoreType.DMA((2,)),
            pltpu.SemaphoreType.DMA((6,)),
            pltpu.SemaphoreType.DMA,
            pltpu.SemaphoreType.DMA((half,)),
            pltpu.SemaphoreType.DMA((block_rows,)),
            pltpu.SemaphoreType.DMA((block_rows - FIRST + 1,)),
            pltpu.SemaphoreType.DMA((block_rows + 1,)),
            pltpu.SemaphoreType.DMA,
            pltpu.SemaphoreType.DMA,
            pltpu.SemaphoreType.DMA((sum(map(len, PARTS)),)),
            pltpu.SemaphoreType.DMA((2,)),
            pltpu.SemaphoreType.REGULAR((3,)),
            pltpu.SemaphoreType.DMA((3,)),
        ],
        compiler_params=pltpu.CompilerParams(
            collective_id=0, has_side_effects=True, vmem_limit_bytes=40 * 1024 * 1024
        ),
    )
    operands = [
        jnp.swapaxes(a_cols.reshape(block_rows, per_row), 0, 1),
        a_count.reshape(1, block_rows),
        b_cols.reshape(slots, 1, inner),
        b_count.reshape(slots, 1, inner),
        a_tiles.reshape(block_rows, per_row, size, size),
        b_tiles.reshape(slots, inner, size, size),
    ]
    return call(*(pltpu.with_memory_space_constraint(x, pltpu.HBM) for x in operands))


def solution(mesh):
    placed = (
        P("row", ("col", "depth"), None, None, None, None),
        P("row", ("col", "depth"), None, None),
        P("row", ("col", "depth"), None),
        P(None, "row", "depth", "col", None, None, None, None),
        P(None, "row", "depth", "col", None, None),
        P(None, "row", "depth", "col", None),
    )
    n_col = mesh.shape["col"]
    if mesh.shape["row"] == 2 and mesh.shape["depth"] == 2 and n_col == 2 * SHIFTS:
        body = functools.partial(local_fast, n_col)
    else:
        body = local
    return jax.shard_map(
        body, mesh=mesh, in_specs=placed, out_specs=P(("row", "depth"), "col"), check_vma=False
    )
```

```python
import functools
import math

import jax
import jax.numpy as jnp
from jax import lax
from jax.experimental import pallas as pl
from jax.experimental.pallas import tpu as pltpu
from jax.sharding import PartitionSpec as P

BC = 12
SHIFTS = 4


def for_sending(array):
    return jax.tree.map(lambda a: a.astype(jnp.bfloat16) if a.dtype == jnp.float32 else a, array)


def shifted(value, axis, steps):
    count = lax.axis_size(axis)
    pairs = [(source, (source + steps) % count) for source in range(count)]
    return lax.ppermute(value, axis, pairs)


def dense_panel(tiles_b, cols_b, count_b, width):
    slot_ids = lax.broadcasted_iota(jnp.int32, cols_b.shape, 1)
    valid_slot = slot_ids < count_b[:, None]
    targets = lax.broadcasted_iota(jnp.int32, (1, 1, width), 2)
    placing = jnp.logical_and(cols_b[:, :, None] == targets, valid_slot[:, :, None]).astype(
        jnp.bfloat16
    )
    spread = jnp.einsum("kuc,kuab->kacb", placing, tiles_b, preferred_element_type=jnp.float32)
    inner_blocks = tiles_b.shape[0]
    tile_size = tiles_b.shape[2]
    return spread.astype(jnp.bfloat16).reshape(inner_blocks, tile_size, width * tile_size)


def panel_product(tiles_a, cols_a, count_a, rows_dense):
    block_rows = tiles_a.shape[0]
    per_row = tiles_a.shape[1]
    tile_size = tiles_a.shape[2]
    slot_ids = lax.broadcasted_iota(jnp.int32, cols_a.shape, 1)
    valid_slot = slot_ids < count_a[:, None]
    masked = jnp.where(valid_slot[:, :, None, None], tiles_a, jnp.zeros_like(tiles_a))
    group_rows = math.gcd(block_rows, 4)

    def one_group(pieces):
        tiles_part, cols_part = pieces
        picks = lax.broadcasted_iota(jnp.int32, cols_part.shape + (rows_dense.shape[0],), 2)
        picks = (cols_part[:, :, None] == picks).astype(rows_dense.dtype)
        chosen = jnp.einsum("rtk,kbn->rtbn", picks, rows_dense, preferred_element_type=jnp.float32)
        chosen = chosen.astype(rows_dense.dtype)
        return jnp.einsum("rtab,rtbn->ran", tiles_part, chosen, preferred_element_type=jnp.float32)

    grouped = lax.map(
        one_group,
        (
            masked.reshape(block_rows // group_rows, group_rows, per_row, tile_size, tile_size),
            cols_a.reshape(block_rows // group_rows, group_rows, per_row),
        ),
    )
    return grouped.reshape(block_rows, tile_size, rows_dense.shape[2])


def roll_slots(stack, offset):
    slot_total = stack[0].shape[0]
    return tuple(
        (
            lax.dynamic_slice_in_dim(
                jnp.concatenate([member, member], 0), offset % slot_total, slot_total, 0
            )
            for member in stack
        )
    )


def select_if(flag, fresh, stale):
    return tuple((jnp.where(flag, new_part, old_part) for new_part, old_part in zip(fresh, stale)))


def local(a_tiles, a_cols, a_count, b_tiles, b_cols, b_count):
    rows_axis = lax.axis_size("row")
    cols_axis = lax.axis_size("col")
    row_group = lax.axis_index("row")
    col_group = lax.axis_index("col")
    tiles_a = a_tiles[0, 0]
    cols_a = a_cols[0, 0]
    count_a = a_count[0, 0]
    tiles_b = b_tiles[:, 0, 0, 0]
    cols_b = b_cols[:, 0, 0, 0]
    count_b = b_count[:, 0, 0, 0]
    for bit_pos in range((rows_axis - 1).bit_length()):
        stride = 1 << bit_pos
        moved = (
            shifted(tiles_a, "col", cols_axis - stride),
            shifted(for_sending(cols_a), "col", cols_axis - stride).astype(cols_a.dtype),
            shifted(for_sending(count_a), "col", cols_axis - stride).astype(count_a.dtype),
        )
        tiles_a, cols_a, count_a = select_if(
            row_group // stride % 2 == 1, moved, (tiles_a, cols_a, count_a)
        )
    for bit_pos in range((cols_axis - 1).bit_length()):
        stride = 1 << bit_pos
        nearby = stride % rows_axis
        if nearby:
            moved = (
                shifted(tiles_b, "row", rows_axis - nearby),
                shifted(for_sending(cols_b), "row", rows_axis - nearby).astype(cols_b.dtype),
                shifted(for_sending(count_b), "row", rows_axis - nearby).astype(count_b.dtype),
            )
        else:
            moved = (tiles_b, cols_b, count_b)
        moved = roll_slots(moved, (row_group + stride) // rows_axis)
        tiles_b, cols_b, count_b = select_if(
            col_group // stride % 2 == 1, moved, (tiles_b, cols_b, count_b)
        )
    tile_size = tiles_a.shape[2]
    running = jnp.zeros((tiles_a.shape[0], tile_size, BC * tile_size), jnp.float32)
    for turn_no in range(SHIFTS):
        current_tiles = tiles_b[0]
        current_cols = cols_b[0]
        current_count = count_b[0]
        rows_dense = dense_panel(current_tiles, current_cols, current_count, BC)
        running = running + panel_product(tiles_a, cols_a, count_a, rows_dense)
        if turn_no + 1 < SHIFTS:
            tiles_a, cols_a, count_a = (
                shifted(tiles_a, "col", cols_axis - 1),
                shifted(for_sending(cols_a), "col", cols_axis - 1).astype(cols_a.dtype),
                shifted(for_sending(count_a), "col", cols_axis - 1).astype(count_a.dtype),
            )
            moved = (
                shifted(tiles_b, "row", rows_axis - 1),
                shifted(for_sending(cols_b), "row", rows_axis - 1).astype(cols_b.dtype),
                shifted(for_sending(count_b), "row", rows_axis - 1).astype(count_b.dtype),
            )
            tiles_b, cols_b, count_b = roll_slots(moved, (row_group + 1) // rows_axis)
    flat_running = running.reshape(-1, running.shape[2])
    summed = lax.psum(flat_running, "depth")
    half_rows = flat_running.shape[0] // lax.axis_size("depth")
    own_rows = lax.dynamic_slice_in_dim(summed, lax.axis_index("depth") * half_rows, half_rows, 0)
    return own_rows.astype(jnp.bfloat16)


REACH = SHIFTS + 1
PARTS = ((16,), (7, 6, 3))
LATE = 1
SPLIT = 6
FIRST = 3
MESH_ID = pl.DeviceIdType.MESH


def gather_multiply(n_col, a_cols, a_count, b_cols, b_count, a_ref, b_ref, out_ref, A, Bn0, Bn1, Bf0, Bf1,
                    Gn0, Gn1, Gf0, Gf1, MA, MB, SA, SB, run, ktab, ptab, ltab,
                    send_m, recv_m, send_a, recv_1, recv_2, recv_3, recv_4, swapped, send_b, recv_b, passed, ready,
                    local_sem):
    row = lax.axis_index("row")
    col = lax.axis_index("col")
    dep = lax.axis_index("depth")
    side = lax.rem(col, 2)
    z = lax.div(col, 2)
    top = n_col // 2 - 1
    per_row, size = A.shape[1:3]
    units = A.shape[0] // REACH
    half = units // 2
    inner = Bn0.shape[0]
    out_cols = out_ref.shape[1] // size
    terms = SHIFTS * 2 * per_row
    zero_at = half * terms
    row0, row1, side0, side1 = row == 0, row == 1, side == 0, side == 1

    def both(*flags):
        return functools.reduce(jnp.logical_and, flags)

    def at(col_offset, flip_depth=False, flip_row=False):
        return (
            1 - row if flip_row else row,
            lax.rem(col + col_offset + n_col, n_col),
            1 - dep if flip_depth else dep,
        )

    twin_dev, row_dev = at(0, True), at(0, False, True)
    side_dev = (row, col + 1 - 2 * side, dep)
    down, up, down2, up2 = at(-2), at(2), at(-4), at(4)

    def remote(src, dst, ssem, rsem, dev):
        return pltpu.make_async_remote_copy(
            src_ref=src, dst_ref=dst, send_sem=ssem, recv_sem=rsem, device_id=dev, device_id_type=MESH_ID
        )

    def signal(sem, dev):
        pl.semaphore_signal(sem, inc=1, device_id=dev, device_id_type=MESH_ID)

    def drain(ref, sem):
        pltpu.make_async_copy(ref, ref, sem).wait()

    def start(copies, *flags):
        def go():
            for copy in copies:
                copy.start()

        if flags:
            pl.when(both(*flags))(go)
        else:
            go()

    s_near = [side + 2 * k for k in range(2)]
    s_far = [1 - side + 2 * k for k in range(2)]
    m_near = [lax.rem(row + col + s, n_col) // 2 for s in s_near]
    m_far = [lax.rem(1 - row + col + s, n_col) // 2 for s in s_far]
    m_mine = [lax.rem(row + col + s, n_col) // 2 for s in s_far]
    near_own, near_twin = (Bn0, Bn1), (Gn0, Gn1)
    far_own, far_twin = (Bf0, Bf1), (Gf0, Gf1)

    index_local = [
        pltpu.make_async_copy(src, dst, local_sem.at[n])
        for src, dst, n in (
            (a_cols, MA.at[0, pl.ds(0, per_row)], 0), (a_count, MA.at[0, pl.ds(per_row, 1)], 0),
            (b_cols, MB.at[0, 0], 1), (b_count, MB.at[0, 1], 1),
        )
    ]
    b_local = [pltpu.make_async_copy(b_ref.at[m_near[k]], near_own[k], local_sem.at[2]) for k in range(2)]
    a_local = pltpu.make_async_copy(a_ref.at[pl.ds(dep * half, half)], A.at[pl.ds(0, half)], local_sem.at[2])
    start(index_local + b_local + [a_local])

    @pl.when(row0)
    def _():
        for slot in range(2 * SHIFTS, 2 * REACH):
            MA[slot] = jnp.zeros(MA.shape[1:], MA.dtype)

    barrier = pltpu.get_barrier_semaphore()
    signal(barrier, twin_dev)
    pl.when(row0)(lambda: signal(barrier, row_dev))
    pl.when(side0)(lambda: signal(barrier, side_dev))
    pl.when(z < top)(lambda: signal(barrier, up))
    pl.when(z == 0)(lambda: signal(barrier, down))
    pl.when(both(row1, z == 1))(lambda: signal(barrier, down2))
    greeted = 1 + row + side + jnp.where(z > 0, 1, 0) + jnp.where(z == top, 1 + row, 0)
    pl.semaphore_wait(barrier, greeted)
    pl.when(z == top)(lambda: signal(ready.at[2], up))
    pl.when(both(row1, z == top))(lambda: signal(ready.at[2], up2))
    pl.when(row1)(lambda: signal(ready.at[0], row_dev))
    pl.when(side1)(lambda: signal(ready.at[1], side_dev))

    def unit(p, u):
        return A.at[p * units + u]

    own = [a_ref.at[dep * half + r] for r in range(half)] + [unit(0, half + r) for r in range(half)]

    def landed(p, u):
        return {1: recv_1, 2: recv_2, 3: recv_3, 4: recv_4}[p].at[{1: u // 2, 3: max(u - FIRST + 1, 0)}.get(p, u)]

    def to_panel(p, sources, dev, split=-1):
        copies = []
        for u, src in enumerate(sources):
            dst = unit(p, u)
            if u == split:
                for t in range(per_row):
                    sem = landed(p, units - 1 + t if p == SHIFTS and t else u)
                    copies.append(remote(src.at[t], dst.at[t], send_a, sem, dev))
            else:
                copies.append(remote(src, dst, send_a, landed(p, u), dev))
        return copies

    def panel(p):
        return [unit(p, u) for u in range(units)]

    swap = [
        remote(a_ref.at[(1 - dep) * half + r], unit(0, half + r), send_a, swapped, twin_dev)
        for r in range(half)
    ]
    chain = to_panel(2, own, down)
    chain2 = to_panel(4, panel(2), down, SPLIT)
    skip = to_panel(4, panel(0), down2, SPLIT)
    wrap = to_panel(2, panel(0)[:half], down)
    own_x1 = to_panel(1, own, side_dev)
    fwd_x1 = to_panel(1, panel(2), side_dev)
    fwd_x3 = to_panel(3, panel(2), side_dev)
    top_x3 = to_panel(3, panel(4)[: units - LATE], side_dev, SPLIT)
    low_x3 = to_panel(3, panel(1), down)

    near_b = [remote(b_ref.at[m_near[k]], near_twin[k], send_b, passed.at[0], twin_dev) for k in range(2)]
    far_b, pass_b = [], []
    for k, sizes in enumerate(PARTS):
        for c, blocks in enumerate(sizes):
            part = pl.ds(sum(sizes[:c]) * inner // 16, blocks * inner // 16)
            far_b.append(
                remote(b_ref.at[m_far[k], part], far_own[k].at[part], send_b, recv_b.at[len(far_b)], row_dev)
            )
            pass_b.append(remote(far_own[k].at[part], far_twin[k].at[part], send_b, passed.at[k], twin_dev))

    def index_a(src, dst, dev):
        return remote(MA.at[pl.ds(src, 2)], MA.at[pl.ds(dst, 2)], send_m.at[0], recv_m.at[min(dst // 2, 3)], dev)

    swap_m = remote(MA.at[0], MA.at[1], send_m.at[0], recv_m.at[0], twin_dev)
    near_m = remote(MB.at[0], MB.at[1], send_m.at[1], recv_m.at[4], twin_dev)
    far_m = remote(MB.at[0], MB.at[2], send_m.at[1], recv_m.at[5], row_dev)
    pass_m = remote(MB.at[2], MB.at[3], send_m.at[1], recv_m.at[4], twin_dev)
    chain_m, chain2_m, skip_m = index_a(0, 4, down), index_a(4, 8, down), index_a(0, 8, down2)
    own_x1_m, fwd_x1_m = index_a(0, 2, side_dev), index_a(4, 2, side_dev)
    fwd_x3_m, low_x3_m = index_a(4, 6, side_dev), index_a(2, 6, down)

    drain(MA.at[0], local_sem.at[0])
    drain(MB.at[0], local_sem.at[1])
    start([swap_m] + swap)
    start(chain[:2], z > 0)
    start(own_x1[:2], side1)
    pl.when(row0)(lambda: pl.semaphore_wait(ready.at[0], 1))
    start([far_m] + far_b + [near_m] + near_b)
    swap_m.wait_recv()
    start([chain_m] + chain[2:half], z > 0)
    start([own_x1_m] + own_x1[2:half], side1)
    drain(A.at[pl.ds(0, half)], swapped)

    def local_data():
        drain(A.at[pl.ds(0, 2 * units + half)], local_sem.at[2])

    @pl.when(z == 0)
    def _():
        local_data()
        pl.semaphore_wait(ready.at[2], 1)
        start([chain_m] + wrap)

    @pl.when(both(row1, z == 1))
    def _():
        local_data()
        pl.semaphore_wait(ready.at[2], 1)
        start([skip_m] + skip)

    pl.when(side0)(lambda: pl.semaphore_wait(ready.at[1], 1))
    run[zero_at] = jnp.zeros(run.shape[1:], jnp.float32)

    def far_part(n):
        far_b[n].wait_recv()
        pass_b[n].start()

    def low(u):
        drain(A.at[pl.ds(0, 2)], landed(1, u))
        for w in (u, u + 1):
            start([low_x3[w]], side1, *([] if w >= units - LATE else [row0]))

    def recv(p, u):
        if p == 4 and u == SPLIT:
            for t in range(per_row):
                recv_half(t)
        elif p != 3 or u >= FIRST:
            drain(unit(p, u), landed(p, u))
        elif u == 0:
            drain(A.at[pl.ds(0, FIRST)], landed(p, u))

    def recv_half(t):
        drain(unit(SHIFTS, SPLIT).at[t], landed(SHIFTS, units - 1 + t if t else SPLIT))

    groups = [(s, m, k, d, far) for k in range(2) for far, s, m in ((0, s_near[k], m_near[k]), (1, s_far[k], m_mine[k]))
              for d in range(2)]

    def tables(r):
        cs = []
        for s, m, _, d, far in groups:
            slot = (s + row) * 2 + d
            used = SA[slot, per_row, dep * half + r]
            for t in range(per_row):
                k = SA[slot, t, dep * half + r]
                c = SB[2 * far + d, 0, m, 0, k]
                ok = jnp.logical_and(used > t, SB[2 * far + d, 1, m, 0, k] > 0)
                c = jnp.where(ok, c, -1)
                here = r * terms + len(cs)
                before = jnp.int32(zero_at)
                for at_p, c_p in enumerate(cs):
                    before = jnp.where(c_p == c, r * terms + at_p, before)
                ktab[here] = k
                ptab[here] = before
                cs.append(c)
        for c in range(out_cols):
            last = jnp.int32(zero_at)
            for at_p, c_p in enumerate(cs):
                last = jnp.where(c_p == c, r * terms + at_p, last)
            ltab[r * out_cols + c] = last

    rights = (Bn0, Gn0, Bf0, Gf0, Bn1, Gn1, Bf1, Gf1)

    def dots(g, r):
        s, _, _, d, _ = groups[g]
        values = []
        for t in range(per_row):
            here = r * terms + g * per_row + t
            left = A[(s + row) * units + d * half + r, t]
            values.append((here, jnp.dot(left, rights[g][ktab[here]], preferred_element_type=jnp.float32)))
        return values

    def add(values):
        for here, value in values:
            run[here] = value + run[ptab[here]]

    def products(wanted):
        held = []
        for g, r in wanted:
            fresh = dots(g, r)
            add(held)
            held = fresh
        add(held)

    def whole_group(g):
        products([(g, r) for r in range(half)])

    for u in range(units):
        recv(2, u)
        if u == 0:
            drain(MA.at[pl.ds(4, 2)], recv_m.at[2])
            start([chain2_m], row1, z > 0)
            start([fwd_x1_m], side0)
            start([fwd_x3_m], side1)
        start([fwd_x1[u]], side0)
        if u == 2:
            drain(MA.at[pl.ds(2, 2)], recv_m.at[1])
            start([low_x3_m], side1)
        if u < half:
            start([chain[half + u]])
            start([own_x1[half + u]], side1)
        else:
            start(chain2[2 * (u - half) : 2 * (u - half) + 2 + (u == units - 1)], row1, z > 0)
            start(fwd_x3[2 * (u - half) : 2 * (u - half) + 2], side1)
        if u == 0:
            far_m.wait_recv()
            pass_m.start()
        if u in (4, 6):
            low(u - 4)
        if u == units - 1:
            far_part(0)

    def arrive_near(*wanted):
        @pl.when(row != side)
        def _():
            for u in wanted:
                recv(3, u)

        @pl.when(both(row1, side1))
        def _():
            for u in wanted:
                recv(4, u)

    def near_units(*wanted):
        arrive_near(*wanted)
        products([(4 + u // half, u % half) for u in wanted])

    def arrive_far(*wanted):
        @pl.when(row == side)
        def _():
            for u in wanted:
                recv(3, u)

        if units - 1 in wanted:
            pl.when(both(row1, side0))(lambda: recv(4, units - 1))

    def far_units(*wanted):
        arrive_far(*wanted)
        products([(6 + u // half, u % half) for u in wanted])

    scalars = [pltpu.make_async_copy(MA.at[pl.ds(0, 2 * REACH)], SA, local_sem.at[0]), pltpu.make_async_copy(MB, SB, local_sem.at[1])]

    for u in range(units):
        if u < units - LATE:
            @pl.when(both(row1, side0))
            def _():
                if u == SPLIT:
                    for t in range(per_row):
                        recv_half(t)
                        top_x3[u + t].start()
                else:
                    recv(4, u)
                    top_x3[u].start()

        if u in (0, 2):
            low(half + u)
        if u == 0:
            pl.when(row0)(lambda: drain(MA.at[pl.ds(6, 2)], recv_m.at[3]))
            pl.when(row1)(lambda: drain(MA.at[pl.ds(6, 4)], recv_m.at[3]))
            drain(MB.at[pl.ds(0, 2)], recv_m.at[4])
            start(scalars)
        if u == 1:
            for copy in scalars:
                copy.wait()
            pl.when(z > row)(local_data)
            drain(A.at[pl.ds(0, 3 * units)], passed.at[0])
        if u in (3, 5):
            far_part(u // 2)
        if u in (1, 2):
            for r in range((u - 1) * half // 2, u * half // 2):
                tables(r)
        if u == 2:
            whole_group(0)
        if u == 3:
            whole_group(1)
            whole_group(2)
        if u == 4:
            whole_group(3)
            near_units(0)
        if u == 5:
            near_units(1, 2)
    far_part(len(far_b) - 1)

    def place(r):
        for c in range(out_cols):
            out_ref[r * size : (r + 1) * size, c * size : (c + 1) * size] = run[ltab[r * out_cols + c]].astype(
                out_ref.dtype
            )

    def finish(*rows, near=False):
        wanted = [half + r for r in rows]
        if near:
            arrive_near(units - 1)
            wanted.append(half - 1)
        arrive_far(*wanted)
        steps = [(7, r) for r in rows]
        if near:
            steps[-1:] = [(5, half - 1), (6, half - 1), (7, half - 1)]
        held = None
        for g, r in steps + [(None, None)]:
            fresh = None if g is None else (g, r, dots(g, r))
            if held is not None:
                add(held[2])
                if held[0] == 7:
                    place(held[1])
            held = fresh

    def last_pass():
        drain(A.at[pl.ds(0, units)], passed.at[1])

    @pl.when(side0)
    def _():
        near_units(3, 4, 5, 6, 7)
        far_units(0, 1, 2, 3)
        last_pass()
        finish(0, 1, 2, 3)

    @pl.when(both(side1, z < top))
    def _():
        near_units(3, 4, 5, 6, 7)
        far_units(0, 1, 2, 3)
        last_pass()
        finish(0, 1)
        finish(3)
        finish(2)

    @pl.when(both(side1, z == top))
    def _():
        near_units(3, 4)
        far_units(0)
        near_units(5)
        far_units(1)
        last_pass()
        near_units(6)
        far_units(2)
        finish(0, 1)
        finish(3, near=True)
        finish(2)

    for r in range(2):
        for side_n, flag in enumerate((side0, side1)):
            for more, where in (((0, z >= 0),) if r == 0 else ((0, z == 0), (2, z == 1), (1, z > 1))):
                here = both(row == r, flag, where)
                across = (0, 2 * units) if r == 0 else (units - LATE, units + LATE)
                n = 2 * units + half + across[side_n] + more * units
                pl.when(here)(functools.partial(drain, run.at[pl.ds(0, n)], send_a))
                pl.when(here)(functools.partial(drain, MA.at[pl.ds(0, 5 + 4 * side_n + 2 * more)], send_m.at[0]))
    drain(run.at[pl.ds(0, 6 * units)], send_b)
    drain(MB.at[pl.ds(0, 3)], send_m.at[1])


def local_fast(n_col, a_tiles, a_cols, a_count, b_tiles, b_cols, b_count):
    block_rows, per_row, size = a_tiles.shape[2:5]
    slots, inner = b_tiles.shape[0], b_tiles.shape[4]
    half = block_rows // 2
    count = half * SHIFTS * 2 * per_row
    hbm = pl.BlockSpec(memory_space=pltpu.HBM)
    index_shapes = [(REACH * 2, per_row + 1, block_rows), (4, 2, slots, 1, inner)]
    index_vmem = [(REACH * 2 + 4, per_row + 1, block_rows), index_shapes[1]]
    call = pl.pallas_call(
        functools.partial(gather_multiply, n_col),
        out_shape=jax.ShapeDtypeStruct((half * size, BC * size), jnp.bfloat16),
        in_specs=[hbm] * 6,
        out_specs=pl.BlockSpec(memory_space=pltpu.VMEM),
        scratch_shapes=[pltpu.VMEM((REACH * block_rows, per_row, size, size), jnp.bfloat16)]
        + [pltpu.VMEM((inner, size, size), jnp.bfloat16)] * 8
        + [pltpu.VMEM(shape, jnp.int32) for shape in index_vmem]
        + [pltpu.SMEM(shape, jnp.int32) for shape in index_shapes]
        + [
            pltpu.VMEM((count + 1, size, size), jnp.float32),
            pltpu.SMEM((count,), jnp.int32),
            pltpu.SMEM((count,), jnp.int32),
            pltpu.SMEM((half * BC,), jnp.int32),
            pltpu.SemaphoreType.DMA((2,)),
            pltpu.SemaphoreType.DMA((6,)),
            pltpu.SemaphoreType.DMA,
            pltpu.SemaphoreType.DMA((half,)),
            pltpu.SemaphoreType.DMA((block_rows,)),
            pltpu.SemaphoreType.DMA((block_rows - FIRST + 1,)),
            pltpu.SemaphoreType.DMA((block_rows + 1,)),
            pltpu.SemaphoreType.DMA,
            pltpu.SemaphoreType.DMA,
            pltpu.SemaphoreType.DMA((sum(map(len, PARTS)),)),
            pltpu.SemaphoreType.DMA((2,)),
            pltpu.SemaphoreType.REGULAR((3,)),
            pltpu.SemaphoreType.DMA((3,)),
        ],
        compiler_params=pltpu.CompilerParams(
            collective_id=0, has_side_effects=True, vmem_limit_bytes=40 * 1024 * 1024
        ),
    )
    operands = [
        jnp.swapaxes(a_cols.reshape(block_rows, per_row), 0, 1),
        a_count.reshape(1, block_rows),
        b_cols.reshape(slots, 1, inner),
        b_count.reshape(slots, 1, inner),
        a_tiles.reshape(block_rows, per_row, size, size),
        b_tiles.reshape(slots, inner, size, size),
    ]
    return call(*(pltpu.with_memory_space_constraint(x, pltpu.HBM) for x in operands))


def solution(mesh):
    placed = (
        P("row", ("col", "depth"), None, None, None, None),
        P("row", ("col", "depth"), None, None),
        P("row", ("col", "depth"), None),
        P(None, "row", "depth", "col", None, None, None, None),
        P(None, "row", "depth", "col", None, None),
        P(None, "row", "depth", "col", None),
    )
    n_col = mesh.shape["col"]
    if mesh.shape["row"] == 2 and mesh.shape["depth"] == 2 and n_col == 2 * SHIFTS:
        body = functools.partial(local_fast, n_col)
    else:
        body = local
    return jax.shard_map(
        body, mesh=mesh, in_specs=placed, out_specs=P(("row", "depth"), "col"), check_vma=False
    )
```

```python
import functools
import math

import jax
import jax.numpy as jnp
from jax import lax
from jax.experimental import pallas as pl
from jax.experimental.pallas import tpu as pltpu
from jax.sharding import PartitionSpec as P

BC = 12
SHIFTS = 4


def for_sending(array):
    return jax.tree.map(lambda a: a.astype(jnp.bfloat16) if a.dtype == jnp.float32 else a, array)


def shifted(value, axis, steps):
    count = lax.axis_size(axis)
    pairs = [(source, (source + steps) % count) for source in range(count)]
    return lax.ppermute(value, axis, pairs)


def dense_panel(tiles_b, cols_b, count_b, width):
    slot_ids = lax.broadcasted_iota(jnp.int32, cols_b.shape, 1)
    valid_slot = slot_ids < count_b[:, None]
    targets = lax.broadcasted_iota(jnp.int32, (1, 1, width), 2)
    placing = jnp.logical_and(cols_b[:, :, None] == targets, valid_slot[:, :, None]).astype(
        jnp.bfloat16
    )
    spread = jnp.einsum("kuc,kuab->kacb", placing, tiles_b, preferred_element_type=jnp.float32)
    inner_blocks = tiles_b.shape[0]
    tile_size = tiles_b.shape[2]
    return spread.astype(jnp.bfloat16).reshape(inner_blocks, tile_size, width * tile_size)


def panel_product(tiles_a, cols_a, count_a, rows_dense):
    block_rows = tiles_a.shape[0]
    per_row = tiles_a.shape[1]
    tile_size = tiles_a.shape[2]
    slot_ids = lax.broadcasted_iota(jnp.int32, cols_a.shape, 1)
    valid_slot = slot_ids < count_a[:, None]
    masked = jnp.where(valid_slot[:, :, None, None], tiles_a, jnp.zeros_like(tiles_a))
    group_rows = math.gcd(block_rows, 4)

    def one_group(pieces):
        tiles_part, cols_part = pieces
        picks = lax.broadcasted_iota(jnp.int32, cols_part.shape + (rows_dense.shape[0],), 2)
        picks = (cols_part[:, :, None] == picks).astype(rows_dense.dtype)
        chosen = jnp.einsum("rtk,kbn->rtbn", picks, rows_dense, preferred_element_type=jnp.float32)
        chosen = chosen.astype(rows_dense.dtype)
        return jnp.einsum("rtab,rtbn->ran", tiles_part, chosen, preferred_element_type=jnp.float32)

    grouped = lax.map(
        one_group,
        (
            masked.reshape(block_rows // group_rows, group_rows, per_row, tile_size, tile_size),
            cols_a.reshape(block_rows // group_rows, group_rows, per_row),
        ),
    )
    return grouped.reshape(block_rows, tile_size, rows_dense.shape[2])


def roll_slots(stack, offset):
    slot_total = stack[0].shape[0]
    return tuple(
        (
            lax.dynamic_slice_in_dim(
                jnp.concatenate([member, member], 0), offset % slot_total, slot_total, 0
            )
            for member in stack
        )
    )


def select_if(flag, fresh, stale):
    return tuple((jnp.where(flag, new_part, old_part) for new_part, old_part in zip(fresh, stale)))


def local(a_tiles, a_cols, a_count, b_tiles, b_cols, b_count):
    rows_axis = lax.axis_size("row")
    cols_axis = lax.axis_size("col")
    row_group = lax.axis_index("row")
    col_group = lax.axis_index("col")
    tiles_a = a_tiles[0, 0]
    cols_a = a_cols[0, 0]
    count_a = a_count[0, 0]
    tiles_b = b_tiles[:, 0, 0, 0]
    cols_b = b_cols[:, 0, 0, 0]
    count_b = b_count[:, 0, 0, 0]
    for bit_pos in range((rows_axis - 1).bit_length()):
        stride = 1 << bit_pos
        moved = (
            shifted(tiles_a, "col", cols_axis - stride),
            shifted(for_sending(cols_a), "col", cols_axis - stride).astype(cols_a.dtype),
            shifted(for_sending(count_a), "col", cols_axis - stride).astype(count_a.dtype),
        )
        tiles_a, cols_a, count_a = select_if(
            row_group // stride % 2 == 1, moved, (tiles_a, cols_a, count_a)
        )
    for bit_pos in range((cols_axis - 1).bit_length()):
        stride = 1 << bit_pos
        nearby = stride % rows_axis
        if nearby:
            moved = (
                shifted(tiles_b, "row", rows_axis - nearby),
                shifted(for_sending(cols_b), "row", rows_axis - nearby).astype(cols_b.dtype),
                shifted(for_sending(count_b), "row", rows_axis - nearby).astype(count_b.dtype),
            )
        else:
            moved = (tiles_b, cols_b, count_b)
        moved = roll_slots(moved, (row_group + stride) // rows_axis)
        tiles_b, cols_b, count_b = select_if(
            col_group // stride % 2 == 1, moved, (tiles_b, cols_b, count_b)
        )
    tile_size = tiles_a.shape[2]
    running = jnp.zeros((tiles_a.shape[0], tile_size, BC * tile_size), jnp.float32)
    for turn_no in range(SHIFTS):
        current_tiles = tiles_b[0]
        current_cols = cols_b[0]
        current_count = count_b[0]
        rows_dense = dense_panel(current_tiles, current_cols, current_count, BC)
        running = running + panel_product(tiles_a, cols_a, count_a, rows_dense)
        if turn_no + 1 < SHIFTS:
            tiles_a, cols_a, count_a = (
                shifted(tiles_a, "col", cols_axis - 1),
                shifted(for_sending(cols_a), "col", cols_axis - 1).astype(cols_a.dtype),
                shifted(for_sending(count_a), "col", cols_axis - 1).astype(count_a.dtype),
            )
            moved = (
                shifted(tiles_b, "row", rows_axis - 1),
                shifted(for_sending(cols_b), "row", rows_axis - 1).astype(cols_b.dtype),
                shifted(for_sending(count_b), "row", rows_axis - 1).astype(count_b.dtype),
            )
            tiles_b, cols_b, count_b = roll_slots(moved, (row_group + 1) // rows_axis)
    flat_running = running.reshape(-1, running.shape[2])
    summed = lax.psum(flat_running, "depth")
    half_rows = flat_running.shape[0] // lax.axis_size("depth")
    own_rows = lax.dynamic_slice_in_dim(summed, lax.axis_index("depth") * half_rows, half_rows, 0)
    return own_rows.astype(jnp.bfloat16)


REACH = SHIFTS + 1
PARTS = ((16,), (7, 6, 3))
LATE = 1
SPLIT = 6
PIECES = ((0, 0, 2), (1, 0, 1), (1, 1, 1))
FIRST = 3
MESH_ID = pl.DeviceIdType.MESH


def gather_multiply(n_col, a_cols, a_count, b_cols, b_count, a_ref, b_ref, out_ref, A, Bn0, Bn1, Bf0, Bf1,
                    Gn0, Gn1, Gf0, Gf1, MA, MB, SA, SB, run, ktab, ptab, ltab,
                    send_m, recv_m, send_a, recv_1, recv_2, recv_3, recv_4, swapped, send_b, recv_b, passed, ready,
                    local_sem):
    row = lax.axis_index("row")
    col = lax.axis_index("col")
    dep = lax.axis_index("depth")
    side = lax.rem(col, 2)
    z = lax.div(col, 2)
    top = n_col // 2 - 1
    per_row, size = A.shape[1:3]
    units = A.shape[0] // REACH
    half = units // 2
    inner = Bn0.shape[0]
    out_cols = out_ref.shape[1] // size
    terms = SHIFTS * 2 * per_row
    zero_at = half * terms
    row0, row1, side0, side1 = row == 0, row == 1, side == 0, side == 1

    def both(*flags):
        return functools.reduce(jnp.logical_and, flags)

    def at(col_offset, flip_depth=False, flip_row=False):
        return (
            1 - row if flip_row else row,
            lax.rem(col + col_offset + n_col, n_col),
            1 - dep if flip_depth else dep,
        )

    twin_dev, row_dev = at(0, True), at(0, False, True)
    side_dev = (row, col + 1 - 2 * side, dep)
    down, up, down2, up2 = at(-2), at(2), at(-4), at(4)

    def remote(src, dst, ssem, rsem, dev):
        return pltpu.make_async_remote_copy(
            src_ref=src, dst_ref=dst, send_sem=ssem, recv_sem=rsem, device_id=dev, device_id_type=MESH_ID
        )

    def signal(sem, dev):
        pl.semaphore_signal(sem, inc=1, device_id=dev, device_id_type=MESH_ID)

    def drain(ref, sem):
        pltpu.make_async_copy(ref, ref, sem).wait()

    def start(copies, *flags):
        def go():
            for copy in copies:
                copy.start()

        if flags:
            pl.when(both(*flags))(go)
        else:
            go()

    s_near = [side + 2 * k for k in range(2)]
    s_far = [1 - side + 2 * k for k in range(2)]
    m_near = [lax.rem(row + col + s, n_col) // 2 for s in s_near]
    m_far = [lax.rem(1 - row + col + s, n_col) // 2 for s in s_far]
    m_mine = [lax.rem(row + col + s, n_col) // 2 for s in s_far]
    near_own, near_twin = (Bn0, Bn1), (Gn0, Gn1)
    far_own, far_twin = (Bf0, Bf1), (Gf0, Gf1)

    index_local = [
        pltpu.make_async_copy(src, dst, local_sem.at[n])
        for src, dst, n in (
            (a_cols, MA.at[0, pl.ds(0, per_row)], 0), (a_count, MA.at[0, pl.ds(per_row, 1)], 0),
            (b_cols, MB.at[0, 0], 1), (b_count, MB.at[0, 1], 1),
        )
    ]
    b_local = [pltpu.make_async_copy(b_ref.at[m_near[k]], near_own[k], local_sem.at[2]) for k in range(2)]
    a_local = pltpu.make_async_copy(a_ref.at[pl.ds(dep * half, half)], A.at[pl.ds(0, half)], local_sem.at[2])
    start(index_local + b_local + [a_local])

    @pl.when(row0)
    def _():
        for slot in range(2 * SHIFTS, 2 * REACH):
            MA[slot] = jnp.zeros(MA.shape[1:], MA.dtype)

    barrier = pltpu.get_barrier_semaphore()
    signal(barrier, twin_dev)
    pl.when(row0)(lambda: signal(barrier, row_dev))
    pl.when(side0)(lambda: signal(barrier, side_dev))
    pl.when(z < top)(lambda: signal(barrier, up))
    pl.when(z == 0)(lambda: signal(barrier, down))
    pl.when(both(row1, z == 1))(lambda: signal(barrier, down2))
    greeted = 1 + row + side + jnp.where(z > 0, 1, 0) + jnp.where(z == top, 1 + row, 0)
    pl.semaphore_wait(barrier, greeted)
    pl.when(z == top)(lambda: signal(ready.at[2], up))
    pl.when(both(row1, z == top))(lambda: signal(ready.at[2], up2))
    pl.when(row1)(lambda: signal(ready.at[0], row_dev))
    pl.when(side1)(lambda: signal(ready.at[1], side_dev))

    def unit(p, u):
        return A.at[p * units + u]

    own = [a_ref.at[dep * half + r] for r in range(half)] + [unit(0, half + r) for r in range(half)]

    def landed(p, u):
        return {1: recv_1, 2: recv_2, 3: recv_3, 4: recv_4}[p].at[{1: u // 2, 3: max(u - FIRST + 1, 0)}.get(p, u)]

    def piece(ref, n):
        t, begin, length = PIECES[n]
        return ref.at[t, pl.ds(begin * size // 2, length * size // 2)]

    def to_panel(p, sources, dev, split=-1):
        copies = []
        for u, src in enumerate(sources):
            dst = unit(p, u)
            if u == split:
                for n in range(len(PIECES)):
                    sem = landed(p, units - 1 + n if p == SHIFTS and n else u)
                    copies.append(remote(piece(src, n), piece(dst, n), send_a, sem, dev))
            else:
                copies.append(remote(src, dst, send_a, landed(p, u), dev))
        return copies

    def panel(p):
        return [unit(p, u) for u in range(units)]

    swap = [
        remote(a_ref.at[(1 - dep) * half + r], unit(0, half + r), send_a, swapped, twin_dev)
        for r in range(half)
    ]
    chain = to_panel(2, own, down)
    chain2 = to_panel(4, panel(2), down, SPLIT)
    skip = to_panel(4, panel(0), down2, SPLIT)
    wrap = to_panel(2, panel(0)[:half], down)
    own_x1 = to_panel(1, own, side_dev)
    fwd_x1 = to_panel(1, panel(2), side_dev)
    fwd_x3 = to_panel(3, panel(2), side_dev)
    top_x3 = to_panel(3, panel(4)[: units - LATE], side_dev, SPLIT)
    low_x3 = to_panel(3, panel(1), down)

    near_b = [remote(b_ref.at[m_near[k]], near_twin[k], send_b, passed.at[0], twin_dev) for k in range(2)]
    far_b, pass_b = [], []
    for k, sizes in enumerate(PARTS):
        for c, blocks in enumerate(sizes):
            part = pl.ds(sum(sizes[:c]) * inner // 16, blocks * inner // 16)
            far_b.append(
                remote(b_ref.at[m_far[k], part], far_own[k].at[part], send_b, recv_b.at[len(far_b)], row_dev)
            )
            pass_b.append(remote(far_own[k].at[part], far_twin[k].at[part], send_b, passed.at[k], twin_dev))

    def index_a(src, dst, dev):
        return remote(MA.at[pl.ds(src, 2)], MA.at[pl.ds(dst, 2)], send_m.at[0], recv_m.at[min(dst // 2, 3)], dev)

    swap_m = remote(MA.at[0], MA.at[1], send_m.at[0], recv_m.at[0], twin_dev)
    near_m = remote(MB.at[0], MB.at[1], send_m.at[1], recv_m.at[4], twin_dev)
    far_m = remote(MB.at[0], MB.at[2], send_m.at[1], recv_m.at[5], row_dev)
    pass_m = remote(MB.at[2], MB.at[3], send_m.at[1], recv_m.at[4], twin_dev)
    chain_m, chain2_m, skip_m = index_a(0, 4, down), index_a(4, 8, down), index_a(0, 8, down2)
    own_x1_m, fwd_x1_m = index_a(0, 2, side_dev), index_a(4, 2, side_dev)
    fwd_x3_m, low_x3_m = index_a(4, 6, side_dev), index_a(2, 6, down)

    drain(MA.at[0], local_sem.at[0])
    drain(MB.at[0], local_sem.at[1])
    start([swap_m] + swap)
    start(chain[:2], z > 0)
    start(own_x1[:2], side1)
    pl.when(row0)(lambda: pl.semaphore_wait(ready.at[0], 1))
    start([far_m] + far_b + [near_m] + near_b)
    swap_m.wait_recv()
    start([chain_m] + chain[2:half], z > 0)
    start([own_x1_m] + own_x1[2:half], side1)
    drain(A.at[pl.ds(0, half)], swapped)

    def local_data():
        drain(A.at[pl.ds(0, 2 * units + half)], local_sem.at[2])

    @pl.when(z == 0)
    def _():
        local_data()
        pl.semaphore_wait(ready.at[2], 1)
        start([chain_m] + wrap)

    @pl.when(both(row1, z == 1))
    def _():
        local_data()
        pl.semaphore_wait(ready.at[2], 1)
        start([skip_m] + skip)

    pl.when(side0)(lambda: pl.semaphore_wait(ready.at[1], 1))
    run[zero_at] = jnp.zeros(run.shape[1:], jnp.float32)

    def far_part(n):
        far_b[n].wait_recv()
        pass_b[n].start()

    def low(u):
        drain(A.at[pl.ds(0, 2)], landed(1, u))
        for w in (u, u + 1):
            start([low_x3[w]], side1, *([] if w >= units - LATE else [row0]))

    def recv(p, u):
        if p == 4 and u == SPLIT:
            for n in range(len(PIECES)):
                recv_piece(n)
        elif p != 3 or u >= FIRST:
            drain(unit(p, u), landed(p, u))
        elif u == 0:
            drain(A.at[pl.ds(0, FIRST)], landed(p, u))

    def recv_piece(n):
        drain(piece(unit(SHIFTS, SPLIT), n), landed(SHIFTS, units - 1 + n if n else SPLIT))

    groups = [(s, m, k, d, far) for k in range(2) for far, s, m in ((0, s_near[k], m_near[k]), (1, s_far[k], m_mine[k]))
              for d in range(2)]

    def tables(r):
        cs = []
        for s, m, _, d, far in groups:
            slot = (s + row) * 2 + d
            used = SA[slot, per_row, dep * half + r]
            for t in range(per_row):
                k = SA[slot, t, dep * half + r]
                c = SB[2 * far + d, 0, m, 0, k]
                ok = jnp.logical_and(used > t, SB[2 * far + d, 1, m, 0, k] > 0)
                c = jnp.where(ok, c, -1)
                here = r * terms + len(cs)
                before = jnp.int32(zero_at)
                for at_p, c_p in enumerate(cs):
                    before = jnp.where(c_p == c, r * terms + at_p, before)
                ktab[here] = k
                ptab[here] = before
                cs.append(c)
        for c in range(out_cols):
            last = jnp.int32(zero_at)
            for at_p, c_p in enumerate(cs):
                last = jnp.where(c_p == c, r * terms + at_p, last)
            ltab[r * out_cols + c] = last

    rights = (Bn0, Gn0, Bf0, Gf0, Bn1, Gn1, Bf1, Gf1)

    def dots(g, r):
        s, _, _, d, _ = groups[g]
        values = []
        for t in range(per_row):
            here = r * terms + g * per_row + t
            left = A[(s + row) * units + d * half + r, t]
            values.append((here, jnp.dot(left, rights[g][ktab[here]], preferred_element_type=jnp.float32)))
        return values

    def add(values):
        for here, value in values:
            run[here] = value + run[ptab[here]]

    def products(wanted):
        held = []
        for g, r in wanted:
            fresh = dots(g, r)
            add(held)
            held = fresh
        add(held)

    def whole_group(g):
        products([(g, r) for r in range(half)])

    for u in range(units):
        recv(2, u)
        if u == 0:
            drain(MA.at[pl.ds(4, 2)], recv_m.at[2])
            start([chain2_m], row1, z > 0)
            start([fwd_x1_m], side0)
            start([fwd_x3_m], side1)
        start([fwd_x1[u]], side0)
        if u == 2:
            drain(MA.at[pl.ds(2, 2)], recv_m.at[1])
            start([low_x3_m], side1)
        if u < half:
            start([chain[half + u]])
            start([own_x1[half + u]], side1)
        else:
            start(chain2[2 * (u - half) : 2 * (u - half) + 2 + (u // (units - 1)) * (len(PIECES) - 1)], row1, z > 0)
            start(fwd_x3[2 * (u - half) : 2 * (u - half) + 2], side1)
        if u == 0:
            far_m.wait_recv()
            pass_m.start()
        if u in (4, 6):
            low(u - 4)
        if u == units - 1:
            far_part(0)

    def arrive_near(*wanted):
        @pl.when(row != side)
        def _():
            for u in wanted:
                recv(3, u)

        @pl.when(both(row1, side1))
        def _():
            for u in wanted:
                recv(4, u)

    def near_units(*wanted):
        arrive_near(*wanted)
        products([(4 + u // half, u % half) for u in wanted])

    def arrive_far(*wanted):
        @pl.when(row == side)
        def _():
            for u in wanted:
                recv(3, u)

        if units - 1 in wanted:
            pl.when(both(row1, side0))(lambda: recv(4, units - 1))

    def far_units(*wanted):
        arrive_far(*wanted)
        products([(6 + u // half, u % half) for u in wanted])

    scalars = [pltpu.make_async_copy(MA.at[pl.ds(0, 2 * REACH)], SA, local_sem.at[0]), pltpu.make_async_copy(MB, SB, local_sem.at[1])]

    for u in range(units):
        if u < units - LATE:
            @pl.when(both(row1, side0))
            def _():
                if u == SPLIT:
                    for n in range(len(PIECES)):
                        recv_piece(n)
                        top_x3[u + n].start()
                else:
                    recv(4, u)
                    top_x3[u].start()

        if u in (0, 2):
            low(half + u)
        if u == 0:
            pl.when(row0)(lambda: drain(MA.at[pl.ds(6, 2)], recv_m.at[3]))
            pl.when(row1)(lambda: drain(MA.at[pl.ds(6, 4)], recv_m.at[3]))
            drain(MB.at[pl.ds(0, 2)], recv_m.at[4])
            start(scalars)
        if u == 1:
            for copy in scalars:
                copy.wait()
            pl.when(z > row)(local_data)
            drain(A.at[pl.ds(0, 3 * units)], passed.at[0])
        if u in (3, 5):
            far_part(u // 2)
        if u in (1, 2):
            for r in range((u - 1) * half // 2, u * half // 2):
                tables(r)
        if u == 2:
            whole_group(0)
        if u == 3:
            whole_group(1)
            whole_group(2)
        if u == 4:
            whole_group(3)
            near_units(0)
        if u == 5:
            near_units(1, 2)
    far_part(len(far_b) - 1)

    def place(r):
        for c in range(out_cols):
            out_ref[r * size : (r + 1) * size, c * size : (c + 1) * size] = run[ltab[r * out_cols + c]].astype(
                out_ref.dtype
            )

    def finish(*rows, near=False):
        wanted = [half + r for r in rows]
        if near:
            arrive_near(units - 1)
            wanted.append(half - 1)
        arrive_far(*wanted)
        steps = [(7, r) for r in rows]
        if near:
            steps[-1:] = [(5, half - 1), (6, half - 1), (7, half - 1)]
        held = None
        for g, r in steps + [(None, None)]:
            fresh = None if g is None else (g, r, dots(g, r))
            if held is not None:
                add(held[2])
                if held[0] == 7:
                    place(held[1])
            held = fresh

    def last_pass():
        drain(A.at[pl.ds(0, units)], passed.at[1])

    @pl.when(side0)
    def _():
        near_units(3, 4, 5, 6, 7)
        far_units(0, 1, 2, 3)
        last_pass()
        finish(0, 1, 2, 3)

    @pl.when(both(side1, z < top))
    def _():
        near_units(3, 4, 5, 6, 7)
        far_units(0, 1, 2, 3)
        last_pass()
        finish(0, 1)
        finish(3)
        finish(2)

    @pl.when(both(side1, z == top))
    def _():
        near_units(3, 4)
        far_units(0)
        near_units(5)
        far_units(1)
        last_pass()
        near_units(6)
        far_units(2)
        finish(0, 1)
        finish(3, near=True)
        finish(2)

    for r in range(2):
        for side_n, flag in enumerate((side0, side1)):
            for more, where in (((0, z >= 0),) if r == 0 else ((0, z == 0), (2, z == 1), (1, z > 1))):
                here = both(row == r, flag, where)
                across = (0, 2 * units) if r == 0 else (units - LATE, units + LATE)
                n = 2 * units + half + across[side_n] + more * units
                pl.when(here)(functools.partial(drain, run.at[pl.ds(0, n)], send_a))
                pl.when(here)(functools.partial(drain, MA.at[pl.ds(0, 5 + 4 * side_n + 2 * more)], send_m.at[0]))
    drain(run.at[pl.ds(0, 6 * units)], send_b)
    drain(MB.at[pl.ds(0, 3)], send_m.at[1])


def local_fast(n_col, a_tiles, a_cols, a_count, b_tiles, b_cols, b_count):
    block_rows, per_row, size = a_tiles.shape[2:5]
    slots, inner = b_tiles.shape[0], b_tiles.shape[4]
    half = block_rows // 2
    count = half * SHIFTS * 2 * per_row
    hbm = pl.BlockSpec(memory_space=pltpu.HBM)
    index_shapes = [(REACH * 2, per_row + 1, block_rows), (4, 2, slots, 1, inner)]
    index_vmem = [(REACH * 2 + 4, per_row + 1, block_rows), index_shapes[1]]
    call = pl.pallas_call(
        functools.partial(gather_multiply, n_col),
        out_shape=jax.ShapeDtypeStruct((half * size, BC * size), jnp.bfloat16),
        in_specs=[hbm] * 6,
        out_specs=pl.BlockSpec(memory_space=pltpu.VMEM),
        scratch_shapes=[pltpu.VMEM((REACH * block_rows, per_row, size, size), jnp.bfloat16)]
        + [pltpu.VMEM((inner, size, size), jnp.bfloat16)] * 8
        + [pltpu.VMEM(shape, jnp.int32) for shape in index_vmem]
        + [pltpu.SMEM(shape, jnp.int32) for shape in index_shapes]
        + [
            pltpu.VMEM((count + 1, size, size), jnp.float32),
            pltpu.SMEM((count,), jnp.int32),
            pltpu.SMEM((count,), jnp.int32),
            pltpu.SMEM((half * BC,), jnp.int32),
            pltpu.SemaphoreType.DMA((2,)),
            pltpu.SemaphoreType.DMA((6,)),
            pltpu.SemaphoreType.DMA,
            pltpu.SemaphoreType.DMA((half,)),
            pltpu.SemaphoreType.DMA((block_rows,)),
            pltpu.SemaphoreType.DMA((block_rows - FIRST + 1,)),
            pltpu.SemaphoreType.DMA((block_rows + len(PIECES) - 1,)),
            pltpu.SemaphoreType.DMA,
            pltpu.SemaphoreType.DMA,
            pltpu.SemaphoreType.DMA((sum(map(len, PARTS)),)),
            pltpu.SemaphoreType.DMA((2,)),
            pltpu.SemaphoreType.REGULAR((3,)),
            pltpu.SemaphoreType.DMA((3,)),
        ],
        compiler_params=pltpu.CompilerParams(
            collective_id=0, has_side_effects=True, vmem_limit_bytes=40 * 1024 * 1024
        ),
    )
    operands = [
        jnp.swapaxes(a_cols.reshape(block_rows, per_row), 0, 1),
        a_count.reshape(1, block_rows),
        b_cols.reshape(slots, 1, inner),
        b_count.reshape(slots, 1, inner),
        a_tiles.reshape(block_rows, per_row, size, size),
        b_tiles.reshape(slots, inner, size, size),
    ]
    return call(*(pltpu.with_memory_space_constraint(x, pltpu.HBM) for x in operands))


def solution(mesh):
    placed = (
        P("row", ("col", "depth"), None, None, None, None),
        P("row", ("col", "depth"), None, None),
        P("row", ("col", "depth"), None),
        P(None, "row", "depth", "col", None, None, None, None),
        P(None, "row", "depth", "col", None, None),
        P(None, "row", "depth", "col", None),
    )
    n_col = mesh.shape["col"]
    if mesh.shape["row"] == 2 and mesh.shape["depth"] == 2 and n_col == 2 * SHIFTS:
        body = functools.partial(local_fast, n_col)
    else:
        body = local
    return jax.shard_map(
        body, mesh=mesh, in_specs=placed, out_specs=P(("row", "depth"), "col"), check_vma=False
    )
```

```python
import functools
import math

import jax
import jax.numpy as jnp
from jax import lax
from jax.experimental import pallas as pl
from jax.experimental.pallas import tpu as pltpu
from jax.sharding import PartitionSpec as P

BC = 12
SHIFTS = 4


def for_sending(array):
    return jax.tree.map(lambda a: a.astype(jnp.bfloat16) if a.dtype == jnp.float32 else a, array)


def shifted(value, axis, steps):
    count = lax.axis_size(axis)
    pairs = [(source, (source + steps) % count) for source in range(count)]
    return lax.ppermute(value, axis, pairs)


def dense_panel(tiles_b, cols_b, count_b, width):
    slot_ids = lax.broadcasted_iota(jnp.int32, cols_b.shape, 1)
    valid_slot = slot_ids < count_b[:, None]
    targets = lax.broadcasted_iota(jnp.int32, (1, 1, width), 2)
    placing = jnp.logical_and(cols_b[:, :, None] == targets, valid_slot[:, :, None]).astype(
        jnp.bfloat16
    )
    spread = jnp.einsum("kuc,kuab->kacb", placing, tiles_b, preferred_element_type=jnp.float32)
    inner_blocks = tiles_b.shape[0]
    tile_size = tiles_b.shape[2]
    return spread.astype(jnp.bfloat16).reshape(inner_blocks, tile_size, width * tile_size)


def panel_product(tiles_a, cols_a, count_a, rows_dense):
    block_rows = tiles_a.shape[0]
    per_row = tiles_a.shape[1]
    tile_size = tiles_a.shape[2]
    slot_ids = lax.broadcasted_iota(jnp.int32, cols_a.shape, 1)
    valid_slot = slot_ids < count_a[:, None]
    masked = jnp.where(valid_slot[:, :, None, None], tiles_a, jnp.zeros_like(tiles_a))
    group_rows = math.gcd(block_rows, 4)

    def one_group(pieces):
        tiles_part, cols_part = pieces
        picks = lax.broadcasted_iota(jnp.int32, cols_part.shape + (rows_dense.shape[0],), 2)
        picks = (cols_part[:, :, None] == picks).astype(rows_dense.dtype)
        chosen = jnp.einsum("rtk,kbn->rtbn", picks, rows_dense, preferred_element_type=jnp.float32)
        chosen = chosen.astype(rows_dense.dtype)
        return jnp.einsum("rtab,rtbn->ran", tiles_part, chosen, preferred_element_type=jnp.float32)

    grouped = lax.map(
        one_group,
        (
            masked.reshape(block_rows // group_rows, group_rows, per_row, tile_size, tile_size),
            cols_a.reshape(block_rows // group_rows, group_rows, per_row),
        ),
    )
    return grouped.reshape(block_rows, tile_size, rows_dense.shape[2])


def roll_slots(stack, offset):
    slot_total = stack[0].shape[0]
    return tuple(
        (
            lax.dynamic_slice_in_dim(
                jnp.concatenate([member, member], 0), offset % slot_total, slot_total, 0
            )
            for member in stack
        )
    )


def select_if(flag, fresh, stale):
    return tuple((jnp.where(flag, new_part, old_part) for new_part, old_part in zip(fresh, stale)))


def local(a_tiles, a_cols, a_count, b_tiles, b_cols, b_count):
    rows_axis = lax.axis_size("row")
    cols_axis = lax.axis_size("col")
    row_group = lax.axis_index("row")
    col_group = lax.axis_index("col")
    tiles_a = a_tiles[0, 0]
    cols_a = a_cols[0, 0]
    count_a = a_count[0, 0]
    tiles_b = b_tiles[:, 0, 0, 0]
    cols_b = b_cols[:, 0, 0, 0]
    count_b = b_count[:, 0, 0, 0]
    for bit_pos in range((rows_axis - 1).bit_length()):
        stride = 1 << bit_pos
        moved = (
            shifted(tiles_a, "col", cols_axis - stride),
            shifted(for_sending(cols_a), "col", cols_axis - stride).astype(cols_a.dtype),
            shifted(for_sending(count_a), "col", cols_axis - stride).astype(count_a.dtype),
        )
        tiles_a, cols_a, count_a = select_if(
            row_group // stride % 2 == 1, moved, (tiles_a, cols_a, count_a)
        )
    for bit_pos in range((cols_axis - 1).bit_length()):
        stride = 1 << bit_pos
        nearby = stride % rows_axis
        if nearby:
            moved = (
                shifted(tiles_b, "row", rows_axis - nearby),
                shifted(for_sending(cols_b), "row", rows_axis - nearby).astype(cols_b.dtype),
                shifted(for_sending(count_b), "row", rows_axis - nearby).astype(count_b.dtype),
            )
        else:
            moved = (tiles_b, cols_b, count_b)
        moved = roll_slots(moved, (row_group + stride) // rows_axis)
        tiles_b, cols_b, count_b = select_if(
            col_group // stride % 2 == 1, moved, (tiles_b, cols_b, count_b)
        )
    tile_size = tiles_a.shape[2]
    running = jnp.zeros((tiles_a.shape[0], tile_size, BC * tile_size), jnp.float32)
    for turn_no in range(SHIFTS):
        current_tiles = tiles_b[0]
        current_cols = cols_b[0]
        current_count = count_b[0]
        rows_dense = dense_panel(current_tiles, current_cols, current_count, BC)
        running = running + panel_product(tiles_a, cols_a, count_a, rows_dense)
        if turn_no + 1 < SHIFTS:
            tiles_a, cols_a, count_a = (
                shifted(tiles_a, "col", cols_axis - 1),
                shifted(for_sending(cols_a), "col", cols_axis - 1).astype(cols_a.dtype),
                shifted(for_sending(count_a), "col", cols_axis - 1).astype(count_a.dtype),
            )
            moved = (
                shifted(tiles_b, "row", rows_axis - 1),
                shifted(for_sending(cols_b), "row", rows_axis - 1).astype(cols_b.dtype),
                shifted(for_sending(count_b), "row", rows_axis - 1).astype(count_b.dtype),
            )
            tiles_b, cols_b, count_b = roll_slots(moved, (row_group + 1) // rows_axis)
    flat_running = running.reshape(-1, running.shape[2])
    summed = lax.psum(flat_running, "depth")
    half_rows = flat_running.shape[0] // lax.axis_size("depth")
    own_rows = lax.dynamic_slice_in_dim(summed, lax.axis_index("depth") * half_rows, half_rows, 0)
    return own_rows.astype(jnp.bfloat16)


REACH = SHIFTS + 1
PARTS = ((16,), (7, 6, 3))
LATE = 1
SPLIT = 6
PIECES = ((0, 0, 2), (1, 0, 1), (1, 1, 1))
FIRST = 3
MESH_ID = pl.DeviceIdType.MESH


def gather_multiply(n_col, a_cols, a_count, b_cols, b_count, a_ref, b_ref, out_ref, A, Bn0, Bn1, Bf0, Bf1,
                    Gn0, Gn1, Gf0, Gf1, MA, MB, SA, SB, run, ktab, ptab, ltab,
                    send_m, recv_m, send_a, recv_1, recv_2, recv_3, recv_4, swapped, send_b, recv_b, passed, ready,
                    local_sem):
    row = lax.axis_index("row")
    col = lax.axis_index("col")
    dep = lax.axis_index("depth")
    side = lax.rem(col, 2)
    z = lax.div(col, 2)
    top = n_col // 2 - 1
    per_row, size = A.shape[1:3]
    units = A.shape[0] // REACH
    half = units // 2
    inner = Bn0.shape[0]
    out_cols = out_ref.shape[1] // size
    terms = SHIFTS * 2 * per_row
    zero_at = half * terms
    row0, row1, side0, side1 = row == 0, row == 1, side == 0, side == 1

    def both(*flags):
        return functools.reduce(jnp.logical_and, flags)

    def at(col_offset, flip_depth=False, flip_row=False):
        return (
            1 - row if flip_row else row,
            lax.rem(col + col_offset + n_col, n_col),
            1 - dep if flip_depth else dep,
        )

    twin_dev, row_dev = at(0, True), at(0, False, True)
    side_dev = (row, col + 1 - 2 * side, dep)
    down, up, down2, up2 = at(-2), at(2), at(-4), at(4)

    def remote(src, dst, ssem, rsem, dev):
        return pltpu.make_async_remote_copy(
            src_ref=src, dst_ref=dst, send_sem=ssem, recv_sem=rsem, device_id=dev, device_id_type=MESH_ID
        )

    def signal(sem, dev):
        pl.semaphore_signal(sem, inc=1, device_id=dev, device_id_type=MESH_ID)

    def drain(ref, sem):
        pltpu.make_async_copy(ref, ref, sem).wait()

    def start(copies, *flags):
        def go():
            for copy in copies:
                copy.start()

        if flags:
            pl.when(both(*flags))(go)
        else:
            go()

    s_near = [side + 2 * k for k in range(2)]
    s_far = [1 - side + 2 * k for k in range(2)]
    m_near = [lax.rem(row + col + s, n_col) // 2 for s in s_near]
    m_far = [lax.rem(1 - row + col + s, n_col) // 2 for s in s_far]
    m_mine = [lax.rem(row + col + s, n_col) // 2 for s in s_far]
    near_own, near_twin = (Bn0, Bn1), (Gn0, Gn1)
    far_own, far_twin = (Bf0, Bf1), (Gf0, Gf1)

    index_local = [
        pltpu.make_async_copy(src, dst, local_sem.at[n])
        for src, dst, n in (
            (a_cols, MA.at[0, pl.ds(0, per_row)], 0), (a_count, MA.at[0, pl.ds(per_row, 1)], 0),
            (b_cols, MB.at[0, 0], 1), (b_count, MB.at[0, 1], 1),
        )
    ]
    b_local = [pltpu.make_async_copy(b_ref.at[m_near[k]], near_own[k], local_sem.at[2]) for k in range(2)]
    a_local = pltpu.make_async_copy(a_ref.at[pl.ds(dep * half, half)], A.at[pl.ds(0, half)], local_sem.at[2])
    start(index_local + b_local + [a_local])

    @pl.when(row0)
    def _():
        for slot in range(2 * SHIFTS, 2 * REACH):
            MA[slot] = jnp.zeros(MA.shape[1:], MA.dtype)

    barrier = pltpu.get_barrier_semaphore()
    signal(barrier, twin_dev)
    pl.when(row0)(lambda: signal(barrier, row_dev))
    pl.when(side0)(lambda: signal(barrier, side_dev))
    pl.when(z < top)(lambda: signal(barrier, up))
    pl.when(z == 0)(lambda: signal(barrier, down))
    pl.when(both(row1, z == 1))(lambda: signal(barrier, down2))
    greeted = 1 + row + side + jnp.where(z > 0, 1, 0) + jnp.where(z == top, 1 + row, 0)
    pl.semaphore_wait(barrier, greeted)
    pl.when(z == top)(lambda: signal(ready.at[2], up))
    pl.when(both(row1, z == top))(lambda: signal(ready.at[2], up2))
    pl.when(row1)(lambda: signal(ready.at[0], row_dev))
    pl.when(side1)(lambda: signal(ready.at[1], side_dev))

    def unit(p, u):
        return A.at[p * units + u]

    own = [a_ref.at[dep * half + r] for r in range(half)] + [unit(0, half + r) for r in range(half)]

    def landed(p, u):
        return {1: recv_1, 2: recv_2, 3: recv_3, 4: recv_4}[p].at[{1: u // 2, 3: max(u - FIRST + 1, 0)}.get(p, u)]

    def piece(ref, n):
        t, begin, length = PIECES[n]
        return ref.at[t, pl.ds(begin * size // 2, length * size // 2)]

    def to_panel(p, sources, dev, split=-1):
        copies = []
        for u, src in enumerate(sources):
            dst = unit(p, u)
            if u == split:
                for n in range(len(PIECES)):
                    sem = landed(p, units - 1 + n if p == SHIFTS and n else u)
                    copies.append(remote(piece(src, n), piece(dst, n), send_a, sem, dev))
            else:
                copies.append(remote(src, dst, send_a, landed(p, u), dev))
        return copies

    def panel(p):
        return [unit(p, u) for u in range(units)]

    swap = [
        remote(a_ref.at[(1 - dep) * half + r], unit(0, half + r), send_a, swapped, twin_dev)
        for r in range(half)
    ]
    chain = to_panel(2, own, down)
    chain2 = to_panel(4, panel(2), down, SPLIT)
    skip = to_panel(4, panel(0), down2, SPLIT)
    wrap = to_panel(2, panel(0)[:half], down)
    own_x1 = to_panel(1, own, side_dev)
    fwd_x1 = to_panel(1, panel(2), side_dev)
    fwd_x3 = to_panel(3, panel(2), side_dev)
    top_x3 = to_panel(3, panel(4)[: units - LATE], side_dev, SPLIT)
    low_x3 = to_panel(3, panel(1), down)

    near_b = [remote(b_ref.at[m_near[k]], near_twin[k], send_b, passed.at[0], twin_dev) for k in range(2)]
    far_b, pass_b = [], []
    for k, sizes in enumerate(PARTS):
        for c, blocks in enumerate(sizes):
            part = pl.ds(sum(sizes[:c]) * inner // 16, blocks * inner // 16)
            far_b.append(
                remote(b_ref.at[m_far[k], part], far_own[k].at[part], send_b, recv_b.at[len(far_b)], row_dev)
            )
            pass_b.append(remote(far_own[k].at[part], far_twin[k].at[part], send_b, passed.at[k], twin_dev))

    def index_a(src, dst, dev):
        return remote(MA.at[pl.ds(src, 2)], MA.at[pl.ds(dst, 2)], send_m.at[0], recv_m.at[min(dst // 2, 3)], dev)

    swap_m = remote(MA.at[0], MA.at[1], send_m.at[0], recv_m.at[0], twin_dev)
    near_m = remote(MB.at[0], MB.at[1], send_m.at[1], recv_m.at[4], twin_dev)
    far_m = remote(MB.at[0], MB.at[2], send_m.at[1], recv_m.at[5], row_dev)
    pass_m = remote(MB.at[2], MB.at[3], send_m.at[1], recv_m.at[4], twin_dev)
    chain_m, chain2_m, skip_m = index_a(0, 4, down), index_a(4, 8, down), index_a(0, 8, down2)
    own_x1_m, fwd_x1_m = index_a(0, 2, side_dev), index_a(4, 2, side_dev)
    fwd_x3_m, low_x3_m = index_a(4, 6, side_dev), index_a(2, 6, down)

    drain(MA.at[0], local_sem.at[0])
    drain(MB.at[0], local_sem.at[1])
    start([swap_m] + swap)
    start(chain[:2], z > 0)
    start(own_x1[:2], side1)
    pl.when(row0)(lambda: pl.semaphore_wait(ready.at[0], 1))
    start([far_m] + far_b + [near_m] + near_b)
    swap_m.wait_recv()
    start([chain_m] + chain[2:half], z > 0)
    start([own_x1_m] + own_x1[2:half], side1)
    drain(A.at[pl.ds(0, half)], swapped)

    def local_data():
        drain(A.at[pl.ds(0, 2 * units + half)], local_sem.at[2])

    @pl.when(z == 0)
    def _():
        local_data()
        pl.semaphore_wait(ready.at[2], 1)
        start([chain_m] + wrap)

    @pl.when(both(row1, z == 1))
    def _():
        local_data()
        pl.semaphore_wait(ready.at[2], 1)
        start([skip_m] + skip)

    pl.when(side0)(lambda: pl.semaphore_wait(ready.at[1], 1))
    run[zero_at] = jnp.zeros(run.shape[1:], jnp.float32)

    def far_part(n):
        far_b[n].wait_recv()
        pass_b[n].start()

    def low(u):
        drain(A.at[pl.ds(0, 2)], landed(1, u))
        for w in (u, u + 1):
            start([low_x3[w]], side1, *([] if w >= units - LATE else [row0]))

    def recv(p, u):
        if p == 4 and u == SPLIT:
            for n in range(len(PIECES)):
                recv_piece(n)
        elif p != 3 or u >= FIRST:
            drain(unit(p, u), landed(p, u))
        elif u == 0:
            drain(A.at[pl.ds(0, FIRST)], landed(p, u))

    def recv_piece(n):
        drain(piece(unit(SHIFTS, SPLIT), n), landed(SHIFTS, units - 1 + n if n else SPLIT))

    groups = [(s, m, k, d, far) for k in range(2) for far, s, m in ((0, s_near[k], m_near[k]), (1, s_far[k], m_mine[k]))
              for d in range(2)]

    def tables(r):
        cs = []
        for s, m, _, d, far in groups:
            slot = (s + row) * 2 + d
            used = SA[slot, per_row, dep * half + r]
            for t in range(per_row):
                k = SA[slot, t, dep * half + r]
                c = SB[2 * far + d, 0, m, 0, k]
                ok = jnp.logical_and(used > t, SB[2 * far + d, 1, m, 0, k] > 0)
                c = jnp.where(ok, c, -1)
                here = r * terms + len(cs)
                before = jnp.int32(zero_at)
                for at_p, c_p in enumerate(cs):
                    before = jnp.where(c_p == c, r * terms + at_p, before)
                ktab[here] = k
                ptab[here] = before
                cs.append(c)
        for c in range(out_cols):
            last = jnp.int32(zero_at)
            for at_p, c_p in enumerate(cs):
                last = jnp.where(c_p == c, r * terms + at_p, last)
            ltab[r * out_cols + c] = last

    rights = (Bn0, Gn0, Bf0, Gf0, Bn1, Gn1, Bf1, Gf1)

    def dots(g, r):
        s, _, _, d, _ = groups[g]
        values = []
        for t in range(per_row):
            here = r * terms + g * per_row + t
            left = A[(s + row) * units + d * half + r, t]
            values.append((here, jnp.dot(left, rights[g][ktab[here]], preferred_element_type=jnp.float32)))
        return values

    def add(values):
        for here, value in values:
            run[here] = value + run[ptab[here]]

    def products(wanted):
        held = []
        for g, r in wanted:
            fresh = dots(g, r)
            add(held)
            held = fresh
        add(held)

    def whole_group(g):
        products([(g, r) for r in range(half)])

    for u in range(units):
        recv(2, u)
        start([fwd_x1[u]], side0)
        if u == 0:
            drain(MA.at[pl.ds(4, 2)], recv_m.at[2])
            start([chain2_m], row1, z > 0)
            start([fwd_x1_m], side0)
            start([fwd_x3_m], side1)
        if u == 2:
            drain(MA.at[pl.ds(2, 2)], recv_m.at[1])
            start([low_x3_m], side1)
        if u < half:
            start([chain[half + u]])
            start([own_x1[half + u]], side1)
        else:
            start(chain2[2 * (u - half) : 2 * (u - half) + 2 + (u // (units - 1)) * (len(PIECES) - 1)], row1, z > 0)
            start(fwd_x3[2 * (u - half) : 2 * (u - half) + 2], side1)
        if u == 0:
            far_m.wait_recv()
            pass_m.start()
        if u in (4, 6):
            low(u - 4)
        if u == units - 1:
            far_part(0)

    def arrive_near(*wanted):
        @pl.when(row != side)
        def _():
            for u in wanted:
                recv(3, u)

        @pl.when(both(row1, side1))
        def _():
            for u in wanted:
                recv(4, u)

    def near_units(*wanted):
        arrive_near(*wanted)
        products([(4 + u // half, u % half) for u in wanted])

    def arrive_far(*wanted):
        @pl.when(row == side)
        def _():
            for u in wanted:
                recv(3, u)

        if units - 1 in wanted:
            pl.when(both(row1, side0))(lambda: recv(4, units - 1))

    def far_units(*wanted):
        arrive_far(*wanted)
        products([(6 + u // half, u % half) for u in wanted])

    scalars = [pltpu.make_async_copy(MA.at[pl.ds(0, 2 * REACH)], SA, local_sem.at[0]), pltpu.make_async_copy(MB, SB, local_sem.at[1])]

    for u in range(units):
        if u < units - LATE:
            @pl.when(both(row1, side0))
            def _():
                if u == SPLIT:
                    for n in range(len(PIECES)):
                        recv_piece(n)
                        top_x3[u + n].start()
                else:
                    recv(4, u)
                    top_x3[u].start()

        if u in (0, 2):
            low(half + u)
        if u == 0:
            pl.when(row0)(lambda: drain(MA.at[pl.ds(6, 2)], recv_m.at[3]))
            pl.when(row1)(lambda: drain(MA.at[pl.ds(6, 4)], recv_m.at[3]))
            drain(MB.at[pl.ds(0, 2)], recv_m.at[4])
            start(scalars)
        if u == 1:
            for copy in scalars:
                copy.wait()
            pl.when(z > row)(local_data)
            drain(A.at[pl.ds(0, 3 * units)], passed.at[0])
        if u in (3, 5):
            far_part(u // 2)
        if u in (1, 2):
            for r in range((u - 1) * half // 2, u * half // 2):
                tables(r)
        if u == 2:
            whole_group(0)
        if u == 3:
            whole_group(1)
            whole_group(2)
        if u == 4:
            whole_group(3)
            near_units(0)
        if u == 5:
            near_units(1, 2)
    far_part(len(far_b) - 1)

    def place(r):
        for c in range(out_cols):
            out_ref[r * size : (r + 1) * size, c * size : (c + 1) * size] = run[ltab[r * out_cols + c]].astype(
                out_ref.dtype
            )

    def finish(*rows, near=False):
        wanted = [half + r for r in rows]
        if near:
            arrive_near(units - 1)
            wanted.append(half - 1)
        arrive_far(*wanted)
        steps = [(7, r) for r in rows]
        if near:
            steps[-1:] = [(5, half - 1), (6, half - 1), (7, half - 1)]
        held = None
        for g, r in steps + [(None, None)]:
            fresh = None if g is None else (g, r, dots(g, r))
            if held is not None:
                add(held[2])
                if held[0] == 7:
                    place(held[1])
            held = fresh

    def last_pass():
        drain(A.at[pl.ds(0, units)], passed.at[1])

    @pl.when(side0)
    def _():
        near_units(3, 4, 5, 6, 7)
        far_units(0, 1, 2, 3)
        last_pass()
        finish(0, 1, 2, 3)

    @pl.when(both(side1, z < top))
    def _():
        near_units(3, 4, 5, 6, 7)
        far_units(0, 1, 2, 3)
        last_pass()
        finish(0, 1)
        finish(3)
        finish(2)

    @pl.when(both(side1, z == top))
    def _():
        near_units(3, 4)
        far_units(0)
        near_units(5)
        far_units(1)
        last_pass()
        near_units(6)
        far_units(2)
        finish(0, 1)
        finish(3, near=True)
        finish(2)

    for r in range(2):
        for side_n, flag in enumerate((side0, side1)):
            for more, where in (((0, z >= 0),) if r == 0 else ((0, z == 0), (2, z == 1), (1, z > 1))):
                here = both(row == r, flag, where)
                across = (0, 2 * units) if r == 0 else (units - LATE, units + LATE)
                n = 2 * units + half + across[side_n] + more * units
                pl.when(here)(functools.partial(drain, run.at[pl.ds(0, n)], send_a))
                pl.when(here)(functools.partial(drain, MA.at[pl.ds(0, 5 + 4 * side_n + 2 * more)], send_m.at[0]))
    drain(run.at[pl.ds(0, 6 * units)], send_b)
    drain(MB.at[pl.ds(0, 3)], send_m.at[1])


def local_fast(n_col, a_tiles, a_cols, a_count, b_tiles, b_cols, b_count):
    block_rows, per_row, size = a_tiles.shape[2:5]
    slots, inner = b_tiles.shape[0], b_tiles.shape[4]
    half = block_rows // 2
    count = half * SHIFTS * 2 * per_row
    hbm = pl.BlockSpec(memory_space=pltpu.HBM)
    index_shapes = [(REACH * 2, per_row + 1, block_rows), (4, 2, slots, 1, inner)]
    index_vmem = [(REACH * 2 + 4, per_row + 1, block_rows), index_shapes[1]]
    call = pl.pallas_call(
        functools.partial(gather_multiply, n_col),
        out_shape=jax.ShapeDtypeStruct((half * size, BC * size), jnp.bfloat16),
        in_specs=[hbm] * 6,
        out_specs=pl.BlockSpec(memory_space=pltpu.VMEM),
        scratch_shapes=[pltpu.VMEM((REACH * block_rows, per_row, size, size), jnp.bfloat16)]
        + [pltpu.VMEM((inner, size, size), jnp.bfloat16)] * 8
        + [pltpu.VMEM(shape, jnp.int32) for shape in index_vmem]
        + [pltpu.SMEM(shape, jnp.int32) for shape in index_shapes]
        + [
            pltpu.VMEM((count + 1, size, size), jnp.float32),
            pltpu.SMEM((count,), jnp.int32),
            pltpu.SMEM((count,), jnp.int32),
            pltpu.SMEM((half * BC,), jnp.int32),
            pltpu.SemaphoreType.DMA((2,)),
            pltpu.SemaphoreType.DMA((6,)),
            pltpu.SemaphoreType.DMA,
            pltpu.SemaphoreType.DMA((half,)),
            pltpu.SemaphoreType.DMA((block_rows,)),
            pltpu.SemaphoreType.DMA((block_rows - FIRST + 1,)),
            pltpu.SemaphoreType.DMA((block_rows + len(PIECES) - 1,)),
            pltpu.SemaphoreType.DMA,
            pltpu.SemaphoreType.DMA,
            pltpu.SemaphoreType.DMA((sum(map(len, PARTS)),)),
            pltpu.SemaphoreType.DMA((2,)),
            pltpu.SemaphoreType.REGULAR((3,)),
            pltpu.SemaphoreType.DMA((3,)),
        ],
        compiler_params=pltpu.CompilerParams(
            collective_id=0, has_side_effects=True, vmem_limit_bytes=40 * 1024 * 1024
        ),
    )
    operands = [
        jnp.swapaxes(a_cols.reshape(block_rows, per_row), 0, 1),
        a_count.reshape(1, block_rows),
        b_cols.reshape(slots, 1, inner),
        b_count.reshape(slots, 1, inner),
        a_tiles.reshape(block_rows, per_row, size, size),
        b_tiles.reshape(slots, inner, size, size),
    ]
    return call(*(pltpu.with_memory_space_constraint(x, pltpu.HBM) for x in operands))


def solution(mesh):
    placed = (
        P("row", ("col", "depth"), None, None, None, None),
        P("row", ("col", "depth"), None, None),
        P("row", ("col", "depth"), None),
        P(None, "row", "depth", "col", None, None, None, None),
        P(None, "row", "depth", "col", None, None),
        P(None, "row", "depth", "col", None),
    )
    n_col = mesh.shape["col"]
    if mesh.shape["row"] == 2 and mesh.shape["depth"] == 2 and n_col == 2 * SHIFTS:
        body = functools.partial(local_fast, n_col)
    else:
        body = local
    return jax.shard_map(
        body, mesh=mesh, in_specs=placed, out_specs=P(("row", "depth"), "col"), check_vma=False
    )
```

```python
import functools
import math

import jax
import jax.numpy as jnp
from jax import lax
from jax.experimental import pallas as pl
from jax.experimental.pallas import tpu as pltpu
from jax.sharding import PartitionSpec as P

BC = 12
SHIFTS = 4


def for_sending(array):
    return jax.tree.map(lambda a: a.astype(jnp.bfloat16) if a.dtype == jnp.float32 else a, array)


def shifted(value, axis, steps):
    count = lax.axis_size(axis)
    pairs = [(source, (source + steps) % count) for source in range(count)]
    return lax.ppermute(value, axis, pairs)


def dense_panel(tiles_b, cols_b, count_b, width):
    slot_ids = lax.broadcasted_iota(jnp.int32, cols_b.shape, 1)
    valid_slot = slot_ids < count_b[:, None]
    targets = lax.broadcasted_iota(jnp.int32, (1, 1, width), 2)
    placing = jnp.logical_and(cols_b[:, :, None] == targets, valid_slot[:, :, None]).astype(
        jnp.bfloat16
    )
    spread = jnp.einsum("kuc,kuab->kacb", placing, tiles_b, preferred_element_type=jnp.float32)
    inner_blocks = tiles_b.shape[0]
    tile_size = tiles_b.shape[2]
    return spread.astype(jnp.bfloat16).reshape(inner_blocks, tile_size, width * tile_size)


def panel_product(tiles_a, cols_a, count_a, rows_dense):
    block_rows = tiles_a.shape[0]
    per_row = tiles_a.shape[1]
    tile_size = tiles_a.shape[2]
    slot_ids = lax.broadcasted_iota(jnp.int32, cols_a.shape, 1)
    valid_slot = slot_ids < count_a[:, None]
    masked = jnp.where(valid_slot[:, :, None, None], tiles_a, jnp.zeros_like(tiles_a))
    group_rows = math.gcd(block_rows, 4)

    def one_group(pieces):
        tiles_part, cols_part = pieces
        picks = lax.broadcasted_iota(jnp.int32, cols_part.shape + (rows_dense.shape[0],), 2)
        picks = (cols_part[:, :, None] == picks).astype(rows_dense.dtype)
        chosen = jnp.einsum("rtk,kbn->rtbn", picks, rows_dense, preferred_element_type=jnp.float32)
        chosen = chosen.astype(rows_dense.dtype)
        return jnp.einsum("rtab,rtbn->ran", tiles_part, chosen, preferred_element_type=jnp.float32)

    grouped = lax.map(
        one_group,
        (
            masked.reshape(block_rows // group_rows, group_rows, per_row, tile_size, tile_size),
            cols_a.reshape(block_rows // group_rows, group_rows, per_row),
        ),
    )
    return grouped.reshape(block_rows, tile_size, rows_dense.shape[2])


def roll_slots(stack, offset):
    slot_total = stack[0].shape[0]
    return tuple(
        (
            lax.dynamic_slice_in_dim(
                jnp.concatenate([member, member], 0), offset % slot_total, slot_total, 0
            )
            for member in stack
        )
    )


def select_if(flag, fresh, stale):
    return tuple((jnp.where(flag, new_part, old_part) for new_part, old_part in zip(fresh, stale)))


def local(a_tiles, a_cols, a_count, b_tiles, b_cols, b_count):
    rows_axis = lax.axis_size("row")
    cols_axis = lax.axis_size("col")
    row_group = lax.axis_index("row")
    col_group = lax.axis_index("col")
    tiles_a = a_tiles[0, 0]
    cols_a = a_cols[0, 0]
    count_a = a_count[0, 0]
    tiles_b = b_tiles[:, 0, 0, 0]
    cols_b = b_cols[:, 0, 0, 0]
    count_b = b_count[:, 0, 0, 0]
    for bit_pos in range((rows_axis - 1).bit_length()):
        stride = 1 << bit_pos
        moved = (
            shifted(tiles_a, "col", cols_axis - stride),
            shifted(for_sending(cols_a), "col", cols_axis - stride).astype(cols_a.dtype),
            shifted(for_sending(count_a), "col", cols_axis - stride).astype(count_a.dtype),
        )
        tiles_a, cols_a, count_a = select_if(
            row_group // stride % 2 == 1, moved, (tiles_a, cols_a, count_a)
        )
    for bit_pos in range((cols_axis - 1).bit_length()):
        stride = 1 << bit_pos
        nearby = stride % rows_axis
        if nearby:
            moved = (
                shifted(tiles_b, "row", rows_axis - nearby),
                shifted(for_sending(cols_b), "row", rows_axis - nearby).astype(cols_b.dtype),
                shifted(for_sending(count_b), "row", rows_axis - nearby).astype(count_b.dtype),
            )
        else:
            moved = (tiles_b, cols_b, count_b)
        moved = roll_slots(moved, (row_group + stride) // rows_axis)
        tiles_b, cols_b, count_b = select_if(
            col_group // stride % 2 == 1, moved, (tiles_b, cols_b, count_b)
        )
    tile_size = tiles_a.shape[2]
    running = jnp.zeros((tiles_a.shape[0], tile_size, BC * tile_size), jnp.float32)
    for turn_no in range(SHIFTS):
        current_tiles = tiles_b[0]
        current_cols = cols_b[0]
        current_count = count_b[0]
        rows_dense = dense_panel(current_tiles, current_cols, current_count, BC)
        running = running + panel_product(tiles_a, cols_a, count_a, rows_dense)
        if turn_no + 1 < SHIFTS:
            tiles_a, cols_a, count_a = (
                shifted(tiles_a, "col", cols_axis - 1),
                shifted(for_sending(cols_a), "col", cols_axis - 1).astype(cols_a.dtype),
                shifted(for_sending(count_a), "col", cols_axis - 1).astype(count_a.dtype),
            )
            moved = (
                shifted(tiles_b, "row", rows_axis - 1),
                shifted(for_sending(cols_b), "row", rows_axis - 1).astype(cols_b.dtype),
                shifted(for_sending(count_b), "row", rows_axis - 1).astype(count_b.dtype),
            )
            tiles_b, cols_b, count_b = roll_slots(moved, (row_group + 1) // rows_axis)
    flat_running = running.reshape(-1, running.shape[2])
    summed = lax.psum(flat_running, "depth")
    half_rows = flat_running.shape[0] // lax.axis_size("depth")
    own_rows = lax.dynamic_slice_in_dim(summed, lax.axis_index("depth") * half_rows, half_rows, 0)
    return own_rows.astype(jnp.bfloat16)


REACH = SHIFTS + 1
PARTS = ((16,), (7, 6, 3))
LATE = 1
SPLIT = 6
PIECES = ((0, 0, 2), (1, 0, 1), (1, 1, 1))
FIRST = 3
MESH_ID = pl.DeviceIdType.MESH


def gather_multiply(n_col, a_cols, a_count, b_cols, b_count, a_ref, b_ref, out_ref, A, Bn0, Bn1, Bf0, Bf1,
                    Gn0, Gn1, Gf0, Gf1, MA, MB, SA, SB, run, ktab, ptab, ltab,
                    send_m, recv_m, send_a, recv_1, recv_2, recv_3, recv_4, swapped, send_b, recv_b, passed, ready,
                    local_sem):
    row = lax.axis_index("row")
    col = lax.axis_index("col")
    dep = lax.axis_index("depth")
    side = lax.rem(col, 2)
    z = lax.div(col, 2)
    top = n_col // 2 - 1
    per_row, size = A.shape[1:3]
    units = A.shape[0] // REACH
    half = units // 2
    inner = Bn0.shape[0]
    out_cols = out_ref.shape[1] // size
    terms = SHIFTS * 2 * per_row
    zero_at = half * terms
    row0, row1, side0, side1 = row == 0, row == 1, side == 0, side == 1

    def both(*flags):
        return functools.reduce(jnp.logical_and, flags)

    def at(col_offset, flip_depth=False, flip_row=False):
        return (
            1 - row if flip_row else row,
            lax.rem(col + col_offset + n_col, n_col),
            1 - dep if flip_depth else dep,
        )

    twin_dev, row_dev = at(0, True), at(0, False, True)
    side_dev = (row, col + 1 - 2 * side, dep)
    down, up, down2, up2 = at(-2), at(2), at(-4), at(4)

    def remote(src, dst, ssem, rsem, dev):
        return pltpu.make_async_remote_copy(
            src_ref=src, dst_ref=dst, send_sem=ssem, recv_sem=rsem, device_id=dev, device_id_type=MESH_ID
        )

    def signal(sem, dev):
        pl.semaphore_signal(sem, inc=1, device_id=dev, device_id_type=MESH_ID)

    def drain(ref, sem):
        pltpu.make_async_copy(ref, ref, sem).wait()

    def start(copies, *flags):
        def go():
            for copy in copies:
                copy.start()

        if flags:
            pl.when(both(*flags))(go)
        else:
            go()

    s_near = [side + 2 * k for k in range(2)]
    s_far = [1 - side + 2 * k for k in range(2)]
    m_near = [lax.rem(row + col + s, n_col) // 2 for s in s_near]
    m_far = [lax.rem(1 - row + col + s, n_col) // 2 for s in s_far]
    m_mine = [lax.rem(row + col + s, n_col) // 2 for s in s_far]
    near_own, near_twin = (Bn0, Bn1), (Gn0, Gn1)
    far_own, far_twin = (Bf0, Bf1), (Gf0, Gf1)

    index_local = [
        pltpu.make_async_copy(src, dst, local_sem.at[n])
        for src, dst, n in (
            (a_cols, MA.at[0, pl.ds(0, per_row)], 0), (a_count, MA.at[0, pl.ds(per_row, 1)], 0),
            (b_cols, MB.at[0, 0], 1), (b_count, MB.at[0, 1], 1),
        )
    ]
    b_local = [pltpu.make_async_copy(b_ref.at[m_near[k]], near_own[k], local_sem.at[2]) for k in range(2)]
    a_local = pltpu.make_async_copy(a_ref.at[pl.ds(dep * half, half)], A.at[pl.ds(0, half)], local_sem.at[2])
    start(index_local + b_local + [a_local])

    @pl.when(row0)
    def _():
        for slot in range(2 * SHIFTS, 2 * REACH):
            MA[slot] = jnp.zeros(MA.shape[1:], MA.dtype)

    barrier = pltpu.get_barrier_semaphore()
    signal(barrier, twin_dev)
    pl.when(row0)(lambda: signal(barrier, row_dev))
    pl.when(side0)(lambda: signal(barrier, side_dev))
    pl.when(z < top)(lambda: signal(barrier, up))
    pl.when(z == 0)(lambda: signal(barrier, down))
    pl.when(both(row1, z == 1))(lambda: signal(barrier, down2))
    greeted = 1 + row + side + jnp.where(z > 0, 1, 0) + jnp.where(z == top, 1 + row, 0)
    pl.semaphore_wait(barrier, greeted)
    pl.when(z == top)(lambda: signal(ready.at[2], up))
    pl.when(both(row1, z == top))(lambda: signal(ready.at[2], up2))
    pl.when(row1)(lambda: signal(ready.at[0], row_dev))
    pl.when(side1)(lambda: signal(ready.at[1], side_dev))

    def unit(p, u):
        return A.at[p * units + u]

    own = [a_ref.at[dep * half + r] for r in range(half)] + [unit(0, half + r) for r in range(half)]

    def landed(p, u):
        return {1: recv_1, 2: recv_2, 3: recv_3, 4: recv_4}[p].at[{1: u // 2, 3: max(u - FIRST + 1, 0)}.get(p, u)]

    def piece(ref, n):
        t, begin, length = PIECES[n]
        return ref.at[t, pl.ds(begin * size // 2, length * size // 2)]

    def to_panel(p, sources, dev, split=-1):
        copies = []
        for u, src in enumerate(sources):
            dst = unit(p, u)
            if u == split:
                for n in range(len(PIECES)):
                    sem = landed(p, units - 1 + n if p == SHIFTS and n else u)
                    copies.append(remote(piece(src, n), piece(dst, n), send_a, sem, dev))
            else:
                copies.append(remote(src, dst, send_a, landed(p, u), dev))
        return copies

    def panel(p):
        return [unit(p, u) for u in range(units)]

    swap = [
        remote(a_ref.at[(1 - dep) * half + r], unit(0, half + r), send_a, swapped, twin_dev)
        for r in range(half)
    ]
    chain = to_panel(2, own, down)
    chain2 = to_panel(4, panel(2), down, SPLIT)
    skip = to_panel(4, panel(0), down2, SPLIT)
    wrap = to_panel(2, panel(0)[:half], down)
    own_x1 = to_panel(1, own, side_dev)
    fwd_x1 = to_panel(1, panel(2), side_dev)
    fwd_x3 = to_panel(3, panel(2), side_dev)
    top_x3 = to_panel(3, panel(4)[: units - LATE], side_dev, SPLIT)
    low_x3 = to_panel(3, panel(1), down)

    near_b = [remote(b_ref.at[m_near[k]], near_twin[k], send_b, passed.at[0], twin_dev) for k in range(2)]
    far_b, pass_b = [], []
    for k, sizes in enumerate(PARTS):
        for c, blocks in enumerate(sizes):
            part = pl.ds(sum(sizes[:c]) * inner // 16, blocks * inner // 16)
            far_b.append(
                remote(b_ref.at[m_far[k], part], far_own[k].at[part], send_b, recv_b.at[len(far_b)], row_dev)
            )
            pass_b.append(remote(far_own[k].at[part], far_twin[k].at[part], send_b, passed.at[k], twin_dev))

    def index_a(src, dst, dev):
        return remote(MA.at[pl.ds(src, 2)], MA.at[pl.ds(dst, 2)], send_m.at[0], recv_m.at[min(dst // 2, 3)], dev)

    swap_m = remote(MA.at[0], MA.at[1], send_m.at[0], recv_m.at[0], twin_dev)
    near_m = remote(MB.at[0], MB.at[1], send_m.at[1], recv_m.at[4], twin_dev)
    far_m = remote(MB.at[0], MB.at[2], send_m.at[1], recv_m.at[5], row_dev)
    pass_m = remote(MB.at[2], MB.at[3], send_m.at[1], recv_m.at[4], twin_dev)
    chain_m, chain2_m, skip_m = index_a(0, 4, down), index_a(4, 8, down), index_a(0, 8, down2)
    own_x1_m, fwd_x1_m = index_a(0, 2, side_dev), index_a(4, 2, side_dev)
    fwd_x3_m, low_x3_m = index_a(4, 6, side_dev), index_a(2, 6, down)

    drain(MA.at[0], local_sem.at[0])
    drain(MB.at[0], local_sem.at[1])
    start([swap_m] + swap)
    start(chain[:2], z > 0)
    start(own_x1[:2], side1)
    pl.when(row0)(lambda: pl.semaphore_wait(ready.at[0], 1))
    start([far_m] + far_b + [near_m] + near_b)
    swap_m.wait_recv()
    start([chain_m] + chain[2:half], z > 0)
    start([own_x1_m] + own_x1[2:half], side1)
    drain(A.at[pl.ds(0, half)], swapped)

    def local_data():
        drain(A.at[pl.ds(0, 2 * units + half)], local_sem.at[2])

    @pl.when(z == 0)
    def _():
        local_data()
        pl.semaphore_wait(ready.at[2], 1)
        start(wrap[:1] + [chain_m] + wrap[1:])

    @pl.when(both(row1, z == 1))
    def _():
        local_data()
        pl.semaphore_wait(ready.at[2], 1)
        start(skip[:1] + [skip_m] + skip[1:])

    pl.when(side0)(lambda: pl.semaphore_wait(ready.at[1], 1))
    run[zero_at] = jnp.zeros(run.shape[1:], jnp.float32)

    def far_part(n):
        far_b[n].wait_recv()
        pass_b[n].start()

    def low(u):
        drain(A.at[pl.ds(0, 2)], landed(1, u))
        for w in (u, u + 1):
            start([low_x3[w]], side1, *([] if w >= units - LATE else [row0]))

    def recv(p, u):
        if p == 4 and u == SPLIT:
            for n in range(len(PIECES)):
                recv_piece(n)
        elif p != 3 or u >= FIRST:
            drain(unit(p, u), landed(p, u))
        elif u == 0:
            drain(A.at[pl.ds(0, FIRST)], landed(p, u))

    def recv_piece(n):
        drain(piece(unit(SHIFTS, SPLIT), n), landed(SHIFTS, units - 1 + n if n else SPLIT))

    groups = [(s, m, k, d, far) for k in range(2) for far, s, m in ((0, s_near[k], m_near[k]), (1, s_far[k], m_mine[k]))
              for d in range(2)]

    def tables(r):
        cs = []
        for s, m, _, d, far in groups:
            slot = (s + row) * 2 + d
            used = SA[slot, per_row, dep * half + r]
            for t in range(per_row):
                k = SA[slot, t, dep * half + r]
                c = SB[2 * far + d, 0, m, 0, k]
                ok = jnp.logical_and(used > t, SB[2 * far + d, 1, m, 0, k] > 0)
                c = jnp.where(ok, c, -1)
                here = r * terms + len(cs)
                before = jnp.int32(zero_at)
                for at_p, c_p in enumerate(cs):
                    before = jnp.where(c_p == c, r * terms + at_p, before)
                ktab[here] = k
                ptab[here] = before
                cs.append(c)
        for c in range(out_cols):
            last = jnp.int32(zero_at)
            for at_p, c_p in enumerate(cs):
                last = jnp.where(c_p == c, r * terms + at_p, last)
            ltab[r * out_cols + c] = last

    rights = (Bn0, Gn0, Bf0, Gf0, Bn1, Gn1, Bf1, Gf1)

    def dots(g, r):
        s, _, _, d, _ = groups[g]
        values = []
        for t in range(per_row):
            here = r * terms + g * per_row + t
            left = A[(s + row) * units + d * half + r, t]
            values.append((here, jnp.dot(left, rights[g][ktab[here]], preferred_element_type=jnp.float32)))
        return values

    def add(values):
        for here, value in values:
            run[here] = value + run[ptab[here]]

    def products(wanted):
        held = []
        for g, r in wanted:
            fresh = dots(g, r)
            add(held)
            held = fresh
        add(held)

    def whole_group(g):
        products([(g, r) for r in range(half)])

    for u in range(units):
        recv(2, u)
        start([fwd_x1[u]], side0)
        if u == 0:
            drain(MA.at[pl.ds(4, 2)], recv_m.at[2])
            start([chain2_m], row1, z > 0)
            start([fwd_x1_m], side0)
            start([fwd_x3_m], side1)
        if u == 2:
            drain(MA.at[pl.ds(2, 2)], recv_m.at[1])
            start([low_x3_m], side1)
        if u < half:
            start([chain[half + u]])
            start([own_x1[half + u]], side1)
        else:
            start(chain2[2 * (u - half) : 2 * (u - half) + 2 + (u // (units - 1)) * (len(PIECES) - 1)], row1, z > 0)
            start(fwd_x3[2 * (u - half) : 2 * (u - half) + 2], side1)
        if u == 0:
            far_m.wait_recv()
            pass_m.start()
        if u in (4, 6):
            low(u - 4)
        if u == units - 1:
            far_part(0)

    def arrive_near(*wanted):
        @pl.when(row != side)
        def _():
            for u in wanted:
                recv(3, u)

        @pl.when(both(row1, side1))
        def _():
            for u in wanted:
                recv(4, u)

    def near_units(*wanted):
        arrive_near(*wanted)
        products([(4 + u // half, u % half) for u in wanted])

    def arrive_far(*wanted):
        @pl.when(row == side)
        def _():
            for u in wanted:
                recv(3, u)

        if units - 1 in wanted:
            pl.when(both(row1, side0))(lambda: recv(4, units - 1))

    def far_units(*wanted):
        arrive_far(*wanted)
        products([(6 + u // half, u % half) for u in wanted])

    scalars = [pltpu.make_async_copy(MA.at[pl.ds(0, 2 * REACH)], SA, local_sem.at[0]), pltpu.make_async_copy(MB, SB, local_sem.at[1])]

    for u in range(units):
        if u < units - LATE:
            @pl.when(both(row1, side0))
            def _():
                if u == SPLIT:
                    for n in range(len(PIECES)):
                        recv_piece(n)
                        top_x3[u + n].start()
                else:
                    recv(4, u)
                    top_x3[u].start()

        if u in (0, 2):
            low(half + u)
        if u == 0:
            pl.when(row0)(lambda: drain(MA.at[pl.ds(6, 2)], recv_m.at[3]))
            pl.when(row1)(lambda: drain(MA.at[pl.ds(6, 4)], recv_m.at[3]))
            drain(MB.at[pl.ds(0, 2)], recv_m.at[4])
            start(scalars)
        if u == 1:
            for copy in scalars:
                copy.wait()
            pl.when(z > row)(local_data)
            drain(A.at[pl.ds(0, 3 * units)], passed.at[0])
        if u in (3, 5):
            far_part(u // 2)
        if u in (1, 2):
            for r in range((u - 1) * half // 2, u * half // 2):
                tables(r)
        if u == 2:
            whole_group(0)
        if u == 3:
            whole_group(1)
            whole_group(2)
        if u == 4:
            whole_group(3)
            near_units(0)
        if u == 5:
            near_units(1, 2)
    far_part(len(far_b) - 1)

    def place(r):
        for c in range(out_cols):
            out_ref[r * size : (r + 1) * size, c * size : (c + 1) * size] = run[ltab[r * out_cols + c]].astype(
                out_ref.dtype
            )

    def finish(*rows, near=False):
        wanted = [half + r for r in rows]
        if near:
            arrive_near(units - 1)
            wanted.append(half - 1)
        arrive_far(*wanted)
        steps = [(7, r) for r in rows]
        if near:
            steps[-1:] = [(5, half - 1), (6, half - 1), (7, half - 1)]
        held = None
        for g, r in steps + [(None, None)]:
            fresh = None if g is None else (g, r, dots(g, r))
            if held is not None:
                add(held[2])
                if held[0] == 7:
                    place(held[1])
            held = fresh

    def all_sent(side_n):
        cases = [(0, 2 * units * side_n, row0)]
        across = units + LATE if side_n else units - LATE
        cases += [(more, across, both(row1, flag)) for more, flag in ((0, z == 0), (2, z == 1), (1, z > 1))]
        for more, extra, here in cases:
            def left(more=more, extra=extra):
                drain(run.at[pl.ds(0, 2 * units + half + extra + more * units)], send_a)
                drain(MA.at[pl.ds(0, 5 + 4 * side_n + 2 * more)], send_m.at[0])

            pl.when(here)(left)
        drain(run.at[pl.ds(0, 6 * units)], send_b)
        drain(MB.at[pl.ds(0, 3)], send_m.at[1])

    def last_pass():
        drain(A.at[pl.ds(0, units)], passed.at[1])

    @pl.when(side0)
    def _():
        near_units(3, 4, 5, 6, 7)
        far_units(0, 1, 2, 3)
        last_pass()
        finish(0, 1, 2, 3)
        all_sent(0)

    @pl.when(both(side1, z < top))
    def _():
        near_units(3, 4, 5, 6, 7)
        far_units(0, 1, 2, 3)
        last_pass()
        finish(0, 1)
        finish(3)
        all_sent(1)
        finish(2)

    @pl.when(both(side1, z == top))
    def _():
        near_units(3, 4)
        far_units(0)
        near_units(5)
        far_units(1)
        last_pass()
        near_units(6)
        far_units(2)
        finish(0, 1)
        all_sent(1)
        finish(3, near=True)
        finish(2)


def local_fast(n_col, a_tiles, a_cols, a_count, b_tiles, b_cols, b_count):
    block_rows, per_row, size = a_tiles.shape[2:5]
    slots, inner = b_tiles.shape[0], b_tiles.shape[4]
    half = block_rows // 2
    count = half * SHIFTS * 2 * per_row
    hbm = pl.BlockSpec(memory_space=pltpu.HBM)
    index_shapes = [(REACH * 2, per_row + 1, block_rows), (4, 2, slots, 1, inner)]
    index_vmem = [(REACH * 2 + 4, per_row + 1, block_rows), index_shapes[1]]
    call = pl.pallas_call(
        functools.partial(gather_multiply, n_col),
        out_shape=jax.ShapeDtypeStruct((half * size, BC * size), jnp.bfloat16),
        in_specs=[hbm] * 6,
        out_specs=pl.BlockSpec(memory_space=pltpu.VMEM),
        scratch_shapes=[pltpu.VMEM((REACH * block_rows, per_row, size, size), jnp.bfloat16)]
        + [pltpu.VMEM((inner, size, size), jnp.bfloat16)] * 8
        + [pltpu.VMEM(shape, jnp.int32) for shape in index_vmem]
        + [pltpu.SMEM(shape, jnp.int32) for shape in index_shapes]
        + [
            pltpu.VMEM((count + 1, size, size), jnp.float32),
            pltpu.SMEM((count,), jnp.int32),
            pltpu.SMEM((count,), jnp.int32),
            pltpu.SMEM((half * BC,), jnp.int32),
            pltpu.SemaphoreType.DMA((2,)),
            pltpu.SemaphoreType.DMA((6,)),
            pltpu.SemaphoreType.DMA,
            pltpu.SemaphoreType.DMA((half,)),
            pltpu.SemaphoreType.DMA((block_rows,)),
            pltpu.SemaphoreType.DMA((block_rows - FIRST + 1,)),
            pltpu.SemaphoreType.DMA((block_rows + len(PIECES) - 1,)),
            pltpu.SemaphoreType.DMA,
            pltpu.SemaphoreType.DMA,
            pltpu.SemaphoreType.DMA((sum(map(len, PARTS)),)),
            pltpu.SemaphoreType.DMA((2,)),
            pltpu.SemaphoreType.REGULAR((3,)),
            pltpu.SemaphoreType.DMA((3,)),
        ],
        compiler_params=pltpu.CompilerParams(
            collective_id=0, has_side_effects=True, vmem_limit_bytes=40 * 1024 * 1024
        ),
    )
    operands = [
        jnp.swapaxes(a_cols.reshape(block_rows, per_row), 0, 1),
        a_count.reshape(1, block_rows),
        b_cols.reshape(slots, 1, inner),
        b_count.reshape(slots, 1, inner),
        a_tiles.reshape(block_rows, per_row, size, size),
        b_tiles.reshape(slots, inner, size, size),
    ]
    return call(*(pltpu.with_memory_space_constraint(x, pltpu.HBM) for x in operands))


def solution(mesh):
    placed = (
        P("row", ("col", "depth"), None, None, None, None),
        P("row", ("col", "depth"), None, None),
        P("row", ("col", "depth"), None),
        P(None, "row", "depth", "col", None, None, None, None),
        P(None, "row", "depth", "col", None, None),
        P(None, "row", "depth", "col", None),
    )
    n_col = mesh.shape["col"]
    if mesh.shape["row"] == 2 and mesh.shape["depth"] == 2 and n_col == 2 * SHIFTS:
        body = functools.partial(local_fast, n_col)
    else:
        body = local
    return jax.shard_map(
        body, mesh=mesh, in_specs=placed, out_specs=P(("row", "depth"), "col"), check_vma=False
    )
```

```python
import functools
import math

import jax
import jax.numpy as jnp
from jax import lax
from jax.experimental import pallas as pl
from jax.experimental.pallas import tpu as pltpu
from jax.sharding import PartitionSpec as P

BC = 12
SHIFTS = 4


def for_sending(array):
    return jax.tree.map(lambda a: a.astype(jnp.bfloat16) if a.dtype == jnp.float32 else a, array)


def shifted(value, axis, steps):
    count = lax.axis_size(axis)
    pairs = [(source, (source + steps) % count) for source in range(count)]
    return lax.ppermute(value, axis, pairs)


def dense_panel(tiles_b, cols_b, count_b, width):
    slot_ids = lax.broadcasted_iota(jnp.int32, cols_b.shape, 1)
    valid_slot = slot_ids < count_b[:, None]
    targets = lax.broadcasted_iota(jnp.int32, (1, 1, width), 2)
    placing = jnp.logical_and(cols_b[:, :, None] == targets, valid_slot[:, :, None]).astype(
        jnp.bfloat16
    )
    spread = jnp.einsum("kuc,kuab->kacb", placing, tiles_b, preferred_element_type=jnp.float32)
    inner_blocks = tiles_b.shape[0]
    tile_size = tiles_b.shape[2]
    return spread.astype(jnp.bfloat16).reshape(inner_blocks, tile_size, width * tile_size)


def panel_product(tiles_a, cols_a, count_a, rows_dense):
    block_rows = tiles_a.shape[0]
    per_row = tiles_a.shape[1]
    tile_size = tiles_a.shape[2]
    slot_ids = lax.broadcasted_iota(jnp.int32, cols_a.shape, 1)
    valid_slot = slot_ids < count_a[:, None]
    masked = jnp.where(valid_slot[:, :, None, None], tiles_a, jnp.zeros_like(tiles_a))
    group_rows = math.gcd(block_rows, 4)

    def one_group(pieces):
        tiles_part, cols_part = pieces
        picks = lax.broadcasted_iota(jnp.int32, cols_part.shape + (rows_dense.shape[0],), 2)
        picks = (cols_part[:, :, None] == picks).astype(rows_dense.dtype)
        chosen = jnp.einsum("rtk,kbn->rtbn", picks, rows_dense, preferred_element_type=jnp.float32)
        chosen = chosen.astype(rows_dense.dtype)
        return jnp.einsum("rtab,rtbn->ran", tiles_part, chosen, preferred_element_type=jnp.float32)

    grouped = lax.map(
        one_group,
        (
            masked.reshape(block_rows // group_rows, group_rows, per_row, tile_size, tile_size),
            cols_a.reshape(block_rows // group_rows, group_rows, per_row),
        ),
    )
    return grouped.reshape(block_rows, tile_size, rows_dense.shape[2])


def roll_slots(stack, offset):
    slot_total = stack[0].shape[0]
    return tuple(
        (
            lax.dynamic_slice_in_dim(
                jnp.concatenate([member, member], 0), offset % slot_total, slot_total, 0
            )
            for member in stack
        )
    )


def select_if(flag, fresh, stale):
    return tuple((jnp.where(flag, new_part, old_part) for new_part, old_part in zip(fresh, stale)))


def local(a_tiles, a_cols, a_count, b_tiles, b_cols, b_count):
    rows_axis = lax.axis_size("row")
    cols_axis = lax.axis_size("col")
    row_group = lax.axis_index("row")
    col_group = lax.axis_index("col")
    tiles_a = a_tiles[0, 0]
    cols_a = a_cols[0, 0]
    count_a = a_count[0, 0]
    tiles_b = b_tiles[:, 0, 0, 0]
    cols_b = b_cols[:, 0, 0, 0]
    count_b = b_count[:, 0, 0, 0]
    for bit_pos in range((rows_axis - 1).bit_length()):
        stride = 1 << bit_pos
        moved = (
            shifted(tiles_a, "col", cols_axis - stride),
            shifted(for_sending(cols_a), "col", cols_axis - stride).astype(cols_a.dtype),
            shifted(for_sending(count_a), "col", cols_axis - stride).astype(count_a.dtype),
        )
        tiles_a, cols_a, count_a = select_if(
            row_group // stride % 2 == 1, moved, (tiles_a, cols_a, count_a)
        )
    for bit_pos in range((cols_axis - 1).bit_length()):
        stride = 1 << bit_pos
        nearby = stride % rows_axis
        if nearby:
            moved = (
                shifted(tiles_b, "row", rows_axis - nearby),
                shifted(for_sending(cols_b), "row", rows_axis - nearby).astype(cols_b.dtype),
                shifted(for_sending(count_b), "row", rows_axis - nearby).astype(count_b.dtype),
            )
        else:
            moved = (tiles_b, cols_b, count_b)
        moved = roll_slots(moved, (row_group + stride) // rows_axis)
        tiles_b, cols_b, count_b = select_if(
            col_group // stride % 2 == 1, moved, (tiles_b, cols_b, count_b)
        )
    tile_size = tiles_a.shape[2]
    running = jnp.zeros((tiles_a.shape[0], tile_size, BC * tile_size), jnp.float32)
    for turn_no in range(SHIFTS):
        current_tiles = tiles_b[0]
        current_cols = cols_b[0]
        current_count = count_b[0]
        rows_dense = dense_panel(current_tiles, current_cols, current_count, BC)
        running = running + panel_product(tiles_a, cols_a, count_a, rows_dense)
        if turn_no + 1 < SHIFTS:
            tiles_a, cols_a, count_a = (
                shifted(tiles_a, "col", cols_axis - 1),
                shifted(for_sending(cols_a), "col", cols_axis - 1).astype(cols_a.dtype),
                shifted(for_sending(count_a), "col", cols_axis - 1).astype(count_a.dtype),
            )
            moved = (
                shifted(tiles_b, "row", rows_axis - 1),
                shifted(for_sending(cols_b), "row", rows_axis - 1).astype(cols_b.dtype),
                shifted(for_sending(count_b), "row", rows_axis - 1).astype(count_b.dtype),
            )
            tiles_b, cols_b, count_b = roll_slots(moved, (row_group + 1) // rows_axis)
    flat_running = running.reshape(-1, running.shape[2])
    summed = lax.psum(flat_running, "depth")
    half_rows = flat_running.shape[0] // lax.axis_size("depth")
    own_rows = lax.dynamic_slice_in_dim(summed, lax.axis_index("depth") * half_rows, half_rows, 0)
    return own_rows.astype(jnp.bfloat16)


REACH = SHIFTS + 1
PARTS = ((16,), (8, 6, 2))
LATE = 1
SPLIT = 6
PIECES = ((0, 0, 2), (1, 0, 1), (1, 1, 1))
FIRST = 3
MESH_ID = pl.DeviceIdType.MESH


def gather_multiply(n_col, a_cols, a_count, b_cols, b_count, a_ref, b_ref, out_ref, A, Bn0, Bn1, Bf0, Bf1,
                    Gn0, Gn1, Gf0, Gf1, MA, MB, SA, SB, run, ktab, ptab, ltab,
                    send_m, recv_m, send_a, recv_1, recv_2, recv_3, recv_4, swapped, send_b, recv_b, passed, ready,
                    local_sem):
    row = lax.axis_index("row")
    col = lax.axis_index("col")
    dep = lax.axis_index("depth")
    side = lax.rem(col, 2)
    z = lax.div(col, 2)
    top = n_col // 2 - 1
    per_row, size = A.shape[1:3]
    units = A.shape[0] // REACH
    half = units // 2
    inner = Bn0.shape[0]
    out_cols = out_ref.shape[1] // size
    terms = SHIFTS * 2 * per_row
    zero_at = half * terms
    row0, row1, side0, side1 = row == 0, row == 1, side == 0, side == 1

    def both(*flags):
        return functools.reduce(jnp.logical_and, flags)

    def at(col_offset, flip_depth=False, flip_row=False):
        return (
            1 - row if flip_row else row,
            lax.rem(col + col_offset + n_col, n_col),
            1 - dep if flip_depth else dep,
        )

    twin_dev, row_dev = at(0, True), at(0, False, True)
    side_dev = (row, col + 1 - 2 * side, dep)
    down, up, down2, up2 = at(-2), at(2), at(-4), at(4)

    def remote(src, dst, ssem, rsem, dev):
        return pltpu.make_async_remote_copy(
            src_ref=src, dst_ref=dst, send_sem=ssem, recv_sem=rsem, device_id=dev, device_id_type=MESH_ID
        )

    def signal(sem, dev):
        pl.semaphore_signal(sem, inc=1, device_id=dev, device_id_type=MESH_ID)

    def drain(ref, sem):
        pltpu.make_async_copy(ref, ref, sem).wait()

    def start(copies, *flags):
        def go():
            for copy in copies:
                copy.start()

        if flags:
            pl.when(both(*flags))(go)
        else:
            go()

    s_near = [side + 2 * k for k in range(2)]
    s_far = [1 - side + 2 * k for k in range(2)]
    m_near = [lax.rem(row + col + s, n_col) // 2 for s in s_near]
    m_far = [lax.rem(1 - row + col + s, n_col) // 2 for s in s_far]
    m_mine = [lax.rem(row + col + s, n_col) // 2 for s in s_far]
    near_own, near_twin = (Bn0, Bn1), (Gn0, Gn1)
    far_own, far_twin = (Bf0, Bf1), (Gf0, Gf1)

    index_local = [
        pltpu.make_async_copy(src, dst, local_sem.at[n])
        for src, dst, n in (
            (a_cols, MA.at[0, pl.ds(0, per_row)], 0), (a_count, MA.at[0, pl.ds(per_row, 1)], 0),
            (b_cols, MB.at[0, 0], 1), (b_count, MB.at[0, 1], 1),
        )
    ]
    b_local = [pltpu.make_async_copy(b_ref.at[m_near[k]], near_own[k], local_sem.at[2]) for k in range(2)]
    a_local = pltpu.make_async_copy(a_ref.at[pl.ds(dep * half, half)], A.at[pl.ds(0, half)], local_sem.at[2])
    start(index_local + b_local + [a_local])

    @pl.when(row0)
    def _():
        for slot in range(2 * SHIFTS, 2 * REACH):
            MA[slot] = jnp.zeros(MA.shape[1:], MA.dtype)

    barrier = pltpu.get_barrier_semaphore()
    signal(barrier, twin_dev)
    pl.when(row0)(lambda: signal(barrier, row_dev))
    pl.when(side0)(lambda: signal(barrier, side_dev))
    pl.when(z < top)(lambda: signal(barrier, up))
    pl.when(z == 0)(lambda: signal(barrier, down))
    pl.when(both(row1, z == 1))(lambda: signal(barrier, down2))
    greeted = 1 + row + side + jnp.where(z > 0, 1, 0) + jnp.where(z == top, 1 + row, 0)
    pl.semaphore_wait(barrier, greeted)
    pl.when(z == top)(lambda: signal(ready.at[2], up))
    pl.when(both(row1, z == top))(lambda: signal(ready.at[2], up2))
    pl.when(row1)(lambda: signal(ready.at[0], row_dev))
    pl.when(side1)(lambda: signal(ready.at[1], side_dev))

    def unit(p, u):
        return A.at[p * units + u]

    own = [a_ref.at[dep * half + r] for r in range(half)] + [unit(0, half + r) for r in range(half)]

    def landed(p, u):
        return {1: recv_1, 2: recv_2, 3: recv_3, 4: recv_4}[p].at[{1: u // 2, 3: max(u - FIRST + 1, 0)}.get(p, u)]

    def piece(ref, n):
        t, begin, length = PIECES[n]
        return ref.at[t, pl.ds(begin * size // 2, length * size // 2)]

    def to_panel(p, sources, dev, split=-1):
        copies = []
        for u, src in enumerate(sources):
            dst = unit(p, u)
            if u == split:
                for n in range(len(PIECES)):
                    sem = landed(p, units - 1 + n if p == SHIFTS and n else u)
                    copies.append(remote(piece(src, n), piece(dst, n), send_a, sem, dev))
            else:
                copies.append(remote(src, dst, send_a, landed(p, u), dev))
        return copies

    def panel(p):
        return [unit(p, u) for u in range(units)]

    swap = [
        remote(a_ref.at[(1 - dep) * half + r], unit(0, half + r), send_a, swapped, twin_dev)
        for r in range(half)
    ]
    chain = to_panel(2, own, down)
    chain2 = to_panel(4, panel(2), down, SPLIT)
    skip = to_panel(4, panel(0), down2, SPLIT)
    wrap = to_panel(2, panel(0)[:half], down)
    own_x1 = to_panel(1, own, side_dev)
    fwd_x1 = to_panel(1, panel(2), side_dev)
    fwd_x3 = to_panel(3, panel(2), side_dev)
    top_x3 = to_panel(3, panel(4)[: units - LATE], side_dev, SPLIT)
    low_x3 = to_panel(3, panel(1), down)

    near_b = [remote(b_ref.at[m_near[k]], near_twin[k], send_b, passed.at[0], twin_dev) for k in range(2)]
    far_b, pass_b = [], []
    for k, sizes in enumerate(PARTS):
        for c, blocks in enumerate(sizes):
            part = pl.ds(sum(sizes[:c]) * inner // 16, blocks * inner // 16)
            far_b.append(
                remote(b_ref.at[m_far[k], part], far_own[k].at[part], send_b, recv_b.at[len(far_b)], row_dev)
            )
            pass_b.append(remote(far_own[k].at[part], far_twin[k].at[part], send_b, passed.at[k], twin_dev))

    def index_a(src, dst, dev):
        return remote(MA.at[pl.ds(src, 2)], MA.at[pl.ds(dst, 2)], send_m.at[0], recv_m.at[min(dst // 2, 3)], dev)

    swap_m = remote(MA.at[0], MA.at[1], send_m.at[0], recv_m.at[0], twin_dev)
    near_m = remote(MB.at[0], MB.at[1], send_m.at[1], recv_m.at[4], twin_dev)
    far_m = remote(MB.at[0], MB.at[2], send_m.at[1], recv_m.at[5], row_dev)
    pass_m = remote(MB.at[2], MB.at[3], send_m.at[1], recv_m.at[4], twin_dev)
    chain_m, chain2_m, skip_m = index_a(0, 4, down), index_a(4, 8, down), index_a(0, 8, down2)
    own_x1_m, fwd_x1_m = index_a(0, 2, side_dev), index_a(4, 2, side_dev)
    fwd_x3_m, low_x3_m = index_a(4, 6, side_dev), index_a(2, 6, down)

    drain(MA.at[0], local_sem.at[0])
    drain(MB.at[0], local_sem.at[1])
    start([swap_m] + swap)
    start(chain[:2], z > 0)
    start(own_x1[:2], side1)
    pl.when(row0)(lambda: pl.semaphore_wait(ready.at[0], 1))
    start([far_m] + far_b + [near_m] + near_b)
    swap_m.wait_recv()
    start([chain_m] + chain[2:half], z > 0)
    start([own_x1_m] + own_x1[2:half], side1)
    drain(A.at[pl.ds(0, half)], swapped)

    def local_data():
        drain(A.at[pl.ds(0, 2 * units + half)], local_sem.at[2])

    @pl.when(z == 0)
    def _():
        local_data()
        pl.semaphore_wait(ready.at[2], 1)
        start(wrap[:1] + [chain_m] + wrap[1:])

    @pl.when(both(row1, z == 1))
    def _():
        local_data()
        pl.semaphore_wait(ready.at[2], 1)
        start(skip[:1] + [skip_m] + skip[1:])

    pl.when(side0)(lambda: pl.semaphore_wait(ready.at[1], 1))
    run[zero_at] = jnp.zeros(run.shape[1:], jnp.float32)

    def far_part(n):
        far_b[n].wait_recv()
        pass_b[n].start()

    def low(u):
        drain(A.at[pl.ds(0, 2)], landed(1, u))
        for w in (u, u + 1):
            start([low_x3[w]], side1, *([] if w >= units - LATE else [row0]))

    def recv(p, u):
        if p == 4 and u == SPLIT:
            for n in range(len(PIECES)):
                recv_piece(n)
        elif p != 3 or u >= FIRST:
            drain(unit(p, u), landed(p, u))
        elif u == 0:
            drain(A.at[pl.ds(0, FIRST)], landed(p, u))

    def recv_piece(n):
        drain(piece(unit(SHIFTS, SPLIT), n), landed(SHIFTS, units - 1 + n if n else SPLIT))

    groups = [(s, m, k, d, far) for k in range(2) for far, s, m in ((0, s_near[k], m_near[k]), (1, s_far[k], m_mine[k]))
              for d in range(2)]

    def tables(r):
        cs = []
        for s, m, _, d, far in groups:
            slot = (s + row) * 2 + d
            used = SA[slot, per_row, dep * half + r]
            for t in range(per_row):
                k = SA[slot, t, dep * half + r]
                c = SB[2 * far + d, 0, m, 0, k]
                ok = jnp.logical_and(used > t, SB[2 * far + d, 1, m, 0, k] > 0)
                c = jnp.where(ok, c, -1)
                here = r * terms + len(cs)
                before = jnp.int32(zero_at)
                for at_p, c_p in enumerate(cs):
                    before = jnp.where(c_p == c, r * terms + at_p, before)
                ktab[here] = k
                ptab[here] = before
                cs.append(c)
        for c in range(out_cols):
            last = jnp.int32(zero_at)
            for at_p, c_p in enumerate(cs):
                last = jnp.where(c_p == c, r * terms + at_p, last)
            ltab[r * out_cols + c] = last

    rights = (Bn0, Gn0, Bf0, Gf0, Bn1, Gn1, Bf1, Gf1)

    def dots(g, r):
        s, _, _, d, _ = groups[g]
        values = []
        for t in range(per_row):
            here = r * terms + g * per_row + t
            left = A[(s + row) * units + d * half + r, t]
            values.append((here, jnp.dot(left, rights[g][ktab[here]], preferred_element_type=jnp.float32)))
        return values

    def add(values):
        for here, value in values:
            run[here] = value + run[ptab[here]]

    def products(wanted):
        held = []
        for g, r in wanted:
            fresh = dots(g, r)
            add(held)
            held = fresh
        add(held)

    def whole_group(g):
        products([(g, r) for r in range(half)])

    for u in range(units):
        recv(2, u)
        start([fwd_x1[u]], side0)
        if u == 0:
            drain(MA.at[pl.ds(4, 2)], recv_m.at[2])
            start([chain2_m], row1, z > 0)
            start([fwd_x1_m], side0)
            start([fwd_x3_m], side1)
        if u == 2:
            drain(MA.at[pl.ds(2, 2)], recv_m.at[1])
            start([low_x3_m], side1)
        if u < half:
            start([chain[half + u]])
            start([own_x1[half + u]], side1)
        else:
            start(chain2[2 * (u - half) : 2 * (u - half) + 2 + (u // (units - 1)) * (len(PIECES) - 1)], row1, z > 0)
            start(fwd_x3[2 * (u - half) : 2 * (u - half) + 2], side1)
        if u == 0:
            far_m.wait_recv()
            pass_m.start()
        if u in (4, 6):
            low(u - 4)
        if u == units - 1:
            far_part(0)

    def arrive_near(*wanted):
        @pl.when(row != side)
        def _():
            for u in wanted:
                recv(3, u)

        @pl.when(both(row1, side1))
        def _():
            for u in wanted:
                recv(4, u)

    def near_units(*wanted):
        arrive_near(*wanted)
        products([(4 + u // half, u % half) for u in wanted])

    def arrive_far(*wanted):
        @pl.when(row == side)
        def _():
            for u in wanted:
                recv(3, u)

        if units - 1 in wanted:
            pl.when(both(row1, side0))(lambda: recv(4, units - 1))

    def far_units(*wanted):
        arrive_far(*wanted)
        products([(6 + u // half, u % half) for u in wanted])

    scalars = [pltpu.make_async_copy(MA.at[pl.ds(0, 2 * REACH)], SA, local_sem.at[0]), pltpu.make_async_copy(MB, SB, local_sem.at[1])]

    for u in range(units):
        if u < units - LATE:
            @pl.when(both(row1, side0))
            def _():
                if u == SPLIT:
                    for n in range(len(PIECES)):
                        recv_piece(n)
                        top_x3[u + n].start()
                else:
                    recv(4, u)
                    top_x3[u].start()

        if u in (0, 2):
            low(half + u)
        if u == 0:
            pl.when(row0)(lambda: drain(MA.at[pl.ds(6, 2)], recv_m.at[3]))
            pl.when(row1)(lambda: drain(MA.at[pl.ds(6, 4)], recv_m.at[3]))
            drain(MB.at[pl.ds(0, 2)], recv_m.at[4])
            start(scalars)
        if u == 1:
            for copy in scalars:
                copy.wait()
            pl.when(z > row)(local_data)
            drain(A.at[pl.ds(0, 3 * units)], passed.at[0])
        if u in (3, 5):
            far_part(u // 2)
        if u in (1, 2):
            for r in range((u - 1) * half // 2, u * half // 2):
                tables(r)
        if u == 2:
            whole_group(0)
        if u == 3:
            whole_group(1)
            whole_group(2)
        if u == 4:
            whole_group(3)
            near_units(0)
        if u == 5:
            near_units(1, 2)
    far_part(len(far_b) - 1)

    def place(r):
        for c in range(out_cols):
            out_ref[r * size : (r + 1) * size, c * size : (c + 1) * size] = run[ltab[r * out_cols + c]].astype(
                out_ref.dtype
            )

    def finish(*rows, near=False):
        wanted = [half + r for r in rows]
        if near:
            arrive_near(units - 1)
            wanted.append(half - 1)
        arrive_far(*wanted)
        steps = [(7, r) for r in rows]
        if near:
            steps[-1:] = [(5, half - 1), (6, half - 1), (7, half - 1)]
        held = None
        for g, r in steps + [(None, None)]:
            fresh = None if g is None else (g, r, dots(g, r))
            if held is not None:
                add(held[2])
                if held[0] == 7:
                    place(held[1])
            held = fresh

    def all_sent(side_n):
        cases = [(0, 2 * units * side_n, row0)]
        across = units + LATE if side_n else units - LATE
        cases += [(more, across, both(row1, flag)) for more, flag in ((0, z == 0), (2, z == 1), (1, z > 1))]
        for more, extra, here in cases:
            def left(more=more, extra=extra):
                drain(run.at[pl.ds(0, 2 * units + half + extra + more * units)], send_a)
                drain(MA.at[pl.ds(0, 5 + 4 * side_n + 2 * more)], send_m.at[0])

            pl.when(here)(left)
        drain(run.at[pl.ds(0, 6 * units)], send_b)
        drain(MB.at[pl.ds(0, 3)], send_m.at[1])

    def last_pass():
        drain(A.at[pl.ds(0, units)], passed.at[1])

    @pl.when(side0)
    def _():
        near_units(3, 4, 5, 6, 7)
        far_units(0, 1, 2, 3)
        last_pass()
        finish(0, 1, 2, 3)
        all_sent(0)

    @pl.when(both(side1, z < top))
    def _():
        near_units(3, 4, 5, 6, 7)
        far_units(0, 1, 2, 3)
        last_pass()
        finish(0, 1)
        finish(3)
        all_sent(1)
        finish(2)

    @pl.when(both(side1, z == top))
    def _():
        near_units(3, 4)
        far_units(0)
        near_units(5)
        far_units(1)
        last_pass()
        near_units(6)
        far_units(2)
        finish(0, 1)
        all_sent(1)
        finish(3, near=True)
        finish(2)


def local_fast(n_col, a_tiles, a_cols, a_count, b_tiles, b_cols, b_count):
    block_rows, per_row, size = a_tiles.shape[2:5]
    slots, inner = b_tiles.shape[0], b_tiles.shape[4]
    half = block_rows // 2
    count = half * SHIFTS * 2 * per_row
    hbm = pl.BlockSpec(memory_space=pltpu.HBM)
    index_shapes = [(REACH * 2, per_row + 1, block_rows), (4, 2, slots, 1, inner)]
    index_vmem = [(REACH * 2 + 4, per_row + 1, block_rows), index_shapes[1]]
    call = pl.pallas_call(
        functools.partial(gather_multiply, n_col),
        out_shape=jax.ShapeDtypeStruct((half * size, BC * size), jnp.bfloat16),
        in_specs=[hbm] * 6,
        out_specs=pl.BlockSpec(memory_space=pltpu.VMEM),
        scratch_shapes=[pltpu.VMEM((REACH * block_rows, per_row, size, size), jnp.bfloat16)]
        + [pltpu.VMEM((inner, size, size), jnp.bfloat16)] * 8
        + [pltpu.VMEM(shape, jnp.int32) for shape in index_vmem]
        + [pltpu.SMEM(shape, jnp.int32) for shape in index_shapes]
        + [
            pltpu.VMEM((count + 1, size, size), jnp.float32),
            pltpu.SMEM((count,), jnp.int32),
            pltpu.SMEM((count,), jnp.int32),
            pltpu.SMEM((half * BC,), jnp.int32),
            pltpu.SemaphoreType.DMA((2,)),
            pltpu.SemaphoreType.DMA((6,)),
            pltpu.SemaphoreType.DMA,
            pltpu.SemaphoreType.DMA((half,)),
            pltpu.SemaphoreType.DMA((block_rows,)),
            pltpu.SemaphoreType.DMA((block_rows - FIRST + 1,)),
            pltpu.SemaphoreType.DMA((block_rows + len(PIECES) - 1,)),
            pltpu.SemaphoreType.DMA,
            pltpu.SemaphoreType.DMA,
            pltpu.SemaphoreType.DMA((sum(map(len, PARTS)),)),
            pltpu.SemaphoreType.DMA((2,)),
            pltpu.SemaphoreType.REGULAR((3,)),
            pltpu.SemaphoreType.DMA((3,)),
        ],
        compiler_params=pltpu.CompilerParams(
            collective_id=0, has_side_effects=True, vmem_limit_bytes=40 * 1024 * 1024
        ),
    )
    operands = [
        jnp.swapaxes(a_cols.reshape(block_rows, per_row), 0, 1),
        a_count.reshape(1, block_rows),
        b_cols.reshape(slots, 1, inner),
        b_count.reshape(slots, 1, inner),
        a_tiles.reshape(block_rows, per_row, size, size),
        b_tiles.reshape(slots, inner, size, size),
    ]
    return call(*(pltpu.with_memory_space_constraint(x, pltpu.HBM) for x in operands))


def solution(mesh):
    placed = (
        P("row", ("col", "depth"), None, None, None, None),
        P("row", ("col", "depth"), None, None),
        P("row", ("col", "depth"), None),
        P(None, "row", "depth", "col", None, None, None, None),
        P(None, "row", "depth", "col", None, None),
        P(None, "row", "depth", "col", None),
    )
    n_col = mesh.shape["col"]
    if mesh.shape["row"] == 2 and mesh.shape["depth"] == 2 and n_col == 2 * SHIFTS:
        body = functools.partial(local_fast, n_col)
    else:
        body = local
    return jax.shard_map(
        body, mesh=mesh, in_specs=placed, out_specs=P(("row", "depth"), "col"), check_vma=False
    )
```
